32 devices in a mesh: ctx: 8 (over z, x), fsdp: 4 (over y, core).
Axes of the slice: x: 2, y: 2, z: 4, core: 2. Of those that a mesh axis runs over, the one named last changes fastest.
Arguments:
- hidden_in: bfloat16 [4, 1024, 2048], P('fsdp', 'ctx'), may hold values from -6 to 6
- positions: int32 [4, 1024], P('fsdp'), may hold values from 0 to 1023, as said below
- ln_gain: bfloat16 [2048], P(('ctx', 'fsdp')), may hold values from 0.25 to 1.75
- ln_bias: bfloat16 [2048], P(('ctx', 'fsdp')), may hold values from -1.75 to 1.75
- w_qkv: bfloat16 [6144, 2048], P(('ctx', 'fsdp')), may hold values from -0.125 to 0.125
- b_qkv: bfloat16 [6144], P(('ctx', 'fsdp')), may hold values from -1.75 to 1.75
- w_dense: bfloat16 [2048, 2048], P(('ctx', 'fsdp')), may hold values from -2 to 2
- b_dense: bfloat16 [2048], P(('ctx', 'fsdp')), may hold values from -1.75 to 1.75
- w_fc1: bfloat16 [8192, 2048], P(('ctx', 'fsdp')), may hold values from -0.125 to 0.125
- b_fc1: bfloat16 [8192], P(('ctx', 'fsdp')), may hold values from -1.75 to 1.75
- w_fc2: bfloat16 [2048, 8192], P(('ctx', 'fsdp')), may hold values from -0.09375 to 0.09375
- b_fc2: bfloat16 [2048], P(('ctx', 'fsdp')), may hold values from -1.75 to 1.75
- out_grad: bfloat16 [4, 1024, 2048], P('fsdp', 'ctx'), may hold values from -6 to 6
Outputs:
- hidden_out: bfloat16 [4, 1024, 2048], P('fsdp', 'ctx')
- grad_in: float32 [4, 1024, 2048], P('fsdp', 'ctx')
- grad_ln_gain: float32 [2048], P(('ctx', 'fsdp'))
- grad_ln_bias: float32 [2048], P(('ctx', 'fsdp'))
- grad_w_qkv: float32 [6144, 2048], P(('ctx', 'fsdp'))
- grad_b_qkv: float32 [6144], P(('ctx', 'fsdp'))
- grad_w_dense: float32 [2048, 2048], P(('ctx', 'fsdp'))
- grad_b_dense: float32 [2048], P(('ctx', 'fsdp'))
- grad_w_fc1: float32 [8192, 2048], P(('ctx', 'fsdp'))
- grad_b_fc1: float32 [8192], P(('ctx', 'fsdp'))
- grad_w_fc2: float32 [2048, 8192], P(('ctx', 'fsdp'))
- grad_b_fc2: float32 [2048], P(('ctx', 'fsdp'))
The draws below stay inside these ranges and needn't reach their ends.
Inputs may be any that keep to these rules, and one draw needn't show every extreme that they name: For each sequence, stored columns 2 b * 64 to 2 b * 64 + 2 * 64 - 1 hold two runs of 64 consecutive rising positions, one starting at j * 64 and one at (15 - j) * 64, in either order; every position of a sequence appears exactly once.
All inputs are finite; a program needn't handle non-finite values.
Results may differ from the reference program's by a relative error of at most 0.012.
Values may be sent and summed in bfloat16 or wider, within the bound.
A program may use at most 512 MiB of HBM per device.

```python
import jax
import jax.numpy as jnp
from jax import lax

D = 2048
FF = 8192
HEAD_DIM = 64
ROT_DIM = 32
HEADS = 32
CH = 64
LEN = 1024
SEQS = 4


def draw_positions(key, part):
    pair_count = LEN // (2 * CH)
    key_order, key_flip = jax.random.split(key)
    scores = jax.random.randint(key_order, (SEQS, pair_count), 0, 1 << 20) * pair_count + jnp.arange(pair_count, dtype=jnp.int32)[None, :]
    pair_order = jnp.argsort(scores, axis=1).astype(jnp.int32)
    flip_bits = jax.random.randint(key_flip, (SEQS, pair_count), 0, 2)
    leading = jnp.where(flip_bits == 1, 2 * pair_count - 1 - pair_order, pair_order)
    trailing = 2 * pair_count - 1 - leading
    blocks = jnp.stack([leading, trailing], axis=2)
    offsets = jnp.arange(CH, dtype=jnp.int32)
    return (blocks[:, :, :, None] * CH + offsets).reshape(SEQS, LEN).astype(jnp.int32)


def levels(own_key, shape, cuts, smallest, largest):
    def one(position, blocks):
        heights = jax.random.uniform(jax.random.fold_in(jax.random.fold_in(own_key, 6), position), (blocks,), jnp.float32, smallest / len(cuts), largest / len(cuts))
        return jnp.repeat(jnp.exp(heights), shape[position] // blocks).reshape((-1,) + (1,) * (len(shape) - position - 1))

    gain = one(*cuts[0])
    for cut in cuts[1:]:
        gain = gain * one(*cut)
    return gain


def gaussian(stream_key, shape, width, reach, cuts=(), held_as=jnp.bfloat16):
    entries = jax.random.normal(stream_key, shape, jnp.float32) * width
    if len(cuts) > 0:
        entries = levels(stream_key, shape, cuts, -0.22, 0.18) * entries
    return jnp.clip(entries, min=-reach, max=reach).astype(held_as)


def setup_inputs(seed: int = 0) -> dict:
    arg_keys = jax.random.split(jax.random.key(seed), 14)
    hidden_in = gaussian(arg_keys[0], (SEQS, LEN, D), 1.0, 6.0, ((0, 4), (1, 8)))
    positions = draw_positions(jax.random.fold_in(arg_keys[13], 71), 0)
    ln_gain = jnp.clip(1.0 + 0.15 * jax.random.normal(arg_keys[2], (D,), jnp.float32), 0.25, 1.75).astype(jnp.bfloat16)
    ln_bias = gaussian(arg_keys[3], (D,), 0.3, 1.75, ((0, 32),))
    w_qkv = gaussian(arg_keys[4], (3 * D, D), D ** -0.5, 0.125, ((0, 32),))
    b_qkv = gaussian(arg_keys[5], (3 * D,), 0.3, 1.75, ((0, 32),))
    w_dense = gaussian(arg_keys[6], (D, D), (max(D // 256, 1)) ** -0.5, 2.0, ((0, 32),))
    b_dense = gaussian(arg_keys[7], (D,), 0.3, 1.75, ((0, 32),))
    w_fc1 = gaussian(arg_keys[8], (FF, D), D ** -0.5, 0.125, ((0, 32),))
    b_fc1 = gaussian(arg_keys[9], (FF,), 0.3, 1.75, ((0, 32),))
    w_fc2 = gaussian(arg_keys[10], (D, FF), (FF // 2) ** -0.5, 0.09375, ((0, 32),))
    b_fc2 = gaussian(arg_keys[11], (D,), 0.3, 1.75, ((0, 32),))
    out_grad = gaussian(arg_keys[12], (SEQS, LEN, D), 1.0, 6.0, ((0, 4), (1, 8)))
    return dict(hidden_in=hidden_in, positions=positions, ln_gain=ln_gain, ln_bias=ln_bias, w_qkv=w_qkv, b_qkv=b_qkv, w_dense=w_dense, b_dense=b_dense, w_fc1=w_fc1, b_fc1=b_fc1, w_fc2=w_fc2, b_fc2=b_fc2, out_grad=out_grad)


@jax.custom_vjp
def low(v):
    return lax.optimization_barrier(v.astype(jnp.bfloat16)).astype(jnp.float32)

@jax.custom_vjp
def low_back(v):
    return v

def low_keep(v):
    return (low(v), None)

def low_pass(kept, grad):
    return (grad,)

def back_keep(v):
    return (v, None)

def back_low(kept, grad):
    return (low(grad),)
low.defvjp(low_keep, low_pass)
low_back.defvjp(back_keep, back_low)
EPSILON = 1e-05
SCORE_SCALE = 0.125
PRECISE = lax.Precision.HIGHEST

def frequencies():
    half_rot = ROT_DIM // 2
    return jnp.power(10000.0, -jnp.arange(half_rot, dtype=jnp.float32) / half_rot)

def rotate(tensor, angles):
    half_rot = ROT_DIM // 2
    cosine = jnp.cos(angles)[:, None, :]
    sine_part = jnp.sin(angles)[:, None, :]
    leading = tensor[..., :half_rot]
    trailing = tensor[..., half_rot:ROT_DIM]
    return jnp.concatenate([leading * cosine - trailing * sine_part, trailing * cosine + leading * sine_part, tensor[..., ROT_DIM:]], axis=-1)

def gelu_tanh(values):
    inner_arg = 0.7978845608028654 * (values + 0.044715 * values * values * values)
    return 0.5 * values * (1.0 + jnp.tanh(inner_arg))

def normalize(values, gain_vec, shift_vec):
    centered = values - lax.optimization_barrier(jnp.mean(values, axis=-1, keepdims=True))
    variance = lax.optimization_barrier(jnp.mean(centered * centered, axis=-1, keepdims=True))
    return centered * lax.rsqrt(variance + EPSILON) * gain_vec + shift_vec

def sequence_layer(params, seq_in, seq_pos):
    ln_gain, ln_bias, w_qkv, b_qkv, w_dense, b_dense, w_fc1, b_fc1, w_fc2, b_fc2 = params
    length = seq_in.shape[0]
    normed = low(normalize(seq_in, ln_gain, ln_bias))
    mixed = low_back(jnp.dot(normed, w_qkv.T, precision=PRECISE) + b_qkv)
    angles = seq_pos.astype(jnp.float32)[:, None] * frequencies()[None, :]
    head_shape = (length, HEADS, HEAD_DIM)
    queries = low(rotate(mixed[:, :D].reshape(head_shape), angles))
    keys_rot = low(rotate(mixed[:, D:2 * D].reshape(head_shape), angles))
    values = low(mixed[:, 2 * D:].reshape(head_shape))
    allowed = seq_pos[None, :] <= seq_pos[:, None]
    per_group = min(4, HEADS)
    group_count = HEADS // per_group

    def split_groups(tensor):
        return tensor.reshape(length, group_count, per_group, HEAD_DIM).transpose(1, 0, 2, 3)

    def attend(operands):
        query_grp, key_grp, value_grp = operands
        scores = low_back(jnp.einsum('qhd,khd->hqk', query_grp, key_grp, precision=PRECISE) * SCORE_SCALE)
        scores = jnp.where(allowed[None], scores, -1e+30)
        soft_probs = low(jax.nn.softmax(scores, axis=-1))
        return jnp.einsum('hqk,khd->qhd', soft_probs, value_grp, precision=PRECISE)
    grouped = lax.map(jax.checkpoint(attend), (split_groups(queries), split_groups(keys_rot), split_groups(values)))
    context = grouped.transpose(1, 0, 2, 3).reshape(length, D)
    context = low(low_back(context))
    upward = low_back(jnp.dot(normed, w_fc1.T, precision=PRECISE) + b_fc1)
    activated = low(gelu_tanh(upward))
    attn_out = jnp.dot(context, w_dense.T, precision=PRECISE) + b_dense
    mlp_out = jnp.dot(activated, w_fc2.T, precision=PRECISE) + b_fc2
    return seq_in + attn_out + mlp_out

def reference(hidden_in, positions, ln_gain, ln_bias, w_qkv, b_qkv, w_dense, b_dense, w_fc1, b_fc1, w_fc2, b_fc2, out_grad):
    params = (ln_gain.astype(jnp.float32), ln_bias.astype(jnp.float32), w_qkv.astype(jnp.float32), b_qkv.astype(jnp.float32), w_dense.astype(jnp.float32), b_dense.astype(jnp.float32), w_fc1.astype(jnp.float32), b_fc1.astype(jnp.float32), w_fc2.astype(jnp.float32), b_fc2.astype(jnp.float32))
    inputs = hidden_in.astype(jnp.float32)

    def forward(weights, activations):

        def one_sequence(operands):
            return sequence_layer(weights, operands[0], operands[1])
        return lax.map(jax.checkpoint(one_sequence), (activations, positions))
    output, pullback = jax.vjp(forward, params, inputs)
    gradients, grad_in = pullback(out_grad.astype(jnp.float32))
    return (output.astype(jnp.bfloat16), grad_in, gradients[0], gradients[1], gradients[2], gradients[3], gradients[4], gradients[5], gradients[6], gradients[7], gradients[8], gradients[9])
```

```python
import functools

import jax
import jax.numpy as jnp
from jax import lax
from jax.experimental import pallas as pl
from jax.experimental.pallas import tpu as pltpu
from jax.sharding import PartitionSpec as P

HEAD_DIM = 64
ROT_DIM = 32
RUN = 64
EPSILON = 1e-05
SCORE_SCALE = 0.125
BOTH = ("ctx", "fsdp")
F32 = jnp.float32
LOW = jnp.bfloat16
MESH = pl.DeviceIdType.MESH
SEMAPHORES = 512
VMEM_BYTES = 60 * 1024 * 1024


def gelu_tanh(values):
    inner_arg = 0.7978845608028654 * (values + 0.044715 * values * values * values)
    return 0.5 * values * (1.0 + jnp.tanh(inner_arg))


def gelu_slope(values):
    inner_arg = 0.7978845608028654 * (values + 0.044715 * values * values * values)
    bend = jnp.tanh(inner_arg)
    inner_slope = 0.7978845608028654 * (1.0 + 3.0 * 0.044715 * values * values)
    return 0.5 * (1.0 + bend) + 0.5 * values * (1.0 - bend * bend) * inner_slope


def dot_nt(a, b):
    return lax.dot_general(a, b, (((1,), (1,)), ((), ())), preferred_element_type=F32)


def dot_nn(a, b):
    return lax.dot_general(a, b, (((1,), (0,)), ((), ())), preferred_element_type=F32)


def dot_tn(a, b):
    return lax.dot_general(a, b, (((0,), (0,)), ((), ())), preferred_element_type=F32)


def rope_tables(length):
    half_rot = ROT_DIM // 2
    freqs = jnp.power(10000.0, -jnp.arange(half_rot, dtype=F32) / half_rot)
    angles = jnp.arange(length, dtype=F32)[:, None] * freqs[None, :]
    cosine, sine = jnp.cos(angles), jnp.sin(angles)
    rest = HEAD_DIM - ROT_DIM
    ones, zeros = jnp.ones((length, rest), F32), jnp.zeros((length, rest), F32)
    gap = jnp.zeros((length, half_rot), F32)
    straight = jnp.concatenate([cosine, cosine, ones] * 2, axis=1)
    from_above = jnp.concatenate([-sine, gap, zeros] * 2, axis=1)
    from_below = jnp.concatenate([gap, sine, zeros] * 2, axis=1)
    return straight, from_above, from_below


def attention_kernel(
    order_ref, q_ref, k_ref, v_ref, g_ref, cos_ref, up_ref, down_ref,
    ctx_out, dq_out, dk_out, dv_out,
    q_s, k_s, v_s, g_s, dk_s, dv_s, ctx_s, dq_s,
):
    length, width = q_ref.shape
    half_rot = ROT_DIM // 2
    runs = length // RUN

    def sort_in(i, carry):
        stored = pl.ds(pl.multiple_of(order_ref[i] * RUN, RUN), RUN)
        rows = pl.ds(pl.multiple_of(i * RUN, RUN), RUN)
        cosine, above, below = cos_ref[rows, :], up_ref[rows, :], down_ref[rows, :]

        def turn(u):
            return (
                u * cosine
                + pltpu.roll(u, width - half_rot, 1) * above
                + pltpu.roll(u, half_rot, 1) * below
            )

        q_s[rows, :] = (turn(q_ref[stored, :]).astype(LOW) * SCORE_SCALE).astype(LOW)
        k_s[rows, :] = turn(k_ref[stored, :]).astype(LOW)
        v_s[rows, :] = v_ref[stored, :].astype(LOW)
        g_s[rows, :] = g_ref[stored, :]
        return carry

    lax.fori_loop(0, runs, sort_in, 0)
    dk_s[...] = jnp.zeros_like(dk_s)
    dv_s[...] = jnp.zeros_like(dv_s)

    tile = min(256, length)
    lanes = lax.broadcasted_iota(jnp.int32, (tile, width), 1)
    diagonal = lax.broadcasted_iota(jnp.int32, (tile, tile), 1) <= lax.broadcasted_iota(
        jnp.int32, (tile, tile), 0
    )
    for step in range(length // tile):
        rows = slice(step * tile, (step + 1) * tile)
        reach = (step + 1) * tile
        q_pair, g_pair = q_s[rows, :], g_s[rows, :]
        context = jnp.zeros((tile, width), F32)
        grad_q = jnp.zeros((tile, width), F32)
        for head in range(width // HEAD_DIM):
            mine = (lanes // HEAD_DIM) == head
            q_own = jnp.where(mine, q_pair, jnp.zeros_like(q_pair))
            g_own = jnp.where(mine, g_pair, jnp.zeros_like(g_pair))
            scores = dot_nt(q_own, k_s[:reach, :])
            last = jnp.where(diagonal, scores[:, reach - tile :], -1e30)
            if step > 0:
                scores = jnp.concatenate([scores[:, : reach - tile], last], axis=1)
            else:
                scores = last
            peak = jnp.max(scores, axis=1, keepdims=True)
            exps = jnp.exp(scores - peak)
            probs = exps * (1.0 / jnp.sum(exps, axis=1, keepdims=True))
            probs_low = probs.astype(LOW)
            context = jnp.where(mine, dot_nn(probs_low, v_s[:reach, :]), context)
            grad_probs = dot_nt(g_own, v_s[:reach, :])
            inner = jnp.sum(probs * grad_probs, axis=1, keepdims=True)
            grad_scores = (probs * (grad_probs - inner)).astype(LOW)
            grad_q = jnp.where(mine, dot_nn(grad_scores, k_s[:reach, :]), grad_q)
            dk_s[:reach, :] += dot_tn(grad_scores, q_own)
            dv_s[:reach, :] += dot_tn(probs_low, g_own)
        ctx_s[rows, :] = context.astype(LOW)
        dq_s[rows, :] = grad_q * SCORE_SCALE

    def sort_out(i, carry):
        stored = pl.ds(pl.multiple_of(order_ref[i] * RUN, RUN), RUN)
        rows = pl.ds(pl.multiple_of(i * RUN, RUN), RUN)
        cosine, above, below = cos_ref[rows, :], up_ref[rows, :], down_ref[rows, :]

        def turn_back(u):
            return (
                u * cosine
                - pltpu.roll(u, width - half_rot, 1) * above
                - pltpu.roll(u, half_rot, 1) * below
            )

        ctx_out[stored, :] = ctx_s[rows, :]
        dq_out[stored, :] = turn_back(dq_s[rows, :]).astype(LOW)
        dk_out[stored, :] = turn_back(dk_s[rows, :]).astype(LOW)
        dv_out[stored, :] = dv_s[rows, :].astype(LOW)
        return carry

    lax.fori_loop(0, runs, sort_out, 0)


def attention(order, mixed, grad_context):
    length, width = grad_context.shape
    pair = 2 * HEAD_DIM
    pairs = width // pair
    tables = rope_tables(length)

    def part(offset):
        return pl.BlockSpec((length, pair), lambda i, order_ref: (0, offset * pairs + i))

    whole = pl.BlockSpec((length, pair), lambda i, order_ref: (0, 0))
    half_pairs = length * length * 5 // 8
    result = jax.ShapeDtypeStruct((length, width), LOW)
    return pl.pallas_call(
        attention_kernel,
        grid_spec=pltpu.PrefetchScalarGridSpec(
            num_scalar_prefetch=1,
            grid=(pairs,),
            in_specs=[part(0), part(1), part(2), part(0), whole, whole, whole],
            out_specs=[part(0)] * 4,
            scratch_shapes=[pltpu.VMEM((length, pair), LOW)] * 4
            + [pltpu.VMEM((length, pair), F32)] * 2
            + [pltpu.VMEM((length, pair), LOW), pltpu.VMEM((length, pair), F32)],
        ),
        out_shape=[result] * 4,
        compiler_params=pltpu.CompilerParams(vmem_limit_bytes=56 * 1024 * 1024),
        cost_estimate=pl.CostEstimate(
            flops=pairs * 2 * half_pairs * 12 * 256,
            bytes_accessed=length * width * 24,
            transcendentals=pairs * 2 * half_pairs,
        ),
        name="attention",
    )(order, mixed, mixed, mixed, grad_context, *tables)


class Grid:
    def __init__(self, ctx_n, fsdp_n):
        self.ctx_n, self.fsdp_n = ctx_n, fsdp_n
        self.x_n = 1 << ((ctx_n.bit_length() - 1) // 2)
        self.z_n = ctx_n // self.x_n
        self.core_n = 2 if fsdp_n % 2 == 0 else 1
        self.y_n = fsdp_n // self.core_n
        self.undo = 1 if ctx_n % 3 == 1 else 2

    def locate(self):
        self.ctx, self.fsdp = lax.axis_index("ctx"), lax.axis_index("fsdp")
        self.z, self.x = self.ctx // self.x_n, self.ctx % self.x_n
        self.y, self.core = self.fsdp // self.core_n, self.fsdp % self.core_n
        return self

    def zx(self, dz, dx):
        return ((self.z + dz + self.z_n) % self.z_n) * self.x_n + (
            self.x + dx + self.x_n
        ) % self.x_n

    def yc(self, dy, dc):
        return ((self.y + dy + self.y_n) % self.y_n) * self.core_n + (
            self.core + dc + self.core_n
        ) % self.core_n

    def qkv_piece(self, ctx, fsdp, m):
        span = 3 * self.fsdp_n
        v = (3 * fsdp + m + span * self.ctx_n - ctx * self.fsdp_n) % span
        return ((v // self.fsdp_n) * self.undo) % 3, v % self.fsdp_n

    def qkv_owner(self, ctx, fsdp, m):
        kind, place = self.qkv_piece(ctx, fsdp, m)
        piece = self.ctx_n * self.fsdp_n * kind + ctx * self.fsdp_n + place
        return piece // 3 // self.fsdp_n

    def qkv_user(self, ctx, fsdp, m):
        piece = 3 * (ctx * self.fsdp_n + fsdp) + m
        return (piece % (self.ctx_n * self.fsdp_n)) // self.fsdp_n

    def greet(self):
        barrier = pltpu.get_barrier_semaphore()
        for k in range(1, self.ctx_n):
            pl.semaphore_signal(
                barrier, inc=1, device_id={"ctx": (self.ctx + k) % self.ctx_n}, device_id_type=MESH
            )
        for k in range(1, self.fsdp_n):
            pl.semaphore_signal(
                barrier,
                inc=1,
                device_id={"fsdp": (self.fsdp + k) % self.fsdp_n},
                device_id_type=MESH,
            )
        pl.semaphore_wait(barrier, self.ctx_n + self.fsdp_n - 2)


class Copies:
    def __init__(self, sems):
        self.sems, self.used, self.sent, self.perhaps = sems, 0, [], []

    def sem(self):
        self.used += 1
        return self.sems.at[self.used - 1]

    def send(self, src, dst, **where):
        send_sem, recv_sem = self.sem(), self.sem()
        copy = pltpu.make_async_remote_copy(
            src_ref=src,
            dst_ref=dst,
            send_sem=send_sem,
            recv_sem=recv_sem,
            device_id=where,
            device_id_type=MESH,
        )
        copy.start()
        self.sent.append(copy)
        return recv_sem

    def send_or_keep(self, src, dst, ctx, own_ctx):
        send_sem, recv_sem = self.sem(), self.sem()
        remote = pltpu.make_async_remote_copy(
            src_ref=src,
            dst_ref=dst,
            send_sem=send_sem,
            recv_sem=recv_sem,
            device_id={"ctx": ctx},
            device_id_type=MESH,
        )

        @pl.when(ctx != own_ctx)
        def _():
            remote.start()

        @pl.when(ctx == own_ctx)
        def _():
            pltpu.make_async_copy(src, dst, recv_sem).start()

        self.perhaps.append((ctx != own_ctx, remote))
        return recv_sem

    def local(self, src, dst):
        copy = pltpu.make_async_copy(src, dst, self.sem())
        copy.start()
        return copy

    def drain(self):
        for copy in self.sent:
            copy.wait_send()
        for sent, copy in self.perhaps:

            @pl.when(sent)
            def _(copy=copy):
                copy.wait_send()


def arrived(ref, sem):
    pltpu.make_async_copy(ref, ref, sem).wait()


class TokenGather:
    def __init__(self, grid, copies, own, buffer):
        self.grid, self.copies, self.buffer = grid, copies, buffer
        self.along_x = []
        self.kept = copies.local(own, buffer.at[grid.ctx])
        self.pass_on(own, 0)

    def pass_on(self, src, k):
        grid, copies = self.grid, self.copies
        slot = self.buffer.at[grid.zx(-k, 0)]
        if k < grid.z_n - 1:
            self.along_z = copies.send(src, slot, ctx=grid.zx(1, 0))
        for l in range(1, grid.x_n):
            sem = copies.send(src, slot, ctx=grid.zx(0, l))
            self.along_x.append((k, l, sem))

    def step(self, k):
        slot = self.buffer.at[self.grid.zx(-k, 0)]
        arrived(slot, self.along_z)
        self.pass_on(slot, k)

    def finish(self):
        self.kept.wait()
        for k, l, sem in self.along_x:
            arrived(self.buffer.at[self.grid.zx(-k, -l)], sem)


class ShardGather:
    def __init__(self, grid, copies, own, view):
        self.grid, self.copies, self.view = grid, copies, view
        self.along_y = [
            copies.send(own, view(grid.fsdp), fsdp=grid.yc(k, 0)) for k in range(1, grid.y_n)
        ]
        self.across = []
        self.cross(own, 0)

    def cross(self, src, k):
        for c in range(1, self.grid.core_n):
            slot = self.view(self.grid.yc(-k, 0))
            self.across.append((k, c, self.copies.send(src, slot, fsdp=self.grid.yc(0, c))))

    def forward(self):
        for k in range(1, self.grid.y_n):
            slot = self.view(self.grid.yc(-k, 0))
            arrived(slot, self.along_y[k - 1])
            self.cross(slot, k)

    def finish(self):
        for k, c, sem in self.across:
            arrived(self.view(self.grid.yc(-k, -c)), sem)


def gather_kernel(
    shape, x_in, g_in, wq_in, wu_in, wf_in, wd_in, small_in,
    x_out, g_out, wi_out, wu_out, wo_out, small_out,
    x_s, g_s, wi_s, wu_s, wo_s, small_s, sems,
):
    grid = Grid(*shape).locate()
    copies = Copies(sems)
    unit = wd_in.shape[0]
    fw, dw = wf_in.shape[1] // grid.ctx_n, wd_in.shape[1] // grid.ctx_n
    grid.greet()

    tokens_x = TokenGather(grid, copies, x_in, x_s)
    kept = [
        copies.local(wu_in, wu_s.at[grid.fsdp]),
        copies.local(small_in, small_s.at[grid.ctx, grid.fsdp]),
    ]
    up = ShardGather(grid, copies, wu_in, lambda f: wu_s.at[f])
    peers = [(k, l) for k in range(grid.z_n) for l in range(grid.x_n) if k or l]
    small_sems = [
        copies.send(small_in, small_s.at[grid.ctx, grid.fsdp], ctx=grid.zx(k, l))
        for k, l in peers
    ]
    qkv_sems = []
    for m in range(3):
        user = grid.qkv_user(grid.ctx, grid.fsdp, m)
        kind, place = grid.qkv_piece(user, grid.fsdp, m)
        qkv_sems.append(
            copies.send_or_keep(
                wq_in.at[pl.ds(m * unit, unit)], wi_s.at[kind, place], user, grid.ctx
            )
        )
    tokens_x.step(1)

    def column_block(ref, index, width):
        return ref.at[:, pl.ds(pl.multiple_of(index * width, 128), width)]

    mine = wo_s.at[grid.ctx, grid.fsdp]
    own_out = [
        copies.local(column_block(wf_in, grid.ctx, fw), mine.at[:, pl.ds(0, fw)]),
        copies.local(column_block(wd_in, grid.ctx, dw), mine.at[:, pl.ds(fw, dw)]),
    ]
    out_sems = {}
    for k, l in peers:
        target = grid.zx(k, l)
        out_sems[k, l] = (
            copies.send(column_block(wf_in, target, fw), mine.at[:, pl.ds(0, fw)], ctx=target),
            copies.send(column_block(wd_in, target, dw), mine.at[:, pl.ds(fw, dw)], ctx=target),
        )
    for k in range(2, grid.z_n):
        tokens_x.step(k)
    tokens_g = TokenGather(grid, copies, g_in, g_s)
    up.forward()
    pieces = []
    for m in range(3):
        kind, place = grid.qkv_piece(grid.ctx, grid.fsdp, m)
        arrived(wi_s.at[kind, place], qkv_sems[m])

        def piece_view(f, m=m):
            kind, place = grid.qkv_piece(grid.ctx, f, m)
            return wi_s.at[kind, place]

        pieces.append(ShardGather(grid, copies, wi_s.at[kind, place], piece_view))
    tokens_g.step(1)
    for (k, l), sem in zip(peers, small_sems):
        arrived(small_s.at[grid.zx(-k, -l), grid.fsdp], sem)
    kept[1].wait()
    small = ShardGather(grid, copies, small_s.at[:, grid.fsdp], lambda f: small_s.at[:, f])
    shards = []
    for k in range(grid.z_n):
        first = ((grid.z - k + grid.z_n) % grid.z_n) * grid.x_n
        for l in range(grid.x_n):
            slot = wo_s.at[grid.zx(-k, -l), grid.fsdp]
            if k or l:
                arrived(slot.at[:, pl.ds(0, fw)], out_sems[k, l][0])
                arrived(slot.at[:, pl.ds(fw, dw)], out_sems[k, l][1])
            else:
                own_out[0].wait()
                own_out[1].wait()

        def out_view(f, first=first):
            return wo_s.at[pl.ds(first, grid.x_n), f]

        shards.append(ShardGather(grid, copies, out_view(grid.fsdp), out_view))
        if k + 2 < grid.z_n:
            tokens_g.step(k + 2)
    for gather in pieces + [small] + shards:
        gather.forward()
    kept[0].wait()
    up.finish()
    puts = [copies.local(wu_s, wu_out)]
    tokens_x.finish()
    puts.append(copies.local(x_s, x_out))
    for gather in pieces:
        gather.finish()
    puts.append(copies.local(wi_s, wi_out))
    small.finish()
    puts.append(copies.local(small_s, small_out))
    for gather in shards:
        gather.finish()
    puts.append(copies.local(wo_s, wo_out))
    tokens_g.finish()
    puts.append(copies.local(g_s, g_out))
    for put in puts:
        put.wait()
    copies.drain()


def accumulate(dst, *sources):
    if len(dst.shape) == 3:

        @pl.loop(0, dst.shape[0])
        def _(i):
            accumulate(dst.at[i], *[source.at[i] for source in sources])

        return
    rows, step = dst.shape[0], 16

    @pl.loop(0, rows // step)
    def _(i):
        part = pl.ds(pl.multiple_of(i * step, step), step)
        total = sources[0][part, :].astype(F32)
        for source in sources[1:]:
            total = total + source[part, :].astype(F32)
        dst[part, :] = total.astype(dst.dtype)


class TokenScatter:
    def __init__(self, grid, copies, parts, own, from_x, from_z, total):
        self.grid, self.copies, self.own = grid, copies, own
        self.from_x, self.from_z, self.total = from_x, from_z, total
        self.order = list(range(1, grid.z_n)) + [0]
        self.sems = {
            (k, l): copies.send(
                parts.at[grid.zx(-k, l)], from_x.at[k, l - 1], ctx=grid.zx(0, l)
            )
            for k in self.order
            for l in range(1, grid.x_n)
        }
        self.kept = {k: copies.local(parts.at[grid.zx(-k, 0)], own.at[k]) for k in self.order}

    def step(self, k):
        grid = self.grid
        self.kept[k].wait()
        terms = [self.own.at[k]]
        for l in range(1, grid.x_n):
            arrived(self.from_x.at[k, l - 1], self.sems[k, l])
            terms.append(self.from_x.at[k, l - 1])
        before = grid.z_n - 1 if k == 0 else k - 1
        if before > 0:
            arrived(self.from_z.at[before - 1], self.along_z)
            terms.append(self.from_z.at[before - 1])
        accumulate(self.total if k == 0 else self.own.at[k], *terms)
        if k > 0:
            self.along_z = self.copies.send(
                self.own.at[k], self.from_z.at[k - 1], ctx=grid.zx(1, 0)
            )


class ShardScatter:
    def __init__(self, grid, copies, views, own, from_core, from_y):
        self.grid, self.copies = grid, copies
        self.own, self.from_core, self.from_y = own, from_core, from_y
        self.sems, self.kept = {}, {}
        for k in list(range(1, grid.y_n)) + [0]:
            theirs = views(grid.yc(k, 1))
            ours = views(grid.yc(k, 0))
            self.sems[k] = [
                copies.send(src, from_core.at[k, i], fsdp=grid.yc(0, 1))
                for i, src in enumerate(theirs)
            ]
            self.kept[k] = [copies.local(src, own.at[k, i]) for i, src in enumerate(ours)]

    def step(self, k):
        for i in range(len(self.kept[k])):
            self.kept[k][i].wait()
            arrived(self.from_core.at[k, i], self.sems[k][i])
            accumulate(self.own.at[k, i], self.own.at[k, i], self.from_core.at[k, i])
        if k > 0:
            self.sems[k] = self.copies.send(
                self.own.at[k], self.from_y.at[k - 1], fsdp=self.grid.yc(k, 0)
            )

    def finish(self, result):
        for k in range(1, self.grid.y_n):
            arrived(self.from_y.at[k - 1], self.sems[k])
        for i in range(result.shape[0]):
            accumulate(
                result.at[i],
                self.own.at[0, i],
                *[self.from_y.at[k - 1, i] for k in range(1, self.grid.y_n)],
            )


def scatter_kernel(
    shape, po_in, pn_in, gu_in, go_in, gi_in, small_in,
    to_out, tn_out, gu_out, go_out, gi_out, small_out,
    po_own, po_x, po_z, po_sum, pn_own, pn_x, pn_z, pn_sum,
    gu_own, gu_core, gu_y, gu_sum, go_own, go_core, go_y, go_sum, go_got,
    gi_own, gi_core, gi_y, gi_sum, gi_got, small_s, small_core, small_y, small_x, small_z, sems,
):
    grid = Grid(*shape).locate()
    copies = Copies(sems)
    grid.greet()

    def small_sum(step, buffer, small_sems):
        for i, sem in enumerate(small_sems):
            arrived(buffer.at[i], sem)
        accumulate(
            small_s.at[step + 1], small_s.at[step], *[buffer.at[i] for i in range(len(small_sems))]
        )

    small_kept = copies.local(small_in, small_s.at[0])
    small_sems = [
        copies.send(small_in, small_core.at[c - 1], fsdp=grid.yc(0, c))
        for c in range(1, grid.core_n)
    ]
    shards_o = ShardScatter(
        grid, copies, lambda f: [go_in.at[:, f]], go_own, go_core, go_y
    )
    tokens_o = TokenScatter(grid, copies, po_in, po_own, po_x, po_z, po_sum)

    def qkv_views(f):
        return [gi_in.at[grid.qkv_piece(grid.ctx, f, m)] for m in range(3)]

    shards_i = ShardScatter(grid, copies, qkv_views, gi_own, gi_core, gi_y)
    shards_u = ShardScatter(grid, copies, lambda f: [gu_in.at[f]], gu_own, gu_core, gu_y)
    small_kept.wait()
    small_sum(0, small_core, small_sems)
    small_sems = [
        copies.send(small_s.at[1], small_y.at[k - 1], fsdp=grid.yc(k, 0))
        for k in range(1, grid.y_n)
    ]
    rounds = list(range(1, grid.y_n)) + [0]
    for k in rounds:
        shards_o.step(k)
    tokens_o.step(1)
    small_sum(1, small_y, small_sems)
    small_sems = [
        copies.send(small_s.at[2], small_x.at[l - 1], ctx=grid.zx(0, l))
        for l in range(1, grid.x_n)
    ]
    tokens_n = TokenScatter(grid, copies, pn_in, pn_own, pn_x, pn_z, pn_sum)
    for k in rounds:
        shards_i.step(k)
    for k in rounds:
        shards_u.step(k)
    for k in range(2, grid.z_n):
        tokens_o.step(k)
    small_sum(2, small_x, small_sems)
    small_sems = [
        copies.send(small_s.at[3], small_z.at[k - 1], ctx=grid.zx(k, 0))
        for k in range(1, grid.z_n)
    ]
    shards_o.finish(go_sum)
    peers = [(k, l) for k in range(grid.z_n) for l in range(grid.x_n) if k or l]
    own_o = copies.local(go_sum.at[0, grid.ctx], go_got.at[grid.ctx])
    out_sems = [
        copies.send(go_sum.at[0, grid.zx(k, l)], go_got.at[grid.ctx], ctx=grid.zx(k, l))
        for k, l in peers
    ]
    tokens_o.step(0)
    puts = [copies.local(po_sum, to_out)]
    tokens_n.step(1)
    shards_i.finish(gi_sum)
    qkv_sems = []
    for m in range(3):
        owner = grid.qkv_owner(grid.ctx, grid.fsdp, m)
        qkv_sems.append(copies.send_or_keep(gi_sum.at[m], gi_got.at[m], owner, grid.ctx))
    for k in range(2, grid.z_n):
        tokens_n.step(k)
    shards_u.finish(gu_sum)
    puts.append(copies.local(gu_sum.at[0], gu_out))
    small_sum(3, small_z, small_sems)
    puts.append(copies.local(small_s.at[4], small_out))
    tokens_n.step(0)
    puts.append(copies.local(pn_sum, tn_out))
    own_o.wait()
    for (k, l), sem in zip(peers, out_sems):
        arrived(go_got.at[grid.zx(-k, -l)], sem)
    puts.append(copies.local(go_got, go_out))
    for m in range(3):
        arrived(gi_got.at[m], qkv_sems[m])
    puts.append(copies.local(gi_got, gi_out))
    for put in puts:
        put.wait()
    copies.drain()


def solution(mesh):
    shape = mesh.shape["ctx"], mesh.shape["fsdp"]
    ctx_n, fsdp_n = shape
    n = ctx_n * fsdp_n
    plan = Grid(*shape)
    x_n, z_n, core_n, y_n = plan.x_n, plan.z_n, plan.core_n, plan.y_n

    def gather(x_own, g_own, w_qkv, w_fc1, w_fc2, w_dense, small):
        local_len, width = x_own.shape
        unit, hidden_units = w_fc2.shape
        cols = (hidden_units + width) // ctx_n
        shapes = [
            (ctx_n, local_len, width),
            (ctx_n, local_len, width),
            (3, fsdp_n, unit, width),
            (fsdp_n,) + w_fc1.shape,
            (ctx_n, fsdp_n, unit, cols),
            (ctx_n, fsdp_n) + small.shape,
        ]
        anywhere = pl.BlockSpec(memory_space=pl.ANY)
        return pl.pallas_call(
            functools.partial(gather_kernel, shape),
            out_shape=[jax.ShapeDtypeStruct(s, LOW) for s in shapes],
            in_specs=[anywhere] * 7,
            out_specs=[anywhere] * 6,
            scratch_shapes=[pltpu.VMEM(s, LOW) for s in shapes]
            + [pltpu.SemaphoreType.DMA((SEMAPHORES,))],
            compiler_params=pltpu.CompilerParams(
                collective_id=0, has_side_effects=True, vmem_limit_bytes=VMEM_BYTES
            ),
            name="gather",
        )(x_own, g_own, w_qkv, w_fc1, w_fc2, w_dense, small)

    def scatter(po, pn, gu, go, gi, small):
        local_len, width = po.shape[1:]
        up_rows = gu.shape[1]
        unit, cols = go.shape[2:]
        tokens = [
            pltpu.VMEM((z_n, local_len, width), LOW),
            pltpu.VMEM((z_n, x_n - 1, local_len, width), LOW),
            pltpu.VMEM((z_n - 1, local_len, width), LOW),
            pltpu.VMEM((local_len, width), F32),
        ]

        def shards(*block):
            return [
                pltpu.VMEM((y_n,) + block, LOW),
                pltpu.VMEM((y_n,) + block, LOW),
                pltpu.VMEM((max(y_n - 1, 1),) + block, LOW),
                pltpu.VMEM(block, LOW),
            ]

        anywhere = pl.BlockSpec(memory_space=pl.ANY)
        return pl.pallas_call(
            functools.partial(scatter_kernel, shape),
            out_shape=[
                jax.ShapeDtypeStruct((local_len, width), F32),
                jax.ShapeDtypeStruct((local_len, width), F32),
                jax.ShapeDtypeStruct((up_rows, width), LOW),
                jax.ShapeDtypeStruct((ctx_n, unit, cols), LOW),
                jax.ShapeDtypeStruct((3, unit, width), LOW),
                jax.ShapeDtypeStruct(small.shape, F32),
            ],
            in_specs=[anywhere] * 6,
            out_specs=[anywhere] * 6,
            scratch_shapes=tokens
            + tokens
            + shards(1, up_rows, width)
            + shards(1, ctx_n, unit, cols)
            + [pltpu.VMEM((ctx_n, unit, cols), LOW)]
            + shards(3, unit, width)
            + [pltpu.VMEM((3, unit, width), LOW)]
            + [pltpu.VMEM((count,) + small.shape, F32) for count in (5, 1, y_n, x_n, z_n)]
            + [pltpu.SemaphoreType.DMA((SEMAPHORES,))],
            compiler_params=pltpu.CompilerParams(
                collective_id=1, has_side_effects=True, vmem_limit_bytes=VMEM_BYTES
            ),
            name="scatter",
        )(po, pn, gu, go, gi, small)

    def body(
        hidden_in, positions, ln_gain, ln_bias, w_qkv, b_qkv, w_dense, b_dense,
        w_fc1, b_fc1, w_fc2, b_fc2, out_grad,
    ):
        local_len, width = hidden_in.shape[1:]
        hidden_units = w_fc2.shape[1]
        unit = w_dense.shape[0]
        up_rows = w_fc1.shape[0]
        fw, dw = hidden_units // ctx_n, width // ctx_n
        my_ctx = lax.axis_index("ctx")
        me = my_ctx * fsdp_n + lax.axis_index("fsdp")
        length = positions.shape[1]
        x_own, g_own = hidden_in[0], out_grad[0]

        small_sizes = [unit, unit, 3 * unit, unit, up_rows, unit]
        offsets = [sum(small_sizes[:i]) for i in range(len(small_sizes) + 1)]
        small_rows = -(-offsets[-1] // 2048) * 16
        own_small = jnp.concatenate([ln_gain, ln_bias, b_qkv, b_dense, b_fc1, b_fc2])
        own_small = jnp.pad(own_small, (0, small_rows * 128 - offsets[-1])).reshape(-1, 128)
        x_all, g_all, wi, wu, wo, small = gather(
            x_own, g_own, w_qkv, w_fc1, w_fc2, w_dense, own_small
        )
        small = small.reshape(n, small_rows * 128).astype(F32)
        gain, shift, bias_qkv, bias_dense, bias_up, bias_down = (
            small[:, offsets[i] : offsets[i + 1]].reshape(-1) for i in range(6)
        )
        x_all, g_all = x_all.reshape(length, width), g_all.reshape(length, width)
        wi = wi.reshape(3 * fsdp_n * unit, width)
        wu = wu.reshape(fw, width)
        wo = wo.reshape(width, fw + dw)

        def standardize(values):
            wide = values.astype(F32)
            centered = wide - jnp.mean(wide, axis=-1, keepdims=True)
            spread = lax.rsqrt(jnp.mean(centered * centered, axis=-1, keepdims=True) + EPSILON)
            return centered * spread, spread

        xhat_all = standardize(x_all)[0]
        normed = (xhat_all * gain + shift).astype(LOW)

        runs = length // RUN
        rank = positions[0, ::RUN] // RUN
        stored = jnp.arange(runs, dtype=jnp.int32)
        order = jnp.sum(
            jnp.where(rank[None, :] == stored[:, None], stored[None, :], 0), axis=1
        ).astype(jnp.int32)

        upward = dot_nt(normed, wu) + lax.dynamic_slice_in_dim(bias_up, my_ctx * fw, fw)
        activated = gelu_tanh(upward).astype(LOW)
        mixed = dot_nt(normed, wi) + lax.dynamic_index_in_dim(
            bias_qkv.reshape(3, ctx_n, dw), my_ctx, 1, False
        ).reshape(3 * dw)
        grad_hidden = dot_nn(g_all, wo)
        grad_upward = (grad_hidden[:, :fw] * gelu_slope(upward)).astype(LOW)
        grad_context = grad_hidden[:, fw:].astype(LOW)
        context, dq, dk, dv = attention(order, mixed, grad_context)
        grad_mixed = jnp.concatenate([dq, dk, dv], axis=1)
        hidden = jnp.concatenate([activated, context], axis=1)

        partial_out = dot_nt(hidden, wo).astype(LOW)
        partial_wide = dot_nn(grad_mixed, wi) + dot_nn(grad_upward, wu)
        partial_normed = partial_wide.astype(LOW)

        def column_sum(array):
            return jnp.sum(array, axis=0, dtype=F32)

        terms = jnp.concatenate(
            [
                lax.dynamic_update_slice(
                    jnp.zeros((3, ctx_n, dw), F32),
                    column_sum(grad_mixed).reshape(3, 1, dw),
                    (0, my_ctx, 0),
                ).reshape(-1),
                lax.dynamic_update_slice(
                    jnp.zeros((hidden_units,), F32), column_sum(grad_upward), (my_ctx * fw,)
                ),
                column_sum(g_own),
                column_sum(partial_wide * xhat_all),
                column_sum(partial_wide),
            ]
        ).reshape(-1, 128)
        total, grad_normed, grad_up, grad_o, grad_qkv, sums = scatter(
            partial_out.reshape(ctx_n, local_len, width),
            partial_normed.reshape(ctx_n, local_len, width),
            dot_tn(grad_upward, normed).astype(LOW).reshape(fsdp_n, up_rows, width),
            dot_tn(g_all, hidden).astype(LOW).reshape(ctx_n, fsdp_n, unit, fw + dw),
            dot_tn(grad_mixed, normed).astype(LOW).reshape(3, fsdp_n, unit, width),
            terms,
        )
        hidden_out = (total + x_own.astype(F32) + bias_dense + bias_down).astype(LOW)
        xhat, spread = standardize(x_own)
        e = grad_normed * gain
        grad_in = (
            e - jnp.mean(e, axis=-1, keepdims=True)
            - xhat * jnp.mean(e * xhat, axis=-1, keepdims=True)
        ) * spread + g_own.astype(F32)
        grad_o = grad_o.transpose(1, 0, 2).astype(F32)
        sums = sums.reshape(-1)

        def own_slice(start, size):
            return lax.dynamic_slice_in_dim(sums, start + me * size, size)

        after_up = 3 * width + hidden_units
        grad_b_out = own_slice(after_up, unit)
        return (
            hidden_out[None],
            grad_in[None],
            own_slice(after_up + width, unit),
            own_slice(after_up + 2 * width, unit),
            grad_qkv.reshape(3 * unit, width).astype(F32),
            own_slice(0, 3 * unit),
            grad_o[:, :, fw:].reshape(unit, width),
            grad_b_out,
            grad_up.astype(F32),
            own_slice(3 * width, up_rows),
            grad_o[:, :, :fw].reshape(unit, hidden_units),
            grad_b_out,
        )

    tokens, rows, cells = P("fsdp", "ctx", None), P(BOTH, None), P(BOTH)
    return jax.shard_map(
        body,
        mesh=mesh,
        in_specs=(
            tokens, P("fsdp", None), cells, cells, rows, cells, rows, cells,
            rows, cells, rows, cells, tokens,
        ),
        out_specs=(
            tokens, tokens, cells, cells, rows, cells, rows, cells, rows, cells, rows, cells,
        ),
        check_vma=False,
    )
```

```python
import functools

import jax
import jax.numpy as jnp
import numpy as np
from jax import lax
from jax.experimental import pallas as pl
from jax.experimental.pallas import tpu as pltpu
from jax.sharding import PartitionSpec as P

HEAD_DIM = 64
ROT_DIM = 32
RUN = 64
EPSILON = 1e-05
SCORE_SCALE = 0.125
BOTH = ("ctx", "fsdp")
F32 = jnp.float32
LOW = jnp.bfloat16
MESH = pl.DeviceIdType.MESH
SEMAPHORES = 512
VMEM_BYTES = 60 * 1024 * 1024
SMALL_ROWS = (
    [(row, (1, 0)) for row in range(4)]
    + [(4, (3, j)) for j in range(3)]
    + [(7, (4, j)) for j in range(4)]
)


def dot_nt(a, b):
    return lax.dot_general(a, b, (((1,), (1,)), ((), ())), preferred_element_type=F32)


def dot_nn(a, b):
    return lax.dot_general(a, b, (((1,), (0,)), ((), ())), preferred_element_type=F32)


def dot_tn(a, b):
    return lax.dot_general(a, b, (((0,), (0,)), ((), ())), preferred_element_type=F32)


def turning_tables(length):
    half_rot = ROT_DIM // 2
    lane = np.arange(2 * HEAD_DIM) % HEAD_DIM
    freqs = np.where(lane < ROT_DIM, 10000.0 ** (-(lane % half_rot) / half_rot), 0.0)
    starts = np.arange(0, length, RUN)[:, None] * freqs[None, :]
    steps = np.arange(RUN)[:, None] * freqs[None, :]
    return (
        np.stack([np.cos(starts), np.sin(starts)]).astype(np.float32),
        np.stack([np.cos(steps), np.sin(steps)]).astype(np.float32),
    )


def run_turn(start_ref, step_ref, run):
    lane = lax.broadcasted_iota(jnp.int32, (RUN, 2 * HEAD_DIM), 1) % HEAD_DIM
    half_rot = ROT_DIM // 2
    cos_a, sin_a = start_ref[0, pl.ds(run, 1), :], start_ref[1, pl.ds(run, 1), :]
    cos_b, sin_b = step_ref[0], step_ref[1]
    cosine = cos_a * cos_b - sin_a * sin_b
    sine = sin_a * cos_b + cos_a * sin_b
    above = jnp.where(lane < half_rot, -sine, 0.0)
    below = jnp.where((lane >= half_rot) & (lane < ROT_DIM), sine, 0.0)
    return cosine, above, below


def turn(u, tables, way=1.0):
    cosine, above, below = tables
    half_rot = ROT_DIM // 2
    width = 2 * HEAD_DIM
    moved = pltpu.roll(u, width - half_rot, 1) * above + pltpu.roll(u, half_rot, 1) * below
    return u * cosine + way * moved


def masked_tile(scores, diagonal, start):
    last = jnp.where(diagonal, scores[:, start:], -1e30)
    return jnp.concatenate([scores[:, :start], last], axis=1) if start > 0 else last


def lower_triangle(tile):
    return lax.broadcasted_iota(jnp.int32, (tile, tile), 1) <= lax.broadcasted_iota(
        jnp.int32, (tile, tile), 0
    )


def head_lanes(tile, head):
    lanes = lax.broadcasted_iota(jnp.int32, (tile, 2 * HEAD_DIM), 1)
    return (lanes // HEAD_DIM) == head


def pick(mine, values):
    return jnp.where(mine, values, jnp.zeros_like(values))


def attend(q_s, k_s, v_s, ctx_s, lse_s):
    length = q_s.shape[0]
    tile = min(256, length)
    diagonal = lower_triangle(tile)
    for start in range(0, length, tile):
        rows, reach = slice(start, start + tile), start + tile
        context = jnp.zeros((tile, 2 * HEAD_DIM), F32)
        lse = jnp.zeros((tile, 2 * HEAD_DIM), F32)
        for head in range(2):
            mine = head_lanes(tile, head)
            scores = dot_nt(pick(mine, q_s[rows, :]), k_s[:reach, :])
            scores = masked_tile(scores, diagonal, start)
            peak = jnp.max(scores, axis=1, keepdims=True)
            exps = jnp.exp(scores - peak)
            total = jnp.sum(exps, axis=1, keepdims=True)
            probs_low = (exps * (1.0 / total)).astype(LOW)
            context = jnp.where(mine, dot_nn(probs_low, v_s[:reach, :]), context)
            lse = jnp.where(mine, peak + jnp.log(total), lse)
        ctx_s[rows, :] = context.astype(LOW)
        lse_s[rows, :] = lse


class Grid:
    def __init__(self, ctx_n, fsdp_n):
        self.ctx_n, self.fsdp_n = ctx_n, fsdp_n
        self.x_n = 1 << ((ctx_n.bit_length() - 1) // 2)
        self.z_n = ctx_n // self.x_n
        self.core_n = 2 if fsdp_n % 2 == 0 else 1
        self.y_n = fsdp_n // self.core_n
        self.undo = 1 if ctx_n % 3 == 1 else 2

    def locate(self):
        self.ctx, self.fsdp = lax.axis_index("ctx"), lax.axis_index("fsdp")
        self.z, self.x = self.ctx // self.x_n, self.ctx % self.x_n
        self.y, self.core = self.fsdp // self.core_n, self.fsdp % self.core_n
        return self

    def zx(self, dz, dx):
        return ((self.z + dz + self.z_n) % self.z_n) * self.x_n + (
            self.x + dx + self.x_n
        ) % self.x_n

    def yc(self, dy, dc):
        return ((self.y + dy + self.y_n) % self.y_n) * self.core_n + (
            self.core + dc + self.core_n
        ) % self.core_n

    def nearest(self, j):
        place = 0
        for z in range(self.z_n):
            order = sorted(range(self.z_n), key=lambda other: (abs(other - z), other))
            place = place + jnp.where(self.z == z, order[j], 0)
        return place

    def qkv_piece(self, ctx, fsdp, m):
        span = 3 * self.fsdp_n
        v = (3 * fsdp + m + span * self.ctx_n - ctx * self.fsdp_n) % span
        return ((v // self.fsdp_n) * self.undo) % 3, v % self.fsdp_n

    def qkv_owner(self, ctx, fsdp, m):
        kind, place = self.qkv_piece(ctx, fsdp, m)
        piece = self.ctx_n * self.fsdp_n * kind + ctx * self.fsdp_n + place
        return piece // 3 // self.fsdp_n

    def qkv_user(self, ctx, fsdp, m):
        piece = 3 * (ctx * self.fsdp_n + fsdp) + m
        return (piece % (self.ctx_n * self.fsdp_n)) // self.fsdp_n

    def greet(self):
        barrier = pltpu.get_barrier_semaphore()
        for k in range(1, self.ctx_n):
            pl.semaphore_signal(
                barrier, inc=1, device_id={"ctx": (self.ctx + k) % self.ctx_n}, device_id_type=MESH
            )
        for k in range(1, self.fsdp_n):
            pl.semaphore_signal(
                barrier,
                inc=1,
                device_id={"fsdp": (self.fsdp + k) % self.fsdp_n},
                device_id_type=MESH,
            )
        pl.semaphore_wait(barrier, self.ctx_n + self.fsdp_n - 2)


class Copies:
    def __init__(self, sems):
        self.sems, self.used, self.sent, self.perhaps = sems, 0, [], []

    def sem(self):
        self.used += 1
        return self.sems.at[self.used - 1]

    def send(self, src, dst, **where):
        send_sem, recv_sem = self.sem(), self.sem()
        copy = pltpu.make_async_remote_copy(
            src_ref=src,
            dst_ref=dst,
            send_sem=send_sem,
            recv_sem=recv_sem,
            device_id=where,
            device_id_type=MESH,
        )
        copy.start()
        self.sent.append(copy)
        return recv_sem

    def send_or_keep(self, src, dst, ctx, own_ctx):
        send_sem, recv_sem = self.sem(), self.sem()
        remote = pltpu.make_async_remote_copy(
            src_ref=src,
            dst_ref=dst,
            send_sem=send_sem,
            recv_sem=recv_sem,
            device_id={"ctx": ctx},
            device_id_type=MESH,
        )

        @pl.when(ctx != own_ctx)
        def _():
            remote.start()

        @pl.when(ctx == own_ctx)
        def _():
            pltpu.make_async_copy(src, dst, recv_sem).start()

        self.perhaps.append((ctx != own_ctx, remote))
        return recv_sem

    def prepare(self, src, dst, **where):
        send_sem, recv_sem = self.sem(), self.sem()
        remote = pltpu.make_async_remote_copy(
            src_ref=src,
            dst_ref=dst,
            send_sem=send_sem,
            recv_sem=recv_sem,
            device_id=where,
            device_id_type=MESH,
        )
        return remote, recv_sem

    def start_if(self, when, remote):
        @pl.when(when)
        def _():
            remote.start()

        self.perhaps.append((when, remote))

    def send_if(self, when, src, dst, **where):
        remote, recv_sem = self.prepare(src, dst, **where)
        self.start_if(when, remote)
        return recv_sem

    def local(self, src, dst):
        copy = pltpu.make_async_copy(src, dst, self.sem())
        copy.start()
        return copy

    def drain(self):
        for copy in self.sent:
            copy.wait_send()
        for sent, copy in self.perhaps:

            @pl.when(sent)
            def _(copy=copy):
                copy.wait_send()


def arrived(ref, sem):
    pltpu.make_async_copy(ref, ref, sem).wait()


class TokenGather:
    def __init__(self, grid, copies, own, buffer):
        self.grid, self.copies, self.buffer = grid, copies, buffer
        self.rows = own.shape[0]
        self.across = []
        self.kept = copies.local(own, self.slot(0, 0))
        self.along = {
            way: copies.send_if(self.ends(way), own, self.slot(0, 0), ctx=grid.zx(way, 0))
            for way in (1, -1)
        }
        for l in range(1, grid.x_n):
            sem = copies.send(own, self.slot(0, 0), ctx=grid.zx(0, l))
            self.across.append((0, 1, l, sem))

    def slot(self, k, l):
        start = pl.multiple_of(self.grid.zx(-k, -l) * self.rows, self.rows)
        return self.buffer.at[pl.ds(start, self.rows)]

    def ends(self, way):
        return self.grid.z < self.grid.z_n - 1 if way > 0 else self.grid.z > 0

    def has(self, k, way):
        z = self.grid.z
        return z >= k if way > 0 else z + k < self.grid.z_n

    def step(self, k):
        grid, copies, along = self.grid, self.copies, {}
        for way in (1, -1):
            slot, here = self.slot(k * way, 0), self.has(k, way)

            @pl.when(here)
            def _(slot=slot, way=way):
                arrived(slot, self.along[way])

            if k < grid.z_n - 1:
                along[way] = copies.send_if(
                    here & self.ends(way), slot, slot, ctx=grid.zx(way, 0)
                )
            for l in range(1, grid.x_n):
                sem = copies.send_if(here, slot, slot, ctx=grid.zx(0, l))
                self.across.append((k, way, l, sem))
        self.along = along

    def ready(self, k):
        if k == 0:
            self.kept.wait()
        for m, way, l, sem in self.across:
            if m == k:

                @pl.when(self.has(k, way))
                def _(way=way, l=l, sem=sem):
                    arrived(self.slot(k * way, l), sem)


class ShardGather:
    def __init__(self, grid, copies, own, view):
        self.grid, self.copies, self.view = grid, copies, view
        self.along_y = [
            copies.send(own, view(grid.fsdp), fsdp=grid.yc(k, 0)) for k in range(1, grid.y_n)
        ]
        self.across = []
        self.cross(own, 0)

    def cross(self, src, k):
        for c in range(1, self.grid.core_n):
            slot = self.view(self.grid.yc(-k, 0))
            self.across.append((k, c, self.copies.send(src, slot, fsdp=self.grid.yc(0, c))))

    def forward(self):
        for k in range(1, self.grid.y_n):
            slot = self.view(self.grid.yc(-k, 0))
            arrived(slot, self.along_y[k - 1])
            self.cross(slot, k)

    def finish(self):
        for k, c, sem in self.across:
            arrived(self.view(self.grid.yc(-k, -c)), sem)


def gather_kernel(
    shape, x_in, g_in, wq_in, wu_in, wf_in, wd_in,
    small_in, row_in, column_in, start_in, step_in,
    x_out, g_out, wi_out, wu_out, wo_out, small_out, normed_out, hidden_out, slope_out,
    qkv_out, lse_out, stats_out,
    x_s, g_s, wi_s, wu_s, wo_s, normed_s, hidden_s, slope_s, qkv_s, lse_s, stats_s,
    mixed_s, ctx_s, small_f, qkv_bias_s, up_bias_s, small_s, small_x, small_core, small_y, small_z, sems,
):
    grid = Grid(*shape).locate()
    copies = Copies(sems)
    local_len, width = x_in.shape
    unit, up_rows = wd_in.shape[0], wu_in.shape[0]
    fw, dw = wf_in.shape[1] // grid.ctx_n, wd_in.shape[1] // grid.ctx_n
    n = grid.ctx_n * grid.fsdp_n
    me = grid.ctx * grid.fsdp_n + grid.fsdp
    peers = [(k, l) for k in range(grid.z_n) for l in range(grid.x_n) if k or l]
    pairs = dw // (2 * HEAD_DIM)
    puts = []

    row_index = lax.broadcasted_iota(jnp.int32, (16, width), 0)
    placed = jnp.zeros((16, width), F32)
    pieces_in = small_in[...].astype(F32)
    for row, (base, each) in enumerate(SMALL_ROWS):
        piece = each[0] * me + each[1]
        value = jnp.broadcast_to(pieces_in[row : row + 1, :], (16, width))
        value = pltpu.roll(value, (piece % n) * unit, 1)
        placed = placed + jnp.where(row_index == piece // n + base, value, 0.0)
    small_s[0] = placed.astype(LOW)
    grid.greet()

    def small_sum(step, buffer, stage):
        for i, sem in enumerate(stage):
            arrived(buffer.at[i], sem)
        accumulate(
            small_s.at[step + 1], small_s.at[step], *[buffer.at[i] for i in range(len(stage))]
        )

    stage = [
        copies.send(small_s.at[0], small_y.at[k - 1], fsdp=grid.yc(k, 0))
        for k in range(1, grid.y_n)
    ]

    def up_slot(f):
        return wu_s.at[pl.ds(pl.multiple_of(f * up_rows, up_rows), up_rows)]

    up_kept = copies.local(wu_in, up_slot(grid.fsdp))
    up = ShardGather(grid, copies, wu_in, up_slot)
    qkv_sems = []

    def piece_slot(ctx, fsdp, m):
        kind, place = grid.qkv_piece(ctx, fsdp, m)
        return wi_s.at[pl.ds(pl.multiple_of((kind * grid.fsdp_n + place) * unit, unit), unit)]

    for m in range(3):
        user = grid.qkv_user(grid.ctx, grid.fsdp, m)
        qkv_sems.append(
            copies.send_or_keep(
                wq_in.at[pl.ds(m * unit, unit)],
                piece_slot(user, grid.fsdp, m),
                user,
                grid.ctx,
            )
        )
    small_sum(0, small_y, stage)
    stage = [
        copies.send(small_s.at[1], small_x.at[l - 1], ctx=grid.zx(0, l))
        for l in range(1, grid.x_n)
    ]
    tokens_x = TokenGather(grid, copies, x_in, x_s)
    small_sum(1, small_x, stage)
    stage = [
        copies.send(small_s.at[2], small_core.at[c - 1], fsdp=grid.yc(0, c))
        for c in range(1, grid.core_n)
    ]
    small_sum(2, small_core, stage)
    stage = [
        copies.send(small_s.at[3], small_z.at[k - 1], ctx=grid.zx(k, 0))
        for k in range(1, grid.z_n)
    ]

    def column_block(ref, index, block):
        return ref.at[:, pl.ds(pl.multiple_of(index * block, 128), block)]

    mine = wo_s.at[grid.ctx, grid.fsdp]
    own_out = [
        copies.local(column_block(wf_in, grid.ctx, fw), mine.at[:, pl.ds(0, fw)]),
        copies.local(column_block(wd_in, grid.ctx, dw), mine.at[:, pl.ds(fw, dw)]),
    ]
    out_sems = {}

    def send_out(k):
        for l in range(grid.x_n):
            if k or l:
                target = grid.zx(k, l)
                out_sems[k, l] = (
                    copies.send(
                        column_block(wf_in, target, fw), mine.at[:, pl.ds(0, fw)], ctx=target
                    ),
                    copies.send(
                        column_block(wd_in, target, dw), mine.at[:, pl.ds(fw, dw)], ctx=target
                    ),
                )

    shards = []

    def spread_out(k):
        first = ((grid.z - k + grid.z_n) % grid.z_n) * grid.x_n
        for l in range(grid.x_n):
            slot = wo_s.at[grid.zx(-k, -l), grid.fsdp]
            if k or l:
                arrived(slot.at[:, pl.ds(0, fw)], out_sems[k, l][0])
                arrived(slot.at[:, pl.ds(fw, dw)], out_sems[k, l][1])
            else:
                own_out[0].wait()
                own_out[1].wait()

        def out_view(f):
            return wo_s.at[pl.ds(first, grid.x_n), f]

        shards.append(ShardGather(grid, copies, out_view(grid.fsdp), out_view))

    group = grid.x_n * local_len

    def group_rows(k):
        return pl.multiple_of(grid.nearest(k) * group, group)

    def normalize(k):
        first = group_rows(k)
        gain, shift = small_f[0:1, :], small_f[1:2, :]

        @pl.loop(0, group // 16)
        def _(i):
            rows = pl.ds(pl.multiple_of(first + i * 16, 16), 16)
            wide = x_s[rows, :].astype(F32)
            mean = jnp.mean(wide, axis=-1, keepdims=True)
            centered = wide - mean
            spread = lax.rsqrt(jnp.mean(centered * centered, axis=-1, keepdims=True) + EPSILON)
            normed_s[rows, :] = (centered * spread * gain + shift).astype(LOW)
            lane = lax.broadcasted_iota(jnp.int32, (16, 2 * HEAD_DIM), 1)
            stats_s[rows, :] = jnp.where(lane < HEAD_DIM, mean, spread)

    tile_rows = min(256, group)

    def project_up(k):
        first = group_rows(k)
        block = min(256, fw)

        @pl.loop(0, (group // tile_rows) * (fw // block))
        def _(i):
            part, col = i // (fw // block), (i % (fw // block)) * block
            rows = pl.ds(pl.multiple_of(first + part * tile_rows, tile_rows), tile_rows)
            cols = pl.ds(pl.multiple_of(col, block), block)
            bias = up_bias_s[i % (fw // block), 0:1, :]
            upward = dot_nt(normed_s[rows, :], wu_s[cols, :]) + bias
            square = upward * upward
            bend = jnp.tanh(0.7978845608028654 * (upward + 0.044715 * square * upward))
            half = 0.5 * (1.0 + bend)
            hidden_s[rows, cols] = (upward * half).astype(LOW)
            inner_slope = 0.7978845608028654 * (1.0 + 3.0 * 0.044715 * square)
            slope = half + 0.5 * upward * (1.0 - bend * bend) * inner_slope
            slope_s[rows, cols] = slope.astype(LOW)

    def project_qkv(k):
        first = group_rows(k)

        @pl.loop(0, group // tile_rows)
        def _(i):
            start = pl.multiple_of(first + i * tile_rows, tile_rows)
            rows = pl.ds(start, tile_rows)
            for kind in range(3):
                result = dot_nt(normed_s[rows, :], wi_s[kind * dw : (kind + 1) * dw, :])
                result = result + qkv_bias_s[kind, 0:1, :]
                if kind == 2:
                    mixed_s[rows, kind * dw : (kind + 1) * dw] = result.astype(LOW)
                    continue
                for run in range(tile_rows // RUN):
                    tables = run_turn(start_in, step_in, start // RUN + run)
                    run_at = pl.ds(pl.multiple_of(start + run * RUN, RUN), RUN)
                    for p in range(pairs):
                        lanes = slice(p * 2 * HEAD_DIM, (p + 1) * 2 * HEAD_DIM)
                        turned = turn(result[run * RUN : (run + 1) * RUN, lanes], tables)
                        low = turned.astype(LOW)
                        if kind == 0:
                            low = (low * SCORE_SCALE).astype(LOW)
                        at = kind * dw + p * 2 * HEAD_DIM
                        mixed_s[run_at, at : at + 2 * HEAD_DIM] = low

    for k in range(grid.z_n):
        send_out(k)
    tokens_g = TokenGather(grid, copies, g_in, g_s)
    tokens_x.step(1)
    pieces = []
    for m in range(3):
        arrived(piece_slot(grid.ctx, grid.fsdp, m), qkv_sems[m])
        pieces.append(
            ShardGather(
                grid,
                copies,
                piece_slot(grid.ctx, grid.fsdp, m),
                lambda f, m=m: piece_slot(grid.ctx, f, m),
            )
        )
    up.forward()
    small_sum(3, small_z, stage)
    puts.append(copies.local(small_s.at[4], small_out))
    small_f[...] = small_s[4].astype(F32)
    for kind in range(3):
        at = pl.ds(pl.multiple_of(grid.ctx * dw, 128), dw)
        row = small_f[4 + kind : 5 + kind, at]
        qkv_bias_s[kind] = jnp.broadcast_to(row, qkv_bias_s.shape[1:])
    block = up_bias_s.shape[2]
    for i in range(fw // block):
        offset = grid.ctx * fw
        at = pl.ds(pl.multiple_of(offset % width + i * block, 128), block)
        row = jnp.zeros((1, block), F32)
        for j in range(4):
            row = row + jnp.where(offset // width == j, small_f[7 + j : 8 + j, at], 0.0)
        up_bias_s[i] = jnp.broadcast_to(row, up_bias_s.shape[1:])
    tokens_x.ready(0)
    normalize(0)
    up_kept.wait()
    up.finish()
    puts.append(copies.local(wu_s, wu_out))
    project_up(0)
    for gather in pieces:
        gather.forward()
    spread_out(0)
    tokens_x.ready(1)
    normalize(1)
    project_up(1)
    for gather in pieces:
        gather.finish()
    puts.append(copies.local(wi_s, wi_out))
    project_qkv(0)
    project_qkv(1)
    tokens_g.step(1)
    for k in range(2, grid.z_n):
        tokens_x.step(k)
        spread_out(k - 1)
        tokens_g.step(k)
        shards[k - 2].forward()
    spread_out(grid.z_n - 1)
    shards[grid.z_n - 2].forward()
    for k in range(2, grid.z_n):
        tokens_x.ready(k)
        normalize(k)
        project_up(k)
        project_qkv(k)
        if k == 2:
            shards[grid.z_n - 1].forward()
    puts.append(copies.local(x_s, x_out))
    puts.append(copies.local(normed_s, normed_out))
    puts.append(copies.local(slope_s, slope_out))
    puts.append(copies.local(stats_s, stats_out))
    length = x_s.shape[0]
    pair = 2 * HEAD_DIM

    tall = min(256, length)

    @pl.loop(0, length // tall)
    def _(i):
        start = pl.multiple_of(i * tall, tall)
        result = dot_nn(to_sorted(row_in, start, tall), mixed_s[...]).astype(LOW)
        for kind in range(3):
            for p in range(pairs):
                at = kind * dw + p * pair
                qkv_s[kind, p, pl.ds(start, tall), :] = result[:, at : at + pair]

    @pl.loop(0, pairs)
    def _(p):
        attend(qkv_s.at[0, p], qkv_s.at[1, p], qkv_s.at[2, p], ctx_s.at[p], lse_s.at[p])

    @pl.loop(0, length // tall)
    def _(i):
        start = pl.multiple_of(i * tall, tall)
        back = to_stored(column_in, start, tall)
        for p in range(pairs):
            at = slice(fw + p * pair, fw + (p + 1) * pair)
            hidden_s[pl.ds(start, tall), at] = dot_nn(back, ctx_s[p]).astype(LOW)

    puts.append(copies.local(hidden_s, hidden_out))
    puts.append(copies.local(qkv_s, qkv_out))
    puts.append(copies.local(lse_s, lse_out))
    for gather in shards:
        gather.finish()
    puts.append(copies.local(wo_s, wo_out))
    for k in range(grid.z_n):
        tokens_g.ready(k)
    puts.append(copies.local(g_s, g_out))
    for put in puts:
        put.wait()
    copies.drain()


def accumulate(dst, *sources):
    if len(dst.shape) == 3:

        @pl.loop(0, dst.shape[0])
        def _(i):
            accumulate(dst.at[i], *[source.at[i] for source in sources])

        return
    rows, step = dst.shape[0], 16

    @pl.loop(0, rows // step)
    def _(i):
        part = pl.ds(pl.multiple_of(i * step, step), step)
        total = sources[0][part, :].astype(F32)
        for source in sources[1:]:
            total = total + source[part, :].astype(F32)
        dst[part, :] = total.astype(dst.dtype)


class TokenScatter:
    def __init__(self, grid, copies, parts, from_x, from_z, total):
        self.grid, self.copies, self.parts = grid, copies, parts
        self.from_x, self.from_z, self.total = from_x, from_z, total
        self.rows = total.shape[0]
        self.along_x, self.sems = {}, {}
        self.order = [t for i in range(grid.z_n // 2) for t in (grid.z_n - 1 - i, i)]

    def block(self, t, dx):
        x = (self.grid.x + dx) % self.grid.x_n
        return self.parts.at[t, pl.ds(pl.multiple_of(x * self.rows, self.rows), self.rows)]

    def launch(self, t):
        for l in range(1, self.grid.x_n):
            self.along_x[t, l] = self.copies.send(
                self.block(t, l), self.from_x.at[t, l - 1], ctx=self.grid.zx(0, l)
            )

    def collect(self, t):
        terms = [self.block(t, 0)]
        for l in range(1, self.grid.x_n):
            arrived(self.from_x.at[t, l - 1], self.along_x[t, l])
            terms.append(self.from_x.at[t, l - 1])
        accumulate(terms[0], *terms)

    def climb(self, t):
        grid, own, slot = self.grid, self.block(t, 0), self.from_z.at[t]
        remote, sem = self.copies.prepare(own, slot, ctx=grid.zx(1, 0))

        @pl.when((grid.z < t) & (grid.z > 0))
        def _():
            arrived(slot, sem)
            accumulate(own, own, slot)

        self.copies.start_if(grid.z < t, remote)
        self.sems[t, 1] = sem

    def descend(self, t):
        grid, own, slot = self.grid, self.block(t, 0), self.from_z.at[t]
        there = self.from_z.at[jnp.where(grid.z - 1 == t, grid.z_n, t)]
        remote, sem = self.copies.prepare(own, there, ctx=grid.zx(-1, 0))

        @pl.when((grid.z > t) & (grid.z < grid.z_n - 1))
        def _():
            arrived(slot, sem)
            accumulate(own, own, slot)

        self.copies.start_if(grid.z > t, remote)
        self.sems[t, -1] = sem

    def step(self, i):
        last = self.grid.z_n - 1
        self.collect(self.order[i])
        known = self.order[: i + 1]
        for t in range(last, 0, -1):
            ready = [u for u in known if u >= t]
            if len(ready) == last - t + 1 and (t, 1) not in self.sems and t in known:
                self.climb(t)
        for t in range(last):
            ready = [u for u in known if u <= t]
            if len(ready) == t + 1 and (t, -1) not in self.sems and t in known:
                self.descend(t)

    def finish(self):
        grid = self.grid
        for t in range(grid.z_n):

            @pl.when(grid.z == t)
            def _(t=t):
                terms = [self.block(t, 0)]
                if t > 0:
                    arrived(self.from_z.at[t], self.sems[t, 1])
                    terms.append(self.from_z.at[t])
                if t < grid.z_n - 1:
                    arrived(self.from_z.at[grid.z_n], self.sems[t, -1])
                    terms.append(self.from_z.at[grid.z_n])
                accumulate(self.total, *terms)


class ShardScatter:
    def __init__(self, grid, copies, views, from_core, from_y):
        self.grid, self.copies, self.views = grid, copies, views
        self.from_core, self.from_y = from_core, from_y
        self.rounds = list(range(1, grid.y_n)) + [0]
        self.across = {
            k: [
                copies.send(part, from_core.at[k, i], fsdp=grid.yc(0, 1))
                for i, part in enumerate(views(grid.yc(k, 1)))
            ]
            for k in self.rounds
        }
        self.along_y = {}

    def step(self, k):
        for i, part in enumerate(self.views(self.grid.yc(k, 0))):
            arrived(self.from_core.at[k, i], self.across[k][i])
            accumulate(part, part, self.from_core.at[k, i])
            if k > 0:
                self.along_y[k, i] = self.copies.send(
                    part, self.from_y.at[k - 1, i], fsdp=self.grid.yc(k, 0)
                )

    def finish(self):
        for i, part in enumerate(self.views(self.grid.fsdp)):
            for k in range(1, self.grid.y_n):
                arrived(self.from_y.at[k - 1, i], self.along_y[k, i])
            accumulate(
                part, part, *[self.from_y.at[k - 1, i] for k in range(1, self.grid.y_n)]
            )


def to_sorted(row_ref, start, tile):
    length = row_ref.shape[1]
    place = lax.broadcasted_iota(jnp.int32, (tile, length), 0) + start
    return jnp.where(place == row_ref[0:1, :], 1.0, 0.0).astype(LOW)


def to_stored(column_ref, start, tile):
    length = column_ref.shape[0]
    place = lax.broadcasted_iota(jnp.int32, (tile, length), 1)
    return jnp.where(place == column_ref[pl.ds(start, tile), :], 1.0, 0.0).astype(LOW)


def run_rows(i):
    return pl.ds(pl.multiple_of(i * RUN, RUN), RUN)


def attend_back(q_s, k_s, v_s, lse_s, g_s, dq_s, dk_s, dv_s):
    length = q_s.shape[0]
    dk_s[...] = jnp.zeros_like(dk_s)
    dv_s[...] = jnp.zeros_like(dv_s)
    tile = min(256, length)
    diagonal = lower_triangle(tile)
    for start in range(0, length, tile):
        rows, reach = slice(start, start + tile), start + tile
        grad_q = jnp.zeros((tile, 2 * HEAD_DIM), F32)
        for head in range(2):
            mine = head_lanes(tile, head)
            q_own, g_own = pick(mine, q_s[rows, :]), pick(mine, g_s[rows, :])
            lse = lse_s[rows, head * HEAD_DIM : head * HEAD_DIM + 1]
            scores = masked_tile(dot_nt(q_own, k_s[:reach, :]), diagonal, start)
            probs = jnp.exp(scores - lse)
            grad_probs = dot_nt(g_own, v_s[:reach, :])
            inner = jnp.sum(probs * grad_probs, axis=1, keepdims=True)
            grad_scores = (probs * (grad_probs - inner)).astype(LOW)
            grad_q = jnp.where(mine, dot_nn(grad_scores, k_s[:reach, :]), grad_q)
            dk_s[:reach, :] += dot_tn(grad_scores, q_own)
            dv_s[:reach, :] += dot_tn(probs.astype(LOW), g_own)
        dq_s[rows, :] = grad_q * SCORE_SCALE


def scatter_out_kernel(
    shape, hidden_in, wo_in, g_in, slope_in, qkv_in, lse_in,
    row_in, column_in, start_in, step_in,
    total_out, go_out, gup_out, gm_out,
    hidden_s, wo_s, g_s, slope_s, qkv_s, lse_s, po_s, po_x, po_z, po_sum,
    go_s, go_core, go_y, go_got, gup_s, gctx_s, gm_s, sorted_s, turned_s, dq_s, dk_s, dv_s, sems,
):
    grid = Grid(*shape).locate()
    copies = Copies(sems)
    length, fw = gup_s.shape
    dw = gctx_s.shape[1]
    width, cols = wo_s.shape
    pair = 2 * HEAD_DIM
    loads = [
        copies.local(src, dst)
        for src, dst in (
            (hidden_in, hidden_s), (wo_in, wo_s), (g_in, g_s),
            (slope_in, slope_s), (qkv_in, qkv_s), (lse_in, lse_s),
        )
    ]
    grid.greet()
    loads[0].wait()
    loads[1].wait()
    group = po_s.shape[1]
    tile = min(256, group)
    tokens = TokenScatter(grid, copies, po_s, po_x, po_z, po_sum)
    for t in tokens.order:

        @pl.loop(0, (group // tile) * (width // 256))
        def _(i, t=t):
            part = pl.multiple_of((i // (width // 256)) * tile, tile)
            at = pl.ds(pl.multiple_of((i % (width // 256)) * 256, 256), 256)
            rows = pl.ds(pl.multiple_of(t * group + part, tile), tile)
            result = dot_nt(hidden_s[rows, :], wo_s[at, :])
            po_s[t, pl.ds(part, tile), at] = result.astype(LOW)

        tokens.launch(t)
    loads[2].wait()
    unit = go_s.shape[2]
    block = grid.fsdp_n * unit

    @pl.loop(0, grid.ctx_n)
    def _(c):
        at = pl.ds(pl.multiple_of(c * block, block), block)
        result = dot_tn(g_s[:, at], hidden_s[...]).astype(LOW)
        go_s[c] = result.reshape(grid.fsdp_n, unit, cols)

    shards = ShardScatter(grid, copies, lambda f: [go_s.at[:, f]], go_core, go_y)
    tokens.step(0)
    for k in shards.rounds:
        shards.step(k)
    tokens.step(1)
    loads[3].wait()
    tall = min(256, length)

    @pl.loop(0, (length // tall) * (fw // 256))
    def _(i):
        rows = pl.ds(pl.multiple_of((i // (fw // 256)) * tall, tall), tall)
        at = pl.ds(pl.multiple_of((i % (fw // 256)) * 256, 256), 256)
        grad = dot_nn(g_s[rows, :], wo_s[:, at])
        gup_s[rows, at] = (grad * slope_s[rows, at].astype(F32)).astype(LOW)

    @pl.loop(0, length // tall)
    def _(i):
        rows = pl.ds(pl.multiple_of(i * tall, tall), tall)
        gctx_s[rows, :] = dot_nn(g_s[rows, :], wo_s[:, pl.ds(fw, dw)]).astype(LOW)

    puts = [copies.local(gup_s, gup_out)]
    for i in range(2, grid.z_n):
        tokens.step(i)
    shards.finish()
    peers = [(k, l) for k in range(grid.z_n) for l in range(grid.x_n) if k or l]
    own_o = copies.local(go_s.at[grid.ctx, grid.fsdp], go_got.at[grid.ctx])
    out_sems = [
        copies.send(go_s.at[grid.zx(k, l), grid.fsdp], go_got.at[grid.ctx], ctx=grid.zx(k, l))
        for k, l in peers
    ]
    loads[4].wait()
    loads[5].wait()

    pairs = dw // pair

    @pl.loop(0, length // tall)
    def _(i):
        start = pl.multiple_of(i * tall, tall)
        result = dot_nn(to_sorted(row_in, start, tall), gctx_s[...]).astype(LOW)
        for p in range(pairs):
            sorted_s[p, pl.ds(start, tall), :] = result[:, p * pair : (p + 1) * pair]

    @pl.loop(0, pairs)
    def _(p):
        attend_back(
            qkv_s.at[0, p], qkv_s.at[1, p], qkv_s.at[2, p], lse_s.at[p],
            sorted_s.at[p], dq_s, dk_s, dv_s,
        )

        @pl.loop(0, length // RUN)
        def _(i):
            tables, rows = run_turn(start_in, step_in, i), run_rows(i)
            turned_s[0, p, rows, :] = turn(dq_s[rows, :], tables, -1.0).astype(LOW)
            turned_s[1, p, rows, :] = turn(dk_s[rows, :], tables, -1.0).astype(LOW)
            turned_s[2, p, rows, :] = dv_s[rows, :].astype(LOW)

    @pl.loop(0, length // tall)
    def _(i):
        start = pl.multiple_of(i * tall, tall)
        back = to_stored(column_in, start, tall)
        for kind in range(3):
            for p in range(pairs):
                at = kind * dw + p * pair
                result = dot_nn(back, turned_s[kind, p])
                gm_s[pl.ds(start, tall), at : at + pair] = result.astype(LOW)

    puts.append(copies.local(gm_s, gm_out))
    tokens.finish()
    puts.append(copies.local(po_sum, total_out))
    own_o.wait()
    for (k, l), sem in zip(peers, out_sems):
        arrived(go_got.at[grid.zx(-k, -l)], sem)
    puts.append(copies.local(go_got, go_out))
    for put in puts:
        put.wait()
    copies.drain()


def scatter_in_kernel(
    shape, gm_in, wi_in, gup_in, wu_in, x_in, stats_in, normed_in, g_own_in,
    total_out, gu_out, gi_out, small_out,
    gm_s, wi_s, gup_s, wu_s, x_s, stats_s, normed_s, g_own_s, pn_s, pn_x, pn_z, pn_sum,
    gu_s, gu_core, gu_y, gi_s, gi_core, gi_y, gi_got,
    small_s, small_y, small_x, small_core, small_z, sems,
):
    grid = Grid(*shape).locate()
    copies = Copies(sems)
    length, fw = gup_s.shape
    width = wi_s.shape[1]
    dw = gm_s.shape[1] // 3
    unit = gi_got.shape[1]
    up_rows = fw // grid.fsdp_n
    loads = [
        copies.local(src, dst)
        for src, dst in (
            (gm_in, gm_s), (wi_in, wi_s), (gup_in, gup_s), (wu_in, wu_s),
            (x_in, x_s), (stats_in, stats_s), (normed_in, normed_s), (g_own_in, g_own_s),
        )
    ]
    grid.greet()
    small_s[0] = jnp.zeros_like(small_s[0])
    for load in loads[:6]:
        load.wait()
    group = pn_s.shape[1]
    tile = min(256, group)
    tokens = TokenScatter(grid, copies, pn_s, pn_x, pn_z, pn_sum)
    for t in tokens.order:

        @pl.loop(0, (group // tile) * (width // 256))
        def _(i, t=t):
            part = pl.multiple_of((i // (width // 256)) * tile, tile)
            at = pl.ds(pl.multiple_of((i % (width // 256)) * 256, 256), 256)
            rows = pl.ds(pl.multiple_of(t * group + part, tile), tile)
            grad = dot_nn(gm_s[rows, :], wi_s[:, at]) + dot_nn(gup_s[rows, :], wu_s[:, at])
            pn_s[t, pl.ds(part, tile), at] = grad.astype(LOW)
            mean, spread = stats_s[rows, 0:1], stats_s[rows, HEAD_DIM : HEAD_DIM + 1]
            xhat = (x_s[rows, at].astype(F32) - mean) * spread
            small_s[0, 0:1, at] += jnp.sum(grad * xhat, axis=0, keepdims=True)
            small_s[0, 1:2, at] += jnp.sum(grad, axis=0, keepdims=True)

        tokens.launch(t)
    for load in loads[6:]:
        load.wait()

    small_s[0, 2:3, :] = jnp.sum(g_own_s[...].astype(F32), axis=0, keepdims=True)
    for kind in range(3):
        at = pl.ds(pl.multiple_of(grid.ctx * dw, 128), dw)
        terms = gm_s[:, kind * dw : (kind + 1) * dw].astype(F32)
        small_s[0, 4 + kind : 5 + kind, at] = jnp.sum(terms, axis=0, keepdims=True)
    offset = grid.ctx * fw
    at = pl.ds(pl.multiple_of(offset % width, 128), fw)
    terms = jnp.sum(gup_s[...].astype(F32), axis=0, keepdims=True)
    for row in range(4):
        small_s[0, 7 + row : 8 + row, at] = jnp.where(offset // width == row, terms, 0.0)

    def small_sum(step, buffer, stage):
        for i, sem in enumerate(stage):
            arrived(buffer.at[i], sem)
        accumulate(
            small_s.at[step + 1], small_s.at[step], *[buffer.at[i] for i in range(len(stage))]
        )

    stage = [
        copies.send(small_s.at[0], small_y.at[k - 1], fsdp=grid.yc(k, 0))
        for k in range(1, grid.y_n)
    ]

    @pl.loop(0, 3 * dw // 128)
    def _(i):
        at = pl.ds(pl.multiple_of(i * 128, 128), 128)
        gi_s[at, :] = dot_tn(gm_s[:, at], normed_s[...]).astype(LOW)

    def piece_slot(f, m):
        kind, place = grid.qkv_piece(grid.ctx, f, m)
        return gi_s.at[pl.ds(pl.multiple_of((kind * grid.fsdp_n + place) * unit, unit), unit)]

    shards_i = ShardScatter(
        grid, copies, lambda f: [piece_slot(f, m) for m in range(3)], gi_core, gi_y
    )
    tokens.step(0)
    small_sum(0, small_y, stage)
    stage = [
        copies.send(small_s.at[1], small_core.at[c - 1], fsdp=grid.yc(0, c))
        for c in range(1, grid.core_n)
    ]
    for k in shards_i.rounds:
        shards_i.step(k)

    @pl.loop(0, fw // 128)
    def _(i):
        at = pl.ds(pl.multiple_of(i * 128, 128), 128)
        gu_s[at, :] = dot_tn(gup_s[:, at], normed_s[...]).astype(LOW)

    def up_slot(f):
        return gu_s.at[pl.ds(pl.multiple_of(f * up_rows, up_rows), up_rows)]

    shards_u = ShardScatter(grid, copies, lambda f: [up_slot(f)], gu_core, gu_y)
    tokens.step(1)
    small_sum(1, small_core, stage)
    stage = [
        copies.send(small_s.at[2], small_x.at[l - 1], ctx=grid.zx(0, l))
        for l in range(1, grid.x_n)
    ]
    for k in shards_u.rounds:
        shards_u.step(k)
    tokens.step(2)
    shards_i.finish()
    qkv_sems = []
    for m in range(3):
        owner = grid.qkv_owner(grid.ctx, grid.fsdp, m)
        qkv_sems.append(
            copies.send_or_keep(piece_slot(grid.fsdp, m), gi_got.at[m], owner, grid.ctx)
        )
    for i in range(3, grid.z_n):
        tokens.step(i)
    small_sum(2, small_x, stage)
    stage = [
        copies.send(small_s.at[3], small_z.at[k - 1], ctx=grid.zx(k, 0))
        for k in range(1, grid.z_n)
    ]
    shards_u.finish()
    puts = [copies.local(up_slot(grid.fsdp), gu_out)]
    tokens.finish()
    puts.append(copies.local(pn_sum, total_out))
    for m in range(3):
        arrived(gi_got.at[m], qkv_sems[m])
    puts.append(copies.local(gi_got, gi_out))
    small_sum(3, small_z, stage)
    puts.append(copies.local(small_s.at[4], small_out))
    for put in puts:
        put.wait()
    copies.drain()


def solution(mesh):
    shape = mesh.shape["ctx"], mesh.shape["fsdp"]
    ctx_n, fsdp_n = shape
    n = ctx_n * fsdp_n
    plan = Grid(*shape)
    x_n, z_n, core_n, y_n = plan.x_n, plan.z_n, plan.core_n, plan.y_n

    def gather(x_own, g_own, w_qkv, w_fc1, w_fc2, w_dense, small, tables):
        local_len, width = x_own.shape
        unit, hidden_units = w_fc2.shape
        length = ctx_n * local_len
        fw, dw = hidden_units // ctx_n, width // ctx_n
        pair = 2 * HEAD_DIM
        small_rows = jax.ShapeDtypeStruct((16, width), LOW)
        kept = [
            jax.ShapeDtypeStruct((length, width), LOW),
            jax.ShapeDtypeStruct((length, width), LOW),
            jax.ShapeDtypeStruct((3 * fsdp_n * unit, width), LOW),
            jax.ShapeDtypeStruct((fw, width), LOW),
            jax.ShapeDtypeStruct((ctx_n, fsdp_n, unit, fw + dw), LOW),
        ]
        made = [
            jax.ShapeDtypeStruct((length, width), LOW),
            jax.ShapeDtypeStruct((length, fw + dw), LOW),
            jax.ShapeDtypeStruct((length, fw), LOW),
            jax.ShapeDtypeStruct((3, dw // pair, length, pair), LOW),
            jax.ShapeDtypeStruct((dw // pair, length, pair), F32),
            jax.ShapeDtypeStruct((length, pair), F32),
        ]
        return pl.pallas_call(
            functools.partial(gather_kernel, shape),
            out_shape=kept + [small_rows] + made,
            in_specs=[anywhere] * 6 + [inside] * 5,
            out_specs=[anywhere] * 12,
            scratch_shapes=[pltpu.VMEM(s.shape, s.dtype) for s in kept + made]
            + [pltpu.VMEM((length, 3 * dw), LOW), pltpu.VMEM((dw // pair, length, pair), LOW)]
            + [pltpu.VMEM((16, width), F32), pltpu.VMEM((3, 8, dw), F32)]
            + [pltpu.VMEM((max(fw // 256, 1), 8, min(fw, 256)), F32)]
            + [pltpu.VMEM((count, 16, width), LOW) for count in (5, x_n, core_n, y_n, z_n)]
            + [pltpu.SemaphoreType.DMA((SEMAPHORES,))],
            compiler_params=pltpu.CompilerParams(
                collective_id=0, has_side_effects=True, vmem_limit_bytes=VMEM_BYTES
            ),
            name="gather",
        )(x_own, g_own, w_qkv, w_fc1, w_fc2, w_dense, small, *tables)

    def token_scratch(local_len, width):
        return [
            pltpu.VMEM((z_n, x_n * local_len, width), LOW),
            pltpu.VMEM((z_n, max(x_n - 1, 1), local_len, width), LOW),
            pltpu.VMEM((z_n + 1, local_len, width), LOW),
            pltpu.VMEM((local_len, width), F32),
        ]

    def shard_scratch(parts, *block):
        return [
            pltpu.VMEM((y_n, parts) + block, LOW),
            pltpu.VMEM((max(y_n - 1, 1), parts) + block, LOW),
        ]

    def inside_like(*arrays):
        return [pltpu.VMEM(a.shape, a.dtype) for a in arrays]

    anywhere = pl.BlockSpec(memory_space=pl.ANY)
    inside = pl.BlockSpec(memory_space=pltpu.VMEM)

    def scatter_out(hidden, wo, g_all, slope, qkv, lse, tables):
        length, cols = hidden.shape
        local_len, width = length // ctx_n, g_all.shape[1]
        unit = width // n
        fw = slope.shape[1]
        dw, pair = cols - fw, 2 * HEAD_DIM
        return pl.pallas_call(
            functools.partial(scatter_out_kernel, shape),
            out_shape=[
                jax.ShapeDtypeStruct((local_len, width), F32),
                jax.ShapeDtypeStruct((ctx_n, unit, cols), LOW),
                jax.ShapeDtypeStruct((length, fw), LOW),
                jax.ShapeDtypeStruct((length, 3 * dw), LOW),
            ],
            in_specs=[anywhere] * 6 + [inside] * 4,
            out_specs=[anywhere] * 4,
            scratch_shapes=inside_like(hidden, wo, g_all, slope, qkv, lse)
            + token_scratch(local_len, width)
            + [pltpu.VMEM((ctx_n, fsdp_n, unit, cols), LOW)]
            + shard_scratch(1, ctx_n, unit, cols)
            + [pltpu.VMEM((ctx_n, unit, cols), LOW)]
            + [pltpu.VMEM((length, c), LOW) for c in (fw, dw, 3 * dw)]
            + [pltpu.VMEM((dw // pair, length, pair), LOW)]
            + inside_like(qkv)
            + [pltpu.VMEM((length, pair), F32)] * 3
            + [pltpu.SemaphoreType.DMA((SEMAPHORES,))],
            compiler_params=pltpu.CompilerParams(
                collective_id=1, has_side_effects=True, vmem_limit_bytes=VMEM_BYTES
            ),
            name="scatter_out",
        )(hidden, wo, g_all, slope, qkv, lse, *tables)

    def scatter_in(gm, wi, gup, wu, x_all, stats, normed, g_own):
        length, width = normed.shape
        local_len = length // ctx_n
        unit, up_rows = width // n, wu.shape[0] // fsdp_n
        return pl.pallas_call(
            functools.partial(scatter_in_kernel, shape),
            out_shape=[
                jax.ShapeDtypeStruct((local_len, width), F32),
                jax.ShapeDtypeStruct((up_rows, width), LOW),
                jax.ShapeDtypeStruct((3, unit, width), LOW),
                jax.ShapeDtypeStruct((16, width), F32),
            ],
            in_specs=[anywhere] * 8,
            out_specs=[anywhere] * 4,
            scratch_shapes=inside_like(gm, wi, gup, wu, x_all, stats, normed, g_own)
            + token_scratch(local_len, width)
            + inside_like(wu)
            + shard_scratch(1, up_rows, width)
            + inside_like(wi)
            + shard_scratch(3, unit, width)
            + [pltpu.VMEM((3, unit, width), LOW)]
            + [pltpu.VMEM((count, 16, width), F32) for count in (5, y_n, x_n, core_n, z_n)]
            + [pltpu.SemaphoreType.DMA((SEMAPHORES,))],
            compiler_params=pltpu.CompilerParams(
                collective_id=2, has_side_effects=True, vmem_limit_bytes=VMEM_BYTES
            ),
            name="scatter_in",
        )(gm, wi, gup, wu, x_all, stats, normed, g_own)

    def body(
        hidden_in, positions, ln_gain, ln_bias, w_qkv, b_qkv, w_dense, b_dense,
        w_fc1, b_fc1, w_fc2, b_fc2, out_grad,
    ):
        local_len, width = hidden_in.shape[1:]
        hidden_units = w_fc2.shape[1]
        unit = w_dense.shape[0]
        up_rows = w_fc1.shape[0]
        fw, dw = hidden_units // ctx_n, width // ctx_n
        my_ctx = lax.axis_index("ctx")
        me = my_ctx * fsdp_n + lax.axis_index("fsdp")
        length = positions.shape[1]
        x_own, g_own = hidden_in[0], out_grad[0]

        rank = positions[0, ::RUN] // RUN
        starts, steps = turning_tables(length)
        ranks = jnp.arange(length // RUN, dtype=jnp.int32)
        chosen = (rank[:, None] == ranks[None, :])[None, :, :, None]
        stored_starts = jnp.sum(jnp.where(chosen, starts[:, None], 0.0), axis=2)
        places = positions, positions.reshape(length, 1)

        own_small = jnp.concatenate([ln_gain, ln_bias, b_dense, b_fc2, b_qkv, b_fc1])
        own_small = jnp.pad(own_small.reshape(-1, unit), ((0, 5), (0, width - unit)))
        x_all, g_all, wi, wu, wo, small, normed, hidden, slope, qkv, lse, stats = gather(
            x_own, g_own, w_qkv, w_fc1, w_fc2, w_dense, own_small, (*places, stored_starts, steps)
        )
        small = small.astype(F32)
        gain, bias_dense, bias_down = small[0], small[2], small[3]
        total, grad_o, grad_upward, grad_mixed = scatter_out(
            hidden, wo.reshape(width, fw + dw), g_all, slope, qkv, lse, (*places, starts, steps)
        )
        grad_normed, grad_up, grad_qkv, sums = scatter_in(
            grad_mixed, wi, grad_upward, wu, x_all, stats, normed, g_own
        )

        def standardize(values):
            wide = values.astype(F32)
            centered = wide - jnp.mean(wide, axis=-1, keepdims=True)
            spread = lax.rsqrt(jnp.mean(centered * centered, axis=-1, keepdims=True) + EPSILON)
            return centered * spread, spread

        hidden_out = (total + x_own.astype(F32) + bias_dense + bias_down).astype(LOW)
        xhat, spread = standardize(x_own)
        e = grad_normed * gain
        grad_in = (
            e - jnp.mean(e, axis=-1, keepdims=True)
            - xhat * jnp.mean(e * xhat, axis=-1, keepdims=True)
        ) * spread + g_own.astype(F32)
        grad_o = grad_o.transpose(1, 0, 2).astype(F32)
        sums = sums.reshape(-1)

        def own_slice(row, size):
            return lax.dynamic_slice_in_dim(sums, row * width + me * size, size)

        grad_b_out = own_slice(2, unit)
        return (
            hidden_out[None],
            grad_in[None],
            own_slice(0, unit),
            own_slice(1, unit),
            grad_qkv.reshape(3 * unit, width).astype(F32),
            own_slice(4, 3 * unit),
            grad_o[:, :, fw:].reshape(unit, width),
            grad_b_out,
            grad_up.astype(F32),
            own_slice(7, up_rows),
            grad_o[:, :, :fw].reshape(unit, hidden_units),
            grad_b_out,
        )

    tokens, rows, cells = P("fsdp", "ctx", None), P(BOTH, None), P(BOTH)
    return jax.shard_map(
        body,
        mesh=mesh,
        in_specs=(
            tokens, P("fsdp", None), cells, cells, rows, cells, rows, cells,
            rows, cells, rows, cells, tokens,
        ),
        out_specs=(
            tokens, tokens, cells, cells, rows, cells, rows, cells, rows, cells, rows, cells,
        ),
        check_vma=False,
    )
```

```python
import functools

import jax
import jax.numpy as jnp
import numpy as np
from jax import lax
from jax.experimental import pallas as pl
from jax.experimental.pallas import tpu as pltpu
from jax.sharding import PartitionSpec as P

HEAD_DIM = 64
ROT_DIM = 32
RUN = 64
EPSILON = 1e-05
SCORE_SCALE = 0.125
BOTH = ("ctx", "fsdp")
F32 = jnp.float32
LOW = jnp.bfloat16
MESH = pl.DeviceIdType.MESH
SEMAPHORES = 512
VMEM_BYTES = 60 * 1024 * 1024
SMALL_ROWS = (
    [(row, (1, 0)) for row in range(4)]
    + [(4, (3, j)) for j in range(3)]
    + [(7, (4, j)) for j in range(4)]
)


def dot_nt(a, b):
    return lax.dot_general(a, b, (((1,), (1,)), ((), ())), preferred_element_type=F32)


def dot_nn(a, b):
    return lax.dot_general(a, b, (((1,), (0,)), ((), ())), preferred_element_type=F32)


def dot_tn(a, b):
    return lax.dot_general(a, b, (((0,), (0,)), ((), ())), preferred_element_type=F32)


def turning_tables(length):
    half_rot = ROT_DIM // 2
    lane = np.arange(2 * HEAD_DIM) % HEAD_DIM
    freqs = np.where(lane < ROT_DIM, 10000.0 ** (-(lane % half_rot) / half_rot), 0.0)
    starts = np.arange(0, length, RUN)[:, None] * freqs[None, :]
    steps = np.arange(RUN)[:, None] * freqs[None, :]
    return (
        np.stack([np.cos(starts), np.sin(starts)]).astype(np.float32),
        np.stack([np.cos(steps), np.sin(steps)]).astype(np.float32),
    )


def run_turn(start_ref, step_ref, run):
    lane = lax.broadcasted_iota(jnp.int32, (RUN, 2 * HEAD_DIM), 1) % HEAD_DIM
    half_rot = ROT_DIM // 2
    cos_a, sin_a = start_ref[0, pl.ds(run, 1), :], start_ref[1, pl.ds(run, 1), :]
    cos_b, sin_b = step_ref[0], step_ref[1]
    cosine = cos_a * cos_b - sin_a * sin_b
    sine = sin_a * cos_b + cos_a * sin_b
    above = jnp.where(lane < half_rot, -sine, 0.0)
    below = jnp.where((lane >= half_rot) & (lane < ROT_DIM), sine, 0.0)
    return cosine, above, below


def turn(u, tables, way=1.0):
    cosine, above, below = tables
    half_rot = ROT_DIM // 2
    width = 2 * HEAD_DIM
    moved = pltpu.roll(u, width - half_rot, 1) * above + pltpu.roll(u, half_rot, 1) * below
    return u * cosine + way * moved


def masked_tile(scores, diagonal, start):
    last = jnp.where(diagonal, scores[:, start:], -1e30)
    return jnp.concatenate([scores[:, :start], last], axis=1) if start > 0 else last


def lower_triangle(tile):
    return lax.broadcasted_iota(jnp.int32, (tile, tile), 1) <= lax.broadcasted_iota(
        jnp.int32, (tile, tile), 0
    )


def head_lanes(tile, head):
    lanes = lax.broadcasted_iota(jnp.int32, (tile, 2 * HEAD_DIM), 1)
    return (lanes // HEAD_DIM) == head


def pick(mine, values):
    return jnp.where(mine, values, jnp.zeros_like(values))


def attend(q_s, k_s, v_s, ctx_s, lse_s):
    length = q_s.shape[0]
    tile = min(256, length)
    diagonal = lower_triangle(tile)
    for start in range(0, length, tile):
        rows, reach = slice(start, start + tile), start + tile
        context = jnp.zeros((tile, 2 * HEAD_DIM), F32)
        lse = jnp.zeros((tile, 2 * HEAD_DIM), F32)
        for head in range(2):
            mine = head_lanes(tile, head)
            scores = dot_nt(pick(mine, q_s[rows, :]), k_s[:reach, :])
            scores = masked_tile(scores, diagonal, start)
            peak = jnp.max(scores, axis=1, keepdims=True)
            exps = jnp.exp(scores - peak)
            total = jnp.sum(exps, axis=1, keepdims=True)
            probs_low = (exps * (1.0 / total)).astype(LOW)
            context = jnp.where(mine, dot_nn(probs_low, v_s[:reach, :]), context)
            lse = jnp.where(mine, peak + jnp.log(total), lse)
        ctx_s[rows, :] = context.astype(LOW)
        lse_s[rows, :] = lse


class Grid:
    def __init__(self, ctx_n, fsdp_n):
        self.ctx_n, self.fsdp_n = ctx_n, fsdp_n
        self.x_n = 1 << ((ctx_n.bit_length() - 1) // 2)
        self.z_n = ctx_n // self.x_n
        self.core_n = 2 if fsdp_n % 2 == 0 else 1
        self.y_n = fsdp_n // self.core_n
        self.undo = 1 if ctx_n % 3 == 1 else 2

    def locate(self):
        self.ctx, self.fsdp = lax.axis_index("ctx"), lax.axis_index("fsdp")
        self.z, self.x = self.ctx // self.x_n, self.ctx % self.x_n
        self.y, self.core = self.fsdp // self.core_n, self.fsdp % self.core_n
        return self

    def zx(self, dz, dx):
        return ((self.z + dz + self.z_n) % self.z_n) * self.x_n + (
            self.x + dx + self.x_n
        ) % self.x_n

    def yc(self, dy, dc):
        return ((self.y + dy + self.y_n) % self.y_n) * self.core_n + (
            self.core + dc + self.core_n
        ) % self.core_n

    def nearest(self, j):
        place = 0
        for z in range(self.z_n):
            order = sorted(range(self.z_n), key=lambda other: (abs(other - z), other))
            place = place + jnp.where(self.z == z, order[j], 0)
        return place

    def qkv_piece(self, ctx, fsdp, m):
        span = 3 * self.fsdp_n
        v = (3 * fsdp + m + span * self.ctx_n - ctx * self.fsdp_n) % span
        return ((v // self.fsdp_n) * self.undo) % 3, v % self.fsdp_n

    def qkv_owner(self, ctx, fsdp, m):
        kind, place = self.qkv_piece(ctx, fsdp, m)
        piece = self.ctx_n * self.fsdp_n * kind + ctx * self.fsdp_n + place
        return piece // 3 // self.fsdp_n

    def qkv_user(self, ctx, fsdp, m):
        piece = 3 * (ctx * self.fsdp_n + fsdp) + m
        return (piece % (self.ctx_n * self.fsdp_n)) // self.fsdp_n

    def greet(self):
        barrier = pltpu.get_barrier_semaphore()
        for k in range(1, self.ctx_n):
            pl.semaphore_signal(
                barrier, inc=1, device_id={"ctx": (self.ctx + k) % self.ctx_n}, device_id_type=MESH
            )
        for k in range(1, self.fsdp_n):
            pl.semaphore_signal(
                barrier,
                inc=1,
                device_id={"fsdp": (self.fsdp + k) % self.fsdp_n},
                device_id_type=MESH,
            )
        pl.semaphore_wait(barrier, self.ctx_n + self.fsdp_n - 2)


class Copies:
    def __init__(self, sems):
        self.sems, self.used, self.sent, self.perhaps = sems, 0, [], []

    def sem(self):
        self.used += 1
        return self.sems.at[self.used - 1]

    def send(self, src, dst, **where):
        send_sem, recv_sem = self.sem(), self.sem()
        copy = pltpu.make_async_remote_copy(
            src_ref=src,
            dst_ref=dst,
            send_sem=send_sem,
            recv_sem=recv_sem,
            device_id=where,
            device_id_type=MESH,
        )
        copy.start()
        self.sent.append(copy)
        return recv_sem

    def send_or_keep(self, src, dst, ctx, own_ctx):
        send_sem, recv_sem = self.sem(), self.sem()
        remote = pltpu.make_async_remote_copy(
            src_ref=src,
            dst_ref=dst,
            send_sem=send_sem,
            recv_sem=recv_sem,
            device_id={"ctx": ctx},
            device_id_type=MESH,
        )

        @pl.when(ctx != own_ctx)
        def _():
            remote.start()

        @pl.when(ctx == own_ctx)
        def _():
            pltpu.make_async_copy(src, dst, recv_sem).start()

        self.perhaps.append((ctx != own_ctx, remote))
        return recv_sem

    def prepare(self, src, dst, **where):
        send_sem, recv_sem = self.sem(), self.sem()
        remote = pltpu.make_async_remote_copy(
            src_ref=src,
            dst_ref=dst,
            send_sem=send_sem,
            recv_sem=recv_sem,
            device_id=where,
            device_id_type=MESH,
        )
        return remote, recv_sem

    def start_if(self, when, remote):
        @pl.when(when)
        def _():
            remote.start()

        self.perhaps.append((when, remote))

    def send_if(self, when, src, dst, **where):
        remote, recv_sem = self.prepare(src, dst, **where)
        self.start_if(when, remote)
        return recv_sem

    def local(self, src, dst):
        copy = pltpu.make_async_copy(src, dst, self.sem())
        copy.start()
        return copy

    def drain(self):
        for copy in self.sent:
            copy.wait_send()
        for sent, copy in self.perhaps:

            @pl.when(sent)
            def _(copy=copy):
                copy.wait_send()


def arrived(ref, sem):
    pltpu.make_async_copy(ref, ref, sem).wait()


class TokenGather:
    def __init__(self, grid, copies, own, buffer):
        self.grid, self.copies, self.buffer = grid, copies, buffer
        self.rows = own.shape[0]
        self.across = []
        self.kept = copies.local(own, self.slot(0, 0))
        self.along = {
            way: copies.send_if(self.ends(way), own, self.slot(0, 0), ctx=grid.zx(way, 0))
            for way in (1, -1)
        }
        for l in range(1, grid.x_n):
            sem = copies.send(own, self.slot(0, 0), ctx=grid.zx(0, l))
            self.across.append((0, 1, l, sem))

    def slot(self, k, l):
        start = pl.multiple_of(self.grid.zx(-k, -l) * self.rows, self.rows)
        return self.buffer.at[pl.ds(start, self.rows)]

    def ends(self, way):
        return self.grid.z < self.grid.z_n - 1 if way > 0 else self.grid.z > 0

    def has(self, k, way):
        z = self.grid.z
        return z >= k if way > 0 else z + k < self.grid.z_n

    def step(self, k):
        grid, copies, along = self.grid, self.copies, {}
        for way in (1, -1):
            slot, here = self.slot(k * way, 0), self.has(k, way)

            @pl.when(here)
            def _(slot=slot, way=way):
                arrived(slot, self.along[way])

            if k < grid.z_n - 1:
                along[way] = copies.send_if(
                    here & self.ends(way), slot, slot, ctx=grid.zx(way, 0)
                )
            for l in range(1, grid.x_n):
                sem = copies.send_if(here, slot, slot, ctx=grid.zx(0, l))
                self.across.append((k, way, l, sem))
        self.along = along

    def ready(self, k):
        if k == 0:
            self.kept.wait()
        for m, way, l, sem in self.across:
            if m == k:

                @pl.when(self.has(k, way))
                def _(way=way, l=l, sem=sem):
                    arrived(self.slot(k * way, l), sem)


class ShardGather:
    def __init__(self, grid, copies, own, view):
        self.grid, self.copies, self.view = grid, copies, view
        self.along_y = [
            copies.send(own, view(grid.fsdp), fsdp=grid.yc(k, 0)) for k in range(1, grid.y_n)
        ]
        self.across = []
        self.cross(own, 0)

    def cross(self, src, k):
        for c in range(1, self.grid.core_n):
            slot = self.view(self.grid.yc(-k, 0))
            self.across.append((k, c, self.copies.send(src, slot, fsdp=self.grid.yc(0, c))))

    def forward(self):
        for k in range(1, self.grid.y_n):
            slot = self.view(self.grid.yc(-k, 0))
            arrived(slot, self.along_y[k - 1])
            self.cross(slot, k)

    def finish(self):
        for k, c, sem in self.across:
            arrived(self.view(self.grid.yc(-k, -c)), sem)


def gather_kernel(
    shape, x_in, g_in, wq_in, wu_in, wf_in, wd_in,
    small_in, row_in, start_in, step_in,
    x_out, g_out, wi_out, wu_out, wo_out, small_out, normed_out, hidden_out, slope_out,
    qkv_out, lse_out, stats_out,
    x_s, g_s, wi_s, wu_s, wo_s, normed_s, hidden_s, slope_s, qkv_s, lse_s, stats_s,
    mixed_s, ctx_s, small_f, qkv_bias_s, up_bias_s, small_s, small_x, small_core, small_y, small_z, sems,
):
    grid = Grid(*shape).locate()
    copies = Copies(sems)
    local_len, width = x_in.shape
    unit, up_rows = wd_in.shape[0], wu_in.shape[0]
    fw, dw = wf_in.shape[1] // grid.ctx_n, wd_in.shape[1] // grid.ctx_n
    n = grid.ctx_n * grid.fsdp_n
    me = grid.ctx * grid.fsdp_n + grid.fsdp
    peers = [(k, l) for k in range(grid.z_n) for l in range(grid.x_n) if k or l]
    pairs = dw // (2 * HEAD_DIM)
    puts = []

    row_index = lax.broadcasted_iota(jnp.int32, (16, width), 0)
    placed = jnp.zeros((16, width), F32)
    pieces_in = small_in[...].astype(F32)
    for row, (base, each) in enumerate(SMALL_ROWS):
        piece = each[0] * me + each[1]
        value = jnp.broadcast_to(pieces_in[row : row + 1, :], (16, width))
        value = pltpu.roll(value, (piece % n) * unit, 1)
        placed = placed + jnp.where(row_index == piece // n + base, value, 0.0)
    small_s[0] = placed.astype(LOW)
    grid.greet()

    def small_sum(step, buffer, stage):
        for i, sem in enumerate(stage):
            arrived(buffer.at[i], sem)
        accumulate(
            small_s.at[step + 1], small_s.at[step], *[buffer.at[i] for i in range(len(stage))]
        )

    stage = [
        copies.send(small_s.at[0], small_y.at[k - 1], fsdp=grid.yc(k, 0))
        for k in range(1, grid.y_n)
    ]

    def up_slot(f):
        return wu_s.at[pl.ds(pl.multiple_of(f * up_rows, up_rows), up_rows)]

    up_kept = copies.local(wu_in, up_slot(grid.fsdp))
    up = ShardGather(grid, copies, wu_in, up_slot)
    qkv_sems = []

    def piece_slot(ctx, fsdp, m):
        kind, place = grid.qkv_piece(ctx, fsdp, m)
        return wi_s.at[pl.ds(pl.multiple_of((kind * grid.fsdp_n + place) * unit, unit), unit)]

    for m in range(3):
        user = grid.qkv_user(grid.ctx, grid.fsdp, m)
        qkv_sems.append(
            copies.send_or_keep(
                wq_in.at[pl.ds(m * unit, unit)],
                piece_slot(user, grid.fsdp, m),
                user,
                grid.ctx,
            )
        )
    small_sum(0, small_y, stage)
    stage = [
        copies.send(small_s.at[1], small_x.at[l - 1], ctx=grid.zx(0, l))
        for l in range(1, grid.x_n)
    ]
    tokens_x = TokenGather(grid, copies, x_in, x_s)
    small_sum(1, small_x, stage)
    stage = [
        copies.send(small_s.at[2], small_core.at[c - 1], fsdp=grid.yc(0, c))
        for c in range(1, grid.core_n)
    ]
    small_sum(2, small_core, stage)
    stage = [
        copies.send(small_s.at[3], small_z.at[k - 1], ctx=grid.zx(k, 0))
        for k in range(1, grid.z_n)
    ]

    def column_block(ref, index, block):
        return ref.at[:, pl.ds(pl.multiple_of(index * block, 128), block)]

    mine = wo_s.at[grid.ctx, grid.fsdp]
    own_out = [
        copies.local(column_block(wf_in, grid.ctx, fw), mine.at[:, pl.ds(0, fw)]),
        copies.local(column_block(wd_in, grid.ctx, dw), mine.at[:, pl.ds(fw, dw)]),
    ]
    out_sems = {}

    def send_out(k):
        for l in range(grid.x_n):
            if k or l:
                target = grid.zx(k, l)
                out_sems[k, l] = (
                    copies.send(
                        column_block(wf_in, target, fw), mine.at[:, pl.ds(0, fw)], ctx=target
                    ),
                    copies.send(
                        column_block(wd_in, target, dw), mine.at[:, pl.ds(fw, dw)], ctx=target
                    ),
                )

    shards = []

    def spread_out(k):
        first = ((grid.z - k + grid.z_n) % grid.z_n) * grid.x_n
        for l in range(grid.x_n):
            slot = wo_s.at[grid.zx(-k, -l), grid.fsdp]
            if k or l:
                arrived(slot.at[:, pl.ds(0, fw)], out_sems[k, l][0])
                arrived(slot.at[:, pl.ds(fw, dw)], out_sems[k, l][1])
            else:
                own_out[0].wait()
                own_out[1].wait()

        def out_view(f):
            return wo_s.at[pl.ds(first, grid.x_n), f]

        shards.append(ShardGather(grid, copies, out_view(grid.fsdp), out_view))

    group = grid.x_n * local_len

    def group_rows(k):
        return pl.multiple_of(grid.nearest(k) * group, group)

    def normalize(k):
        first = group_rows(k)
        gain, shift = small_f[0:1, :], small_f[1:2, :]

        @pl.loop(0, group // 16)
        def _(i):
            rows = pl.ds(pl.multiple_of(first + i * 16, 16), 16)
            wide = x_s[rows, :].astype(F32)
            mean = jnp.mean(wide, axis=-1, keepdims=True)
            centered = wide - mean
            spread = lax.rsqrt(jnp.mean(centered * centered, axis=-1, keepdims=True) + EPSILON)
            normed_s[rows, :] = (centered * spread * gain + shift).astype(LOW)
            lane = lax.broadcasted_iota(jnp.int32, (16, 2 * HEAD_DIM), 1)
            stats_s[rows, :] = jnp.where(lane < HEAD_DIM, mean, spread)

    tile_rows = min(256, group)

    def project_up(k):
        first = group_rows(k)
        block = min(256, fw)

        @pl.loop(0, (group // tile_rows) * (fw // block))
        def _(i):
            part, col = i // (fw // block), (i % (fw // block)) * block
            rows = pl.ds(pl.multiple_of(first + part * tile_rows, tile_rows), tile_rows)
            cols = pl.ds(pl.multiple_of(col, block), block)
            bias = up_bias_s[i % (fw // block), 0:1, :]
            upward = dot_nt(normed_s[rows, :], wu_s[cols, :]) + bias
            square = upward * upward
            bend = jnp.tanh(0.7978845608028654 * (upward + 0.044715 * square * upward))
            half = 0.5 * (1.0 + bend)
            hidden_s[rows, cols] = (upward * half).astype(LOW)
            inner_slope = 0.7978845608028654 * (1.0 + 3.0 * 0.044715 * square)
            slope = half + 0.5 * upward * (1.0 - bend * bend) * inner_slope
            slope_s[rows, cols] = slope.astype(LOW)

    def project_qkv(k):
        first = group_rows(k)

        @pl.loop(0, group // tile_rows)
        def _(i):
            start = pl.multiple_of(first + i * tile_rows, tile_rows)
            rows = pl.ds(start, tile_rows)
            for kind in range(3):
                result = dot_nt(normed_s[rows, :], wi_s[kind * dw : (kind + 1) * dw, :])
                result = result + qkv_bias_s[kind, 0:1, :]
                if kind == 2:
                    mixed_s[rows, kind * dw : (kind + 1) * dw] = result.astype(LOW)
                    continue
                for run in range(tile_rows // RUN):
                    tables = run_turn(start_in, step_in, start // RUN + run)
                    run_at = pl.ds(pl.multiple_of(start + run * RUN, RUN), RUN)
                    for p in range(pairs):
                        lanes = slice(p * 2 * HEAD_DIM, (p + 1) * 2 * HEAD_DIM)
                        turned = turn(result[run * RUN : (run + 1) * RUN, lanes], tables)
                        low = turned.astype(LOW)
                        if kind == 0:
                            low = (low * SCORE_SCALE).astype(LOW)
                        at = kind * dw + p * 2 * HEAD_DIM
                        mixed_s[run_at, at : at + 2 * HEAD_DIM] = low

    last = grid.z_n - 1
    tokens_x.step(1)
    send_out(0)
    for k in range(2, last):
        tokens_x.step(k)
        send_out(k - 1)
    tokens_g = TokenGather(grid, copies, g_in, g_s)
    send_out(last - 1)
    tokens_x.step(last)
    send_out(last)
    pieces = []
    for m in range(3):
        arrived(piece_slot(grid.ctx, grid.fsdp, m), qkv_sems[m])
        pieces.append(
            ShardGather(
                grid,
                copies,
                piece_slot(grid.ctx, grid.fsdp, m),
                lambda f, m=m: piece_slot(grid.ctx, f, m),
            )
        )
    up.forward()
    small_sum(3, small_z, stage)
    puts.append(copies.local(small_s.at[4], small_out))
    small_f[...] = small_s[4].astype(F32)
    for kind in range(3):
        at = pl.ds(pl.multiple_of(grid.ctx * dw, 128), dw)
        row = small_f[4 + kind : 5 + kind, at]
        qkv_bias_s[kind] = jnp.broadcast_to(row, qkv_bias_s.shape[1:])
    block = up_bias_s.shape[2]
    for i in range(fw // block):
        offset = grid.ctx * fw
        at = pl.ds(pl.multiple_of(offset % width + i * block, 128), block)
        row = jnp.zeros((1, block), F32)
        for j in range(4):
            row = row + jnp.where(offset // width == j, small_f[7 + j : 8 + j, at], 0.0)
        up_bias_s[i] = jnp.broadcast_to(row, up_bias_s.shape[1:])
    tokens_x.ready(0)
    normalize(0)
    up_kept.wait()
    up.finish()
    puts.append(copies.local(wu_s, wu_out))
    project_up(0)
    for gather in pieces:
        gather.forward()
    tokens_x.ready(1)
    normalize(1)
    project_up(1)
    for gather in pieces:
        gather.finish()
    puts.append(copies.local(wi_s, wi_out))
    project_qkv(0)
    project_qkv(1)
    tokens_g.step(1)
    spread_out(0)
    for k in range(2, grid.z_n):
        tokens_x.ready(k)
        normalize(k)
        project_up(k)
        project_qkv(k)
        spread_out(k - 1)
        shards[k - 2].forward()
        if k == last:
            spread_out(last)
        if k > 2:
            tokens_g.step(k - 1)
    puts.append(copies.local(x_s, x_out))
    puts.append(copies.local(normed_s, normed_out))
    puts.append(copies.local(slope_s, slope_out))
    puts.append(copies.local(stats_s, stats_out))
    length = x_s.shape[0]
    pair = 2 * HEAD_DIM

    tall = min(256, length)

    @pl.loop(0, length // tall)
    def _(i):
        start = pl.multiple_of(i * tall, tall)
        result = dot_nn(to_sorted(row_in, start, tall), mixed_s[...]).astype(LOW)
        for kind in range(3):
            for p in range(pairs):
                at = kind * dw + p * pair
                qkv_s[kind, p, pl.ds(start, tall), :] = result[:, at : at + pair]

    @pl.loop(0, pairs)
    def _(p):
        attend(qkv_s.at[0, p], qkv_s.at[1, p], qkv_s.at[2, p], ctx_s.at[p], lse_s.at[p])

    @pl.loop(0, length // tall)
    def _(i):
        start = pl.multiple_of(i * tall, tall)
        back = to_stored(row_in, start, tall)
        for p in range(pairs):
            at = slice(fw + p * pair, fw + (p + 1) * pair)
            hidden_s[pl.ds(start, tall), at] = dot_tn(back, ctx_s[p]).astype(LOW)

    tokens_g.step(last)
    for gather in shards[last - 1 :]:
        gather.forward()
    puts.append(copies.local(hidden_s, hidden_out))
    puts.append(copies.local(qkv_s, qkv_out))
    puts.append(copies.local(lse_s, lse_out))
    for gather in shards:
        gather.finish()
    puts.append(copies.local(wo_s, wo_out))
    for k in range(grid.z_n):
        tokens_g.ready(k)
    puts.append(copies.local(g_s, g_out))
    for put in puts:
        put.wait()
    copies.drain()


def accumulate(dst, *sources):
    if len(dst.shape) == 3:

        @pl.loop(0, dst.shape[0])
        def _(i):
            accumulate(dst.at[i], *[source.at[i] for source in sources])

        return
    rows, step = dst.shape[0], 16

    @pl.loop(0, rows // step)
    def _(i):
        part = pl.ds(pl.multiple_of(i * step, step), step)
        total = sources[0][part, :].astype(F32)
        for source in sources[1:]:
            total = total + source[part, :].astype(F32)
        dst[part, :] = total.astype(dst.dtype)


class TokenScatter:
    def __init__(self, grid, copies, parts, from_x, from_z, total, half):
        self.grid, self.copies, self.parts = grid, copies, parts
        self.rows = total.shape[0]
        self.cols = pl.ds(half * (total.shape[1] // 2), total.shape[1] // 2)
        self.from_x, self.from_z = from_x.at[:, :, :, self.cols], from_z.at[:, :, self.cols]
        self.total = total.at[:, self.cols]
        self.along_x, self.sems = {}, {}
        self.order = [t for i in range(grid.z_n // 2) for t in (grid.z_n - 1 - i, i)]

    def block(self, t, dx):
        x = (self.grid.x + dx) % self.grid.x_n
        rows = pl.ds(pl.multiple_of(x * self.rows, self.rows), self.rows)
        return self.parts.at[t, rows, self.cols]

    def launch(self, t):
        for l in range(1, self.grid.x_n):
            self.along_x[t, l] = self.copies.send(
                self.block(t, l), self.from_x.at[t, l - 1], ctx=self.grid.zx(0, l)
            )

    def collect(self, t):
        terms = [self.block(t, 0)]
        for l in range(1, self.grid.x_n):
            arrived(self.from_x.at[t, l - 1], self.along_x[t, l])
            terms.append(self.from_x.at[t, l - 1])
        accumulate(terms[0], *terms)

    def climb(self, t):
        grid, own, slot = self.grid, self.block(t, 0), self.from_z.at[t]
        remote, sem = self.copies.prepare(own, slot, ctx=grid.zx(1, 0))

        @pl.when((grid.z < t) & (grid.z > 0))
        def _():
            arrived(slot, sem)
            accumulate(own, own, slot)

        self.copies.start_if(grid.z < t, remote)
        self.sems[t, 1] = sem

    def descend(self, t):
        grid, own, slot = self.grid, self.block(t, 0), self.from_z.at[t]
        there = self.from_z.at[jnp.where(grid.z - 1 == t, grid.z_n, t)]
        remote, sem = self.copies.prepare(own, there, ctx=grid.zx(-1, 0))

        @pl.when((grid.z > t) & (grid.z < grid.z_n - 1))
        def _():
            arrived(slot, sem)
            accumulate(own, own, slot)

        self.copies.start_if(grid.z > t, remote)
        self.sems[t, -1] = sem

    def step(self, i):
        last = self.grid.z_n - 1
        self.collect(self.order[i])
        known = self.order[: i + 1]
        for t in range(last, 0, -1):
            ready = [u for u in known if u >= t]
            if len(ready) == last - t + 1 and (t, 1) not in self.sems and t in known:
                self.climb(t)
        for t in range(last):
            ready = [u for u in known if u <= t]
            if len(ready) == t + 1 and (t, -1) not in self.sems and t in known:
                self.descend(t)

    def finish(self):
        grid = self.grid
        for t in range(grid.z_n):

            @pl.when(grid.z == t)
            def _(t=t):
                terms = [self.block(t, 0)]
                if t > 0:
                    arrived(self.from_z.at[t], self.sems[t, 1])
                    terms.append(self.from_z.at[t])
                if t < grid.z_n - 1:
                    arrived(self.from_z.at[grid.z_n], self.sems[t, -1])
                    terms.append(self.from_z.at[grid.z_n])
                accumulate(self.total, *terms)


class ShardScatter:
    def __init__(self, grid, copies, views, from_core, from_y):
        self.grid, self.copies, self.views = grid, copies, views
        self.from_core, self.from_y = from_core, from_y
        self.rounds = list(range(1, grid.y_n)) + [0]
        self.across = {
            k: [
                copies.send(part, from_core.at[k, i], fsdp=grid.yc(0, 1))
                for i, part in enumerate(views(grid.yc(k, 1)))
            ]
            for k in self.rounds
        }
        self.along_y = {}

    def step(self, k):
        for i, part in enumerate(self.views(self.grid.yc(k, 0))):
            arrived(self.from_core.at[k, i], self.across[k][i])
            accumulate(part, part, self.from_core.at[k, i])
            if k > 0:
                self.along_y[k, i] = self.copies.send(
                    part, self.from_y.at[k - 1, i], fsdp=self.grid.yc(k, 0)
                )

    def finish(self):
        for i, part in enumerate(self.views(self.grid.fsdp)):
            for k in range(1, self.grid.y_n):
                arrived(self.from_y.at[k - 1, i], self.along_y[k, i])
            accumulate(
                part, part, *[self.from_y.at[k - 1, i] for k in range(1, self.grid.y_n)]
            )


def to_sorted(row_ref, start, tile):
    length = row_ref.shape[1]
    place = lax.broadcasted_iota(jnp.int32, (tile, length), 0) + start
    return jnp.where(place == row_ref[0:1, :], 1.0, 0.0).astype(LOW)


def to_stored(row_ref, start, tile):
    length = row_ref.shape[1]
    place = lax.broadcasted_iota(jnp.int32, (length, tile), 0)
    return jnp.where(place == row_ref[0:1, pl.ds(start, tile)], 1.0, 0.0).astype(LOW)


def run_rows(i):
    return pl.ds(pl.multiple_of(i * RUN, RUN), RUN)


def attend_back(q_s, k_s, v_s, lse_s, g_s, dq_s, dk_s, dv_s):
    length = q_s.shape[0]
    dk_s[...] = jnp.zeros_like(dk_s)
    dv_s[...] = jnp.zeros_like(dv_s)
    tile = min(256, length)
    diagonal = lower_triangle(tile)
    for start in range(0, length, tile):
        rows, reach = slice(start, start + tile), start + tile
        grad_q = jnp.zeros((tile, 2 * HEAD_DIM), F32)
        for head in range(2):
            mine = head_lanes(tile, head)
            q_own, g_own = pick(mine, q_s[rows, :]), pick(mine, g_s[rows, :])
            lse = lse_s[rows, head * HEAD_DIM : head * HEAD_DIM + 1]
            scores = masked_tile(dot_nt(q_own, k_s[:reach, :]), diagonal, start)
            probs = jnp.exp(scores - lse)
            grad_probs = dot_nt(g_own, v_s[:reach, :])
            inner = jnp.sum(probs * grad_probs, axis=1, keepdims=True)
            grad_scores = (probs * (grad_probs - inner)).astype(LOW)
            grad_q = jnp.where(mine, dot_nn(grad_scores, k_s[:reach, :]), grad_q)
            dk_s[:reach, :] += dot_tn(grad_scores, q_own)
            dv_s[:reach, :] += dot_tn(probs.astype(LOW), g_own)
        dq_s[rows, :] = grad_q * SCORE_SCALE


def scatter_out_kernel(
    shape, hidden_in, wo_in, g_in, slope_in, qkv_in, lse_in,
    row_in, start_in, step_in,
    total_out, go_out, gup_out, gm_out,
    hidden_s, wo_s, g_s, slope_s, qkv_s, lse_s, po_s, po_x, po_z, po_sum,
    go_s, go_core, go_y, gup_s, gctx_s, gm_s, sorted_s, turned_s, dq_s, dk_s, dv_s, sems,
):
    grid = Grid(*shape).locate()
    copies = Copies(sems)
    length, fw = gup_s.shape
    dw = gctx_s.shape[1]
    width, cols = wo_s.shape
    pair = 2 * HEAD_DIM
    loads = [
        copies.local(src, dst)
        for src, dst in (
            (hidden_in, hidden_s), (wo_in, wo_s), (g_in, g_s),
            (slope_in, slope_s), (qkv_in, qkv_s), (lse_in, lse_s),
        )
    ]
    grid.greet()
    loads[0].wait()
    loads[1].wait()
    group = po_s.shape[1]
    tile = min(256, group)
    early, late = (
        TokenScatter(grid, copies, po_s, po_x, po_z, po_sum, half) for half in range(2)
    )
    unit = go_s.shape[2]
    block = grid.fsdp_n * unit
    part_n = grid.ctx_n // 2

    def make_out(t):
        @pl.loop(0, (group // tile) * (width // 256))
        def _(i):
            part = pl.multiple_of((i // (width // 256)) * tile, tile)
            at = pl.ds(pl.multiple_of((i % (width // 256)) * 256, 256), 256)
            rows = pl.ds(pl.multiple_of(t * group + part, tile), tile)
            result = dot_nt(hidden_s[rows, :], wo_s[at, :])
            po_s[t, pl.ds(part, tile), at] = result.astype(LOW)

        early.launch(t)

    def make_grad_out(part):
        @pl.loop(part * part_n, (part + 1) * part_n)
        def _(c):
            at = pl.ds(pl.multiple_of(c * block, block), block)
            result = dot_tn(g_s[:, at], hidden_s[...]).astype(LOW)
            go_s[c] = result.reshape(grid.fsdp_n, unit, cols)

        span = pl.ds(part * part_n, part_n)
        return ShardScatter(
            grid,
            copies,
            lambda f: [go_s.at[span, f]],
            go_core.at[:, :, span],
            go_y.at[:, :, span],
        )

    make_out(early.order[0])
    make_out(early.order[1])
    loads[2].wait()
    shards = [make_grad_out(0)]
    for t in early.order[2:]:
        make_out(t)
    for t in late.order:
        late.launch(t)
    early.step(0)
    shards.append(make_grad_out(1))
    early.step(1)
    for k in shards[0].rounds:
        shards[0].step(k)
    early.step(2)
    for k in shards[1].rounds:
        shards[1].step(k)
    loads[3].wait()
    tall = min(256, length)

    @pl.loop(0, (length // tall) * (fw // 256))
    def _(i):
        rows = pl.ds(pl.multiple_of((i // (fw // 256)) * tall, tall), tall)
        at = pl.ds(pl.multiple_of((i % (fw // 256)) * 256, 256), 256)
        grad = dot_nn(g_s[rows, :], wo_s[:, at])
        gup_s[rows, at] = (grad * slope_s[rows, at].astype(F32)).astype(LOW)

    puts = [copies.local(gup_s, gup_out)]
    early.step(3)

    @pl.loop(0, length // tall)
    def _(i):
        rows = pl.ds(pl.multiple_of(i * tall, tall), tall)
        gctx_s[rows, :] = dot_nn(g_s[rows, :], wo_s[:, pl.ds(fw, dw)]).astype(LOW)

    late.step(0)
    loads[4].wait()
    loads[5].wait()
    pairs = dw // pair

    @pl.loop(0, length // tall)
    def _(i):
        start = pl.multiple_of(i * tall, tall)
        result = dot_nn(to_sorted(row_in, start, tall), gctx_s[...]).astype(LOW)
        for p in range(pairs):
            sorted_s[p, pl.ds(start, tall), :] = result[:, p * pair : (p + 1) * pair]

    def attend_pairs(first, last):
        @pl.loop(first, last)
        def _(p):
            attend_back(
                qkv_s.at[0, p], qkv_s.at[1, p], qkv_s.at[2, p], lse_s.at[p],
                sorted_s.at[p], dq_s, dk_s, dv_s,
            )

            @pl.loop(0, length // RUN)
            def _(i):
                tables, rows = run_turn(start_in, step_in, i), run_rows(i)
                turned_s[0, p, rows, :] = turn(dq_s[rows, :], tables, -1.0).astype(LOW)
                turned_s[1, p, rows, :] = turn(dk_s[rows, :], tables, -1.0).astype(LOW)
                turned_s[2, p, rows, :] = dv_s[rows, :].astype(LOW)

    late.step(1)
    attend_pairs(0, (pairs + 1) // 2)
    late.step(2)
    late.step(3)
    if pairs > 1:
        attend_pairs((pairs + 1) // 2, pairs)
    for shard in shards:
        shard.finish()
    puts.append(copies.local(go_s.at[:, grid.fsdp], go_out))

    @pl.loop(0, length // tall)
    def _(i):
        start = pl.multiple_of(i * tall, tall)
        back = to_stored(row_in, start, tall)
        for kind in range(3):
            for p in range(pairs):
                at = kind * dw + p * pair
                result = dot_tn(back, turned_s[kind, p])
                gm_s[pl.ds(start, tall), at : at + pair] = result.astype(LOW)

    puts.append(copies.local(gm_s, gm_out))
    early.finish()
    late.finish()
    puts.append(copies.local(po_sum, total_out))
    for put in puts:
        put.wait()
    copies.drain()


def scatter_in_kernel(
    shape, gm_in, wi_in, gup_in, wu_in, x_in, stats_in, normed_in, g_own_in, go_in,
    total_out, gu_out, gi_out, go_out, small_out,
    gm_s, wi_s, gup_s, wu_s, x_s, stats_s, normed_s, g_own_s, pn_s, pn_x, pn_z, pn_sum,
    gu_s, gu_core, gu_y, gi_s, gi_core, gi_y, gi_got, go_got,
    small_s, small_y, small_x, small_core, small_z, sems,
):
    grid = Grid(*shape).locate()
    copies = Copies(sems)
    length, fw = gup_s.shape
    width = wi_s.shape[1]
    dw = gm_s.shape[1] // 3
    unit = gi_got.shape[1]
    up_rows = fw // grid.fsdp_n
    loads = [
        copies.local(src, dst)
        for src, dst in (
            (gm_in, gm_s), (wi_in, wi_s), (gup_in, gup_s), (wu_in, wu_s),
            (x_in, x_s), (stats_in, stats_s), (normed_in, normed_s), (g_own_in, g_own_s),
        )
    ]
    grid.greet()
    peers = [(k, l) for k in range(grid.z_n) for l in range(grid.x_n) if k or l]
    own_o = copies.local(go_in.at[grid.ctx], go_got.at[grid.ctx])
    out_sems = [
        copies.send(go_in.at[grid.zx(k, l)], go_got.at[grid.ctx], ctx=grid.zx(k, l))
        for k, l in peers
    ]
    small_s[0] = jnp.zeros_like(small_s[0])
    for load in loads[:6]:
        load.wait()
    group = pn_s.shape[1]
    tile = min(256, group)
    early, late = (
        TokenScatter(grid, copies, pn_s, pn_x, pn_z, pn_sum, half) for half in range(2)
    )

    def make_normed(t):
        @pl.loop(0, (group // tile) * (width // 256))
        def _(i):
            part = pl.multiple_of((i // (width // 256)) * tile, tile)
            at = pl.ds(pl.multiple_of((i % (width // 256)) * 256, 256), 256)
            rows = pl.ds(pl.multiple_of(t * group + part, tile), tile)
            grad = dot_nn(gm_s[rows, :], wi_s[:, at]) + dot_nn(gup_s[rows, :], wu_s[:, at])
            pn_s[t, pl.ds(part, tile), at] = grad.astype(LOW)
            mean, spread = stats_s[rows, 0:1], stats_s[rows, HEAD_DIM : HEAD_DIM + 1]
            xhat = (x_s[rows, at].astype(F32) - mean) * spread
            small_s[0, 0:1, at] += jnp.sum(grad * xhat, axis=0, keepdims=True)
            small_s[0, 1:2, at] += jnp.sum(grad, axis=0, keepdims=True)

        early.launch(t)

    make_normed(early.order[0])
    make_normed(early.order[1])
    for load in loads[6:]:
        load.wait()

    @pl.loop(0, 3)
    def _(i):
        at = pl.ds(pl.multiple_of(i * dw, dw), dw)
        gi_s[at, :] = dot_tn(gm_s[:, at], normed_s[...]).astype(LOW)

    def piece_slot(f, m):
        kind, place = grid.qkv_piece(grid.ctx, f, m)
        return gi_s.at[pl.ds(pl.multiple_of((kind * grid.fsdp_n + place) * unit, unit), unit)]

    shards_i = ShardScatter(
        grid, copies, lambda f: [piece_slot(f, m) for m in range(3)], gi_core, gi_y
    )
    for t in early.order[2:]:
        make_normed(t)
    for t in late.order:
        late.launch(t)

    small_s[0, 2:3, :] = jnp.sum(g_own_s[...].astype(F32), axis=0, keepdims=True)
    for kind in range(3):
        at = pl.ds(pl.multiple_of(grid.ctx * dw, 128), dw)
        terms = gm_s[:, kind * dw : (kind + 1) * dw].astype(F32)
        small_s[0, 4 + kind : 5 + kind, at] = jnp.sum(terms, axis=0, keepdims=True)
    offset = grid.ctx * fw
    at = pl.ds(pl.multiple_of(offset % width, 128), fw)
    terms = jnp.sum(gup_s[...].astype(F32), axis=0, keepdims=True)
    for row in range(4):
        small_s[0, 7 + row : 8 + row, at] = jnp.where(offset // width == row, terms, 0.0)

    def small_sum(step, buffer, stage):
        for i, sem in enumerate(stage):
            arrived(buffer.at[i], sem)
        accumulate(
            small_s.at[step + 1], small_s.at[step], *[buffer.at[i] for i in range(len(stage))]
        )

    stage = [
        copies.send(small_s.at[0], small_y.at[k - 1], fsdp=grid.yc(k, 0))
        for k in range(1, grid.y_n)
    ]

    def up_slot(f):
        return gu_s.at[pl.ds(pl.multiple_of(f * up_rows, up_rows), up_rows)]

    def make_grad_up(part):
        half = fw // 256 // 2

        @pl.loop(part * half, (part + 1) * half)
        def _(i):
            at = pl.ds(pl.multiple_of(i * 256, 256), 256)
            gu_s[at, :] = dot_tn(gup_s[:, at], normed_s[...]).astype(LOW)

    early.step(0)
    for k in shards_i.rounds:
        shards_i.step(k)
    make_grad_up(0)
    early.step(1)
    make_grad_up(1)
    shards_u = ShardScatter(grid, copies, lambda f: [up_slot(f)], gu_core, gu_y)
    early.step(2)
    small_sum(0, small_y, stage)
    stage = [
        copies.send(small_s.at[1], small_core.at[c - 1], fsdp=grid.yc(0, c))
        for c in range(1, grid.core_n)
    ]
    for k in shards_u.rounds:
        shards_u.step(k)
    early.step(3)
    late.step(0)
    late.step(1)
    small_sum(1, small_core, stage)
    stage = [
        copies.send(small_s.at[2], small_x.at[l - 1], ctx=grid.zx(0, l))
        for l in range(1, grid.x_n)
    ]
    late.step(2)
    shards_i.finish()
    qkv_sems = []
    for m in range(3):
        owner = grid.qkv_owner(grid.ctx, grid.fsdp, m)
        qkv_sems.append(
            copies.send_or_keep(piece_slot(grid.fsdp, m), gi_got.at[m], owner, grid.ctx)
        )
    late.step(3)
    small_sum(2, small_x, stage)
    stage = [
        copies.send(small_s.at[3], small_z.at[k - 1], ctx=grid.zx(k, 0))
        for k in range(1, grid.z_n)
    ]
    shards_u.finish()
    puts = [copies.local(up_slot(grid.fsdp), gu_out)]
    early.finish()
    late.finish()
    puts.append(copies.local(pn_sum, total_out))
    own_o.wait()
    for (k, l), sem in zip(peers, out_sems):
        arrived(go_got.at[grid.zx(-k, -l)], sem)
    puts.append(copies.local(go_got, go_out))
    for m in range(3):
        arrived(gi_got.at[m], qkv_sems[m])
    puts.append(copies.local(gi_got, gi_out))
    small_sum(3, small_z, stage)
    puts.append(copies.local(small_s.at[4], small_out))
    for put in puts:
        put.wait()
    copies.drain()


def solution(mesh):
    shape = mesh.shape["ctx"], mesh.shape["fsdp"]
    ctx_n, fsdp_n = shape
    n = ctx_n * fsdp_n
    plan = Grid(*shape)
    x_n, z_n, core_n, y_n = plan.x_n, plan.z_n, plan.core_n, plan.y_n

    def gather(x_own, g_own, w_qkv, w_fc1, w_fc2, w_dense, small, tables):
        local_len, width = x_own.shape
        unit, hidden_units = w_fc2.shape
        length = ctx_n * local_len
        fw, dw = hidden_units // ctx_n, width // ctx_n
        pair = 2 * HEAD_DIM
        small_rows = jax.ShapeDtypeStruct((16, width), LOW)
        kept = [
            jax.ShapeDtypeStruct((length, width), LOW),
            jax.ShapeDtypeStruct((length, width), LOW),
            jax.ShapeDtypeStruct((3 * fsdp_n * unit, width), LOW),
            jax.ShapeDtypeStruct((fw, width), LOW),
            jax.ShapeDtypeStruct((ctx_n, fsdp_n, unit, fw + dw), LOW),
        ]
        made = [
            jax.ShapeDtypeStruct((length, width), LOW),
            jax.ShapeDtypeStruct((length, fw + dw), LOW),
            jax.ShapeDtypeStruct((length, fw), LOW),
            jax.ShapeDtypeStruct((3, dw // pair, length, pair), LOW),
            jax.ShapeDtypeStruct((dw // pair, length, pair), F32),
            jax.ShapeDtypeStruct((length, pair), F32),
        ]
        return pl.pallas_call(
            functools.partial(gather_kernel, shape),
            out_shape=kept + [small_rows] + made,
            in_specs=[anywhere] * 6 + [inside] * 4,
            out_specs=[anywhere] * 12,
            scratch_shapes=[pltpu.VMEM(s.shape, s.dtype) for s in kept + made]
            + [pltpu.VMEM((length, 3 * dw), LOW), pltpu.VMEM((dw // pair, length, pair), LOW)]
            + [pltpu.VMEM((16, width), F32), pltpu.VMEM((3, 8, dw), F32)]
            + [pltpu.VMEM((max(fw // 256, 1), 8, min(fw, 256)), F32)]
            + [pltpu.VMEM((count, 16, width), LOW) for count in (5, x_n, core_n, y_n, z_n)]
            + [pltpu.SemaphoreType.DMA((SEMAPHORES,))],
            compiler_params=pltpu.CompilerParams(
                collective_id=0, has_side_effects=True, vmem_limit_bytes=VMEM_BYTES
            ),
            name="gather",
        )(x_own, g_own, w_qkv, w_fc1, w_fc2, w_dense, small, *tables)

    def token_scratch(local_len, width):
        return [
            pltpu.VMEM((z_n, x_n * local_len, width), LOW),
            pltpu.VMEM((z_n, max(x_n - 1, 1), local_len, width), LOW),
            pltpu.VMEM((z_n + 1, local_len, width), LOW),
            pltpu.VMEM((local_len, width), F32),
        ]

    def shard_scratch(parts, *block):
        return [
            pltpu.VMEM((y_n, parts) + block, LOW),
            pltpu.VMEM((max(y_n - 1, 1), parts) + block, LOW),
        ]

    def inside_like(*arrays):
        return [pltpu.VMEM(a.shape, a.dtype) for a in arrays]

    anywhere = pl.BlockSpec(memory_space=pl.ANY)
    inside = pl.BlockSpec(memory_space=pltpu.VMEM)

    def scatter_out(hidden, wo, g_all, slope, qkv, lse, tables):
        length, cols = hidden.shape
        local_len, width = length // ctx_n, g_all.shape[1]
        unit = width // n
        fw = slope.shape[1]
        dw, pair = cols - fw, 2 * HEAD_DIM
        return pl.pallas_call(
            functools.partial(scatter_out_kernel, shape),
            out_shape=[
                jax.ShapeDtypeStruct((local_len, width), F32),
                jax.ShapeDtypeStruct((ctx_n, unit, cols), LOW),
                jax.ShapeDtypeStruct((length, fw), LOW),
                jax.ShapeDtypeStruct((length, 3 * dw), LOW),
            ],
            in_specs=[anywhere] * 6 + [inside] * 3,
            out_specs=[anywhere] * 4,
            scratch_shapes=inside_like(hidden, wo, g_all, slope, qkv, lse)
            + token_scratch(local_len, width)
            + [pltpu.VMEM((ctx_n, fsdp_n, unit, cols), LOW)]
            + shard_scratch(1, ctx_n, unit, cols)
            + [pltpu.VMEM((length, c), LOW) for c in (fw, dw, 3 * dw)]
            + [pltpu.VMEM((dw // pair, length, pair), LOW)]
            + inside_like(qkv)
            + [pltpu.VMEM((length, pair), F32)] * 3
            + [pltpu.SemaphoreType.DMA((SEMAPHORES,))],
            compiler_params=pltpu.CompilerParams(
                collective_id=1, has_side_effects=True, vmem_limit_bytes=VMEM_BYTES
            ),
            name="scatter_out",
        )(hidden, wo, g_all, slope, qkv, lse, *tables)

    def scatter_in(gm, wi, gup, wu, x_all, stats, normed, g_own, go):
        length, width = normed.shape
        local_len = length // ctx_n
        unit, up_rows = width // n, wu.shape[0] // fsdp_n
        return pl.pallas_call(
            functools.partial(scatter_in_kernel, shape),
            out_shape=[
                jax.ShapeDtypeStruct((local_len, width), F32),
                jax.ShapeDtypeStruct((up_rows, width), LOW),
                jax.ShapeDtypeStruct((3, unit, width), LOW),
                jax.ShapeDtypeStruct(go.shape, LOW),
                jax.ShapeDtypeStruct((16, width), F32),
            ],
            in_specs=[anywhere] * 9,
            out_specs=[anywhere] * 5,
            scratch_shapes=inside_like(gm, wi, gup, wu, x_all, stats, normed, g_own)
            + token_scratch(local_len, width)
            + inside_like(wu)
            + shard_scratch(1, up_rows, width)
            + inside_like(wi)
            + shard_scratch(3, unit, width)
            + [pltpu.VMEM((3, unit, width), LOW)]
            + inside_like(go)
            + [pltpu.VMEM((count, 16, width), F32) for count in (5, y_n, x_n, core_n, z_n)]
            + [pltpu.SemaphoreType.DMA((SEMAPHORES,))],
            compiler_params=pltpu.CompilerParams(
                collective_id=2, has_side_effects=True, vmem_limit_bytes=VMEM_BYTES
            ),
            name="scatter_in",
        )(gm, wi, gup, wu, x_all, stats, normed, g_own, go)

    def body(
        hidden_in, positions, ln_gain, ln_bias, w_qkv, b_qkv, w_dense, b_dense,
        w_fc1, b_fc1, w_fc2, b_fc2, out_grad,
    ):
        local_len, width = hidden_in.shape[1:]
        hidden_units = w_fc2.shape[1]
        unit = w_dense.shape[0]
        up_rows = w_fc1.shape[0]
        fw, dw = hidden_units // ctx_n, width // ctx_n
        my_ctx = lax.axis_index("ctx")
        me = my_ctx * fsdp_n + lax.axis_index("fsdp")
        length = positions.shape[1]
        x_own, g_own = hidden_in[0], out_grad[0]

        rank = positions[0, ::RUN] // RUN
        starts, steps = turning_tables(length)
        ranks = jnp.arange(length // RUN, dtype=jnp.int32)
        chosen = (rank[:, None] == ranks[None, :])[None, :, :, None]
        stored_starts = jnp.sum(jnp.where(chosen, starts[:, None], 0.0), axis=2)

        own_small = jnp.concatenate([ln_gain, ln_bias, b_dense, b_fc2, b_qkv, b_fc1])
        own_small = jnp.pad(own_small.reshape(-1, unit), ((0, 5), (0, width - unit)))
        x_all, g_all, wi, wu, wo, small, normed, hidden, slope, qkv, lse, stats = gather(
            x_own, g_own, w_qkv, w_fc1, w_fc2, w_dense, own_small, (positions, stored_starts, steps)
        )
        small = small.astype(F32)
        gain, bias_dense, bias_down = small[0], small[2], small[3]
        total, grad_o, grad_upward, grad_mixed = scatter_out(
            hidden, wo.reshape(width, fw + dw), g_all, slope, qkv, lse, (positions, starts, steps)
        )
        grad_normed, grad_up, grad_qkv, grad_o, sums = scatter_in(
            grad_mixed, wi, grad_upward, wu, x_all, stats, normed, g_own, grad_o
        )

        def standardize(values):
            wide = values.astype(F32)
            centered = wide - jnp.mean(wide, axis=-1, keepdims=True)
            spread = lax.rsqrt(jnp.mean(centered * centered, axis=-1, keepdims=True) + EPSILON)
            return centered * spread, spread

        hidden_out = (total + x_own.astype(F32) + bias_dense + bias_down).astype(LOW)
        xhat, spread = standardize(x_own)
        e = grad_normed * gain
        grad_in = (
            e - jnp.mean(e, axis=-1, keepdims=True)
            - xhat * jnp.mean(e * xhat, axis=-1, keepdims=True)
        ) * spread + g_own.astype(F32)
        grad_o = grad_o.transpose(1, 0, 2).astype(F32)
        sums = sums.reshape(-1)

        def own_slice(row, size):
            return lax.dynamic_slice_in_dim(sums, row * width + me * size, size)

        grad_b_out = own_slice(2, unit)
        return (
            hidden_out[None],
            grad_in[None],
            own_slice(0, unit),
            own_slice(1, unit),
            grad_qkv.reshape(3 * unit, width).astype(F32),
            own_slice(4, 3 * unit),
            grad_o[:, :, fw:].reshape(unit, width),
            grad_b_out,
            grad_up.astype(F32),
            own_slice(7, up_rows),
            grad_o[:, :, :fw].reshape(unit, hidden_units),
            grad_b_out,
        )

    tokens, rows, cells = P("fsdp", "ctx", None), P(BOTH, None), P(BOTH)
    return jax.shard_map(
        body,
        mesh=mesh,
        in_specs=(
            tokens, P("fsdp", None), cells, cells, rows, cells, rows, cells,
            rows, cells, rows, cells, tokens,
        ),
        out_specs=(
            tokens, tokens, cells, cells, rows, cells, rows, cells, rows, cells, rows, cells,
        ),
        check_vma=False,
    )
```

```python
import functools

import jax
import jax.numpy as jnp
import numpy as np
from jax import lax
from jax.experimental import pallas as pl
from jax.experimental.pallas import tpu as pltpu
from jax.sharding import PartitionSpec as P

HEAD_DIM = 64
ROT_DIM = 32
RUN = 64
EPSILON = 1e-05
SCORE_SCALE = 0.125
BOTH = ("ctx", "fsdp")
F32 = jnp.float32
LOW = jnp.bfloat16
MESH = pl.DeviceIdType.MESH
SEMAPHORES = 512
VMEM_BYTES = 60 * 1024 * 1024
SMALL_ROWS = (
    [(row, (1, 0)) for row in range(4)]
    + [(4, (3, j)) for j in range(3)]
    + [(7, (4, j)) for j in range(4)]
)


def dot_nt(a, b):
    return lax.dot_general(a, b, (((1,), (1,)), ((), ())), preferred_element_type=F32)


def dot_nn(a, b):
    return lax.dot_general(a, b, (((1,), (0,)), ((), ())), preferred_element_type=F32)


def dot_tn(a, b):
    return lax.dot_general(a, b, (((0,), (0,)), ((), ())), preferred_element_type=F32)


def turning_tables(length):
    half_rot = ROT_DIM // 2
    lane = np.arange(2 * HEAD_DIM) % HEAD_DIM
    freqs = np.where(lane < ROT_DIM, 10000.0 ** (-(lane % half_rot) / half_rot), 0.0)
    starts = np.arange(0, length, RUN)[:, None] * freqs[None, :]
    steps = np.arange(RUN)[:, None] * freqs[None, :]
    return (
        np.stack([np.cos(starts), np.sin(starts)]).astype(np.float32),
        np.stack([np.cos(steps), np.sin(steps)]).astype(np.float32),
    )


def run_turn(start_ref, step_ref, run):
    lane = lax.broadcasted_iota(jnp.int32, (RUN, 2 * HEAD_DIM), 1) % HEAD_DIM
    half_rot = ROT_DIM // 2
    cos_a, sin_a = start_ref[0, pl.ds(run, 1), :], start_ref[1, pl.ds(run, 1), :]
    cos_b, sin_b = step_ref[0], step_ref[1]
    cosine = cos_a * cos_b - sin_a * sin_b
    sine = sin_a * cos_b + cos_a * sin_b
    above = jnp.where(lane < half_rot, -sine, 0.0)
    below = jnp.where((lane >= half_rot) & (lane < ROT_DIM), sine, 0.0)
    return cosine, above, below


def turn(u, tables, way=1.0):
    cosine, above, below = tables
    half_rot = ROT_DIM // 2
    width = 2 * HEAD_DIM
    moved = pltpu.roll(u, width - half_rot, 1) * above + pltpu.roll(u, half_rot, 1) * below
    return u * cosine + way * moved


def masked_tile(scores, diagonal, start):
    last = jnp.where(diagonal, scores[:, start:], -1e30)
    return jnp.concatenate([scores[:, :start], last], axis=1) if start > 0 else last


def lower_triangle(tile):
    return lax.broadcasted_iota(jnp.int32, (tile, tile), 1) <= lax.broadcasted_iota(
        jnp.int32, (tile, tile), 0
    )


def head_lanes(tile, head):
    lanes = lax.broadcasted_iota(jnp.int32, (tile, 2 * HEAD_DIM), 1)
    return (lanes // HEAD_DIM) == head


def pick(mine, values):
    return jnp.where(mine, values, jnp.zeros_like(values))


def attend(q_s, k_s, v_s, ctx_s, lse_s):
    length = q_s.shape[0]
    tile = min(256, length)
    diagonal = lower_triangle(tile)
    for start in range(0, length, tile):
        rows, reach = slice(start, start + tile), start + tile

        @pl.loop(0, 2)
        def _(head, rows=rows, reach=reach, start=start):
            mine = head_lanes(tile, head)
            scores = dot_nt(pick(mine, q_s[rows, :]), k_s[:reach, :])
            scores = masked_tile(scores, diagonal, start)
            peak = jnp.max(scores, axis=1, keepdims=True)
            exps = jnp.exp(scores - peak)
            total = jnp.sum(exps, axis=1, keepdims=True)
            probs_low = (exps * (1.0 / total)).astype(LOW)
            context = dot_nn(probs_low, v_s[:reach, :]).astype(LOW)
            ctx_s[rows, :] = jnp.where(mine, context, ctx_s[rows, :])
            lse_s[rows, :] = jnp.where(mine, peak + jnp.log(total), lse_s[rows, :])


class Grid:
    def __init__(self, ctx_n, fsdp_n):
        self.ctx_n, self.fsdp_n = ctx_n, fsdp_n
        self.x_n = 1 << ((ctx_n.bit_length() - 1) // 2)
        self.z_n = ctx_n // self.x_n
        self.core_n = 2 if fsdp_n % 2 == 0 else 1
        self.y_n = fsdp_n // self.core_n
        self.undo = 1 if ctx_n % 3 == 1 else 2

    def locate(self):
        self.ctx, self.fsdp = lax.axis_index("ctx"), lax.axis_index("fsdp")
        self.z, self.x = self.ctx // self.x_n, self.ctx % self.x_n
        self.y, self.core = self.fsdp // self.core_n, self.fsdp % self.core_n
        return self

    def zx(self, dz, dx):
        return ((self.z + dz + self.z_n) % self.z_n) * self.x_n + (
            self.x + dx + self.x_n
        ) % self.x_n

    def yc(self, dy, dc):
        return ((self.y + dy + self.y_n) % self.y_n) * self.core_n + (
            self.core + dc + self.core_n
        ) % self.core_n

    def nearest(self, j):
        place = 0
        for z in range(self.z_n):
            order = sorted(range(self.z_n), key=lambda other: (abs(other - z), other))
            place = place + jnp.where(self.z == z, order[j], 0)
        return place

    def qkv_piece(self, ctx, fsdp, m):
        span = 3 * self.fsdp_n
        v = (3 * fsdp + m + span * self.ctx_n - ctx * self.fsdp_n) % span
        return ((v // self.fsdp_n) * self.undo) % 3, v % self.fsdp_n

    def qkv_owner(self, ctx, fsdp, m):
        kind, place = self.qkv_piece(ctx, fsdp, m)
        piece = self.ctx_n * self.fsdp_n * kind + ctx * self.fsdp_n + place
        return piece // 3 // self.fsdp_n

    def qkv_user(self, ctx, fsdp, m):
        piece = 3 * (ctx * self.fsdp_n + fsdp) + m
        return (piece % (self.ctx_n * self.fsdp_n)) // self.fsdp_n

    def greet(self):
        barrier = pltpu.get_barrier_semaphore()
        for k in range(1, self.ctx_n):
            pl.semaphore_signal(
                barrier, inc=1, device_id={"ctx": (self.ctx + k) % self.ctx_n}, device_id_type=MESH
            )
        for k in range(1, self.fsdp_n):
            pl.semaphore_signal(
                barrier,
                inc=1,
                device_id={"fsdp": (self.fsdp + k) % self.fsdp_n},
                device_id_type=MESH,
            )
        pl.semaphore_wait(barrier, self.ctx_n + self.fsdp_n - 2)


class Copies:
    def __init__(self, sems):
        self.sems, self.used, self.sent, self.perhaps = sems, 0, [], []

    def sem(self):
        self.used += 1
        return self.sems.at[self.used - 1]

    def send(self, src, dst, **where):
        send_sem, recv_sem = self.sem(), self.sem()
        copy = pltpu.make_async_remote_copy(
            src_ref=src,
            dst_ref=dst,
            send_sem=send_sem,
            recv_sem=recv_sem,
            device_id=where,
            device_id_type=MESH,
        )
        copy.start()
        self.sent.append(copy)
        return recv_sem

    def send_or_keep(self, src, dst, ctx, own_ctx):
        send_sem, recv_sem = self.sem(), self.sem()
        remote = pltpu.make_async_remote_copy(
            src_ref=src,
            dst_ref=dst,
            send_sem=send_sem,
            recv_sem=recv_sem,
            device_id={"ctx": ctx},
            device_id_type=MESH,
        )

        @pl.when(ctx != own_ctx)
        def _():
            remote.start()

        @pl.when(ctx == own_ctx)
        def _():
            pltpu.make_async_copy(src, dst, recv_sem).start()

        self.perhaps.append((ctx != own_ctx, remote))
        return recv_sem

    def prepare(self, src, dst, **where):
        send_sem, recv_sem = self.sem(), self.sem()
        remote = pltpu.make_async_remote_copy(
            src_ref=src,
            dst_ref=dst,
            send_sem=send_sem,
            recv_sem=recv_sem,
            device_id=where,
            device_id_type=MESH,
        )
        return remote, recv_sem

    def start_if(self, when, remote):
        @pl.when(when)
        def _():
            remote.start()

        self.perhaps.append((when, remote))

    def send_if(self, when, src, dst, **where):
        remote, recv_sem = self.prepare(src, dst, **where)
        self.start_if(when, remote)
        return recv_sem

    def local(self, src, dst):
        copy = pltpu.make_async_copy(src, dst, self.sem())
        copy.start()
        return copy

    def drain(self):
        for copy in self.sent:
            copy.wait_send()
        for sent, copy in self.perhaps:

            @pl.when(sent)
            def _(copy=copy):
                copy.wait_send()


def arrived(ref, sem):
    pltpu.make_async_copy(ref, ref, sem).wait()


class TokenGather:
    def __init__(self, grid, copies, own, buffer):
        self.grid, self.copies, self.buffer = grid, copies, buffer
        self.rows = own.shape[0]
        self.across = []
        self.kept = copies.local(own, self.slot(0, 0))
        self.along = {
            way: copies.send_if(self.ends(way), own, self.slot(0, 0), ctx=grid.zx(way, 0))
            for way in (1, -1)
        }
        for l in range(1, grid.x_n):
            sem = copies.send(own, self.slot(0, 0), ctx=grid.zx(0, l))
            self.across.append((0, 1, l, sem))

    def slot(self, k, l):
        start = pl.multiple_of(self.grid.zx(-k, -l) * self.rows, self.rows)
        return self.buffer.at[pl.ds(start, self.rows)]

    def ends(self, way):
        return self.grid.z < self.grid.z_n - 1 if way > 0 else self.grid.z > 0

    def has(self, k, way):
        z = self.grid.z
        return z >= k if way > 0 else z + k < self.grid.z_n

    def step(self, k):
        grid, copies, along = self.grid, self.copies, {}
        for way in (1, -1):
            slot, here = self.slot(k * way, 0), self.has(k, way)

            @pl.when(here)
            def _(slot=slot, way=way):
                arrived(slot, self.along[way])

            if k < grid.z_n - 1:
                along[way] = copies.send_if(
                    here & self.ends(way), slot, slot, ctx=grid.zx(way, 0)
                )
            for l in range(1, grid.x_n):
                sem = copies.send_if(here, slot, slot, ctx=grid.zx(0, l))
                self.across.append((k, way, l, sem))
        self.along = along

    def ready(self, k):
        if k == 0:
            self.kept.wait()
        for m, way, l, sem in self.across:
            if m == k:

                @pl.when(self.has(k, way))
                def _(way=way, l=l, sem=sem):
                    arrived(self.slot(k * way, l), sem)


class ShardGather:
    def __init__(self, grid, copies, own, view):
        self.grid, self.copies, self.view = grid, copies, view
        self.along_y = [
            copies.send(own, view(grid.fsdp), fsdp=grid.yc(k, 0)) for k in range(1, grid.y_n)
        ]
        self.across = []
        self.cross(own, 0)

    def cross(self, src, k):
        for c in range(1, self.grid.core_n):
            slot = self.view(self.grid.yc(-k, 0))
            self.across.append((k, c, self.copies.send(src, slot, fsdp=self.grid.yc(0, c))))

    def forward(self):
        for k in range(1, self.grid.y_n):
            slot = self.view(self.grid.yc(-k, 0))
            arrived(slot, self.along_y[k - 1])
            self.cross(slot, k)

    def finish(self):
        for k, c, sem in self.across:
            arrived(self.view(self.grid.yc(-k, -c)), sem)


def gather_kernel(
    shape, x_in, g_in, wq_in, wu_in, wf_in, wd_in,
    gain_in, shift_in, bd_in, bf_in, bq_in, bu_in, row_in, start_in, step_in,
    x_out, g_out, wi_out, wu_out, wo_out, small_out, normed_out, hidden_out, slope_out,
    qkv_out, lse_out, stats_out,
    x_s, g_s, wi_s, wu_s, wo_s, normed_s, hidden_s, slope_s, qkv_s, lse_s, stats_s,
    mixed_s, ctx_s, small_f, qkv_bias_s, up_bias_s, small_s, small_x, small_core, small_y, small_z, sems,
):
    grid = Grid(*shape).locate()
    copies = Copies(sems)
    local_len, width = x_in.shape
    unit, up_rows = wd_in.shape[0], wu_in.shape[0]
    fw, dw = wf_in.shape[1] // grid.ctx_n, wd_in.shape[1] // grid.ctx_n
    n = grid.ctx_n * grid.fsdp_n
    me = grid.ctx * grid.fsdp_n + grid.fsdp
    peers = [(k, l) for k in range(grid.z_n) for l in range(grid.x_n) if k or l]
    pairs = dw // (2 * HEAD_DIM)
    small_in = gain_in, shift_in, bd_in, bf_in, bq_in, bu_in
    puts = []

    row_index = lax.broadcasted_iota(jnp.int32, (16, width), 0)
    placed = jnp.zeros((16, width), F32)
    small_f[...] = jnp.zeros_like(small_f)
    row = 0
    for piece_in in small_in:
        small_f[row : row + piece_in.shape[0], 0:unit] = piece_in[...].astype(F32)
        row += piece_in.shape[0]
    pieces_in = small_f[...]
    for row, (base, each) in enumerate(SMALL_ROWS):
        piece = each[0] * me + each[1]
        value = jnp.broadcast_to(pieces_in[row : row + 1, :], (16, width))
        value = pltpu.roll(value, (piece % n) * unit, 1)
        placed = placed + jnp.where(row_index == piece // n + base, value, 0.0)
    small_s[0] = placed.astype(LOW)
    grid.greet()

    def small_sum(step, buffer, stage):
        for i, sem in enumerate(stage):
            arrived(buffer.at[i], sem)
        accumulate(
            small_s.at[step + 1], small_s.at[step], *[buffer.at[i] for i in range(len(stage))]
        )

    stage = [
        copies.send(small_s.at[0], small_y.at[k - 1], fsdp=grid.yc(k, 0))
        for k in range(1, grid.y_n)
    ]

    def up_slot(f):
        return wu_s.at[pl.ds(pl.multiple_of(f * up_rows, up_rows), up_rows)]

    up_kept = copies.local(wu_in, up_slot(grid.fsdp))
    up = ShardGather(grid, copies, wu_in, up_slot)
    qkv_sems = []

    def piece_slot(ctx, fsdp, m):
        kind, place = grid.qkv_piece(ctx, fsdp, m)
        return wi_s.at[pl.ds(pl.multiple_of((kind * grid.fsdp_n + place) * unit, unit), unit)]

    for m in range(3):
        user = grid.qkv_user(grid.ctx, grid.fsdp, m)
        qkv_sems.append(
            copies.send_or_keep(
                wq_in.at[pl.ds(m * unit, unit)],
                piece_slot(user, grid.fsdp, m),
                user,
                grid.ctx,
            )
        )
    small_sum(0, small_y, stage)
    stage = [
        copies.send(small_s.at[1], small_x.at[l - 1], ctx=grid.zx(0, l))
        for l in range(1, grid.x_n)
    ]
    tokens_x = TokenGather(grid, copies, x_in, x_s)
    small_sum(1, small_x, stage)
    stage = [
        copies.send(small_s.at[2], small_core.at[c - 1], fsdp=grid.yc(0, c))
        for c in range(1, grid.core_n)
    ]
    small_sum(2, small_core, stage)
    stage = [
        copies.send(small_s.at[3], small_z.at[k - 1], ctx=grid.zx(k, 0))
        for k in range(1, grid.z_n)
    ]

    def column_block(ref, index, block):
        return ref.at[:, pl.ds(pl.multiple_of(index * block, 128), block)]

    mine = wo_s.at[grid.ctx, grid.fsdp]
    own_out = [
        copies.local(column_block(wf_in, grid.ctx, fw), mine.at[:, pl.ds(0, fw)]),
        copies.local(column_block(wd_in, grid.ctx, dw), mine.at[:, pl.ds(fw, dw)]),
    ]
    out_sems = {}

    def send_out(k):
        for l in range(grid.x_n):
            if k or l:
                target = grid.zx(k, l)
                out_sems[k, l] = (
                    copies.send(
                        column_block(wf_in, target, fw), mine.at[:, pl.ds(0, fw)], ctx=target
                    ),
                    copies.send(
                        column_block(wd_in, target, dw), mine.at[:, pl.ds(fw, dw)], ctx=target
                    ),
                )

    shards = []

    def spread_out(k):
        first = ((grid.z - k + grid.z_n) % grid.z_n) * grid.x_n
        for l in range(grid.x_n):
            slot = wo_s.at[grid.zx(-k, -l), grid.fsdp]
            if k or l:
                arrived(slot.at[:, pl.ds(0, fw)], out_sems[k, l][0])
                arrived(slot.at[:, pl.ds(fw, dw)], out_sems[k, l][1])
            else:
                own_out[0].wait()
                own_out[1].wait()

        def out_view(f):
            return wo_s.at[pl.ds(first, grid.x_n), f]

        shards.append(ShardGather(grid, copies, out_view(grid.fsdp), out_view))

    group = grid.x_n * local_len

    def group_rows(first, i, parts):
        place = grid.nearest(first)
        for later in range(first + 1, min(first + 2, grid.z_n)):
            place = jnp.where(i // parts == later - first, grid.nearest(later), place)
        return pl.multiple_of(place * group + (i % parts) * tile_rows, tile_rows)

    def normalize(k):
        first = pl.multiple_of(grid.nearest(k) * group, group)
        gain, shift = small_f[0:1, :], small_f[1:2, :]

        @pl.loop(0, group // 16)
        def _(i):
            rows = pl.ds(pl.multiple_of(first + i * 16, 16), 16)
            wide = x_s[rows, :].astype(F32)
            mean = jnp.mean(wide, axis=-1, keepdims=True)
            centered = wide - mean
            spread = lax.rsqrt(jnp.mean(centered * centered, axis=-1, keepdims=True) + EPSILON)
            normed_s[rows, :] = (centered * spread * gain + shift).astype(LOW)
            lane = lax.broadcasted_iota(jnp.int32, (16, 2 * HEAD_DIM), 1)
            stats_s[rows, :] = jnp.where(lane < HEAD_DIM, mean, spread)

    tile_rows = min(256, group)

    tiles = group // tile_rows

    def project_up(k, groups=1):
        block = min(256, fw)

        @pl.loop(0, groups * tiles * (fw // block))
        def _(i):
            col = (i % (fw // block)) * block
            rows = pl.ds(group_rows(k, i // (fw // block), tiles), tile_rows)
            cols = pl.ds(pl.multiple_of(col, block), block)
            bias = up_bias_s[i % (fw // block), 0:1, :]
            upward = dot_nt(normed_s[rows, :], wu_s[cols, :]) + bias
            square = upward * upward
            bend = jnp.tanh(0.7978845608028654 * (upward + 0.044715 * square * upward))
            half = 0.5 * (1.0 + bend)
            hidden_s[rows, cols] = (upward * half).astype(LOW)
            inner_slope = 0.7978845608028654 * (1.0 + 3.0 * 0.044715 * square)
            slope = half + 0.5 * upward * (1.0 - bend * bend) * inner_slope
            slope_s[rows, cols] = slope.astype(LOW)

    def project_qkv(k, groups=1):
        @pl.loop(0, groups * tiles)
        def _(i):
            start = group_rows(k, i, tiles)
            rows = pl.ds(start, tile_rows)
            for kind in range(3):
                result = dot_nt(normed_s[rows, :], wi_s[kind * dw : (kind + 1) * dw, :])
                result = result + qkv_bias_s[kind, 0:1, :]
                if kind == 2:
                    mixed_s[rows, kind * dw : (kind + 1) * dw] = result.astype(LOW)
                    continue
                for run in range(tile_rows // RUN):
                    tables = run_turn(start_in, step_in, start // RUN + run)
                    run_at = pl.ds(pl.multiple_of(start + run * RUN, RUN), RUN)
                    for p in range(pairs):
                        lanes = slice(p * 2 * HEAD_DIM, (p + 1) * 2 * HEAD_DIM)
                        turned = turn(result[run * RUN : (run + 1) * RUN, lanes], tables)
                        low = turned.astype(LOW)
                        if kind == 0:
                            low = (low * SCORE_SCALE).astype(LOW)
                        at = kind * dw + p * 2 * HEAD_DIM
                        mixed_s[run_at, at : at + 2 * HEAD_DIM] = low

    last = grid.z_n - 1
    tokens_x.step(1)
    send_out(0)
    for k in range(2, last):
        tokens_x.step(k)
        send_out(k - 1)
    tokens_g = TokenGather(grid, copies, g_in, g_s)
    send_out(last - 1)
    tokens_x.step(last)
    send_out(last)
    pieces = []
    for m in range(3):
        arrived(piece_slot(grid.ctx, grid.fsdp, m), qkv_sems[m])
        pieces.append(
            ShardGather(
                grid,
                copies,
                piece_slot(grid.ctx, grid.fsdp, m),
                lambda f, m=m: piece_slot(grid.ctx, f, m),
            )
        )
    up.forward()
    small_sum(3, small_z, stage)
    puts.append(copies.local(small_s.at[4], small_out))
    small_f[...] = small_s[4].astype(F32)
    for kind in range(3):
        at = pl.ds(pl.multiple_of(grid.ctx * dw, 128), dw)
        row = small_f[4 + kind : 5 + kind, at]
        qkv_bias_s[kind] = jnp.broadcast_to(row, qkv_bias_s.shape[1:])
    block = up_bias_s.shape[2]
    for i in range(fw // block):
        offset = grid.ctx * fw
        at = pl.ds(pl.multiple_of(offset % width + i * block, 128), block)
        row = jnp.zeros((1, block), F32)
        for j in range(4):
            row = row + jnp.where(offset // width == j, small_f[7 + j : 8 + j, at], 0.0)
        up_bias_s[i] = jnp.broadcast_to(row, up_bias_s.shape[1:])
    tokens_x.ready(0)
    normalize(0)
    up_kept.wait()
    up.finish()
    puts.append(copies.local(wu_s, wu_out))
    for gather in pieces:
        gather.forward()
    tokens_x.ready(1)
    normalize(1)
    project_up(0, 2)
    for gather in pieces:
        gather.finish()
    puts.append(copies.local(wi_s, wi_out))
    project_qkv(0, 2)
    tokens_g.step(1)
    spread_out(0)
    for k in range(2, grid.z_n):
        tokens_x.ready(k)
        normalize(k)
        project_up(k)
        project_qkv(k)
        spread_out(k - 1)
        shards[k - 2].forward()
        if k == last:
            spread_out(last)
        if k > 2:
            tokens_g.step(k - 1)
    puts.append(copies.local(x_s, x_out))
    puts.append(copies.local(normed_s, normed_out))
    puts.append(copies.local(slope_s, slope_out))
    puts.append(copies.local(stats_s, stats_out))
    length = x_s.shape[0]
    pair = 2 * HEAD_DIM

    tall = min(256, length)

    @pl.loop(0, length // tall)
    def _(i):
        start = pl.multiple_of(i * tall, tall)
        result = dot_nn(to_sorted(row_in, start, tall), mixed_s[...]).astype(LOW)
        for kind in range(3):
            for p in range(pairs):
                at = kind * dw + p * pair
                qkv_s[kind, p, pl.ds(start, tall), :] = result[:, at : at + pair]

    @pl.loop(0, pairs)
    def _(p):
        attend(qkv_s.at[0, p], qkv_s.at[1, p], qkv_s.at[2, p], ctx_s.at[p], lse_s.at[p])

    @pl.loop(0, length // tall)
    def _(i):
        start = pl.multiple_of(i * tall, tall)
        back = to_stored(row_in, start, tall)
        for p in range(pairs):
            at = slice(fw + p * pair, fw + (p + 1) * pair)
            hidden_s[pl.ds(start, tall), at] = dot_tn(back, ctx_s[p]).astype(LOW)

    tokens_g.step(last)
    for gather in shards[last - 1 :]:
        gather.forward()
    puts.append(copies.local(hidden_s, hidden_out))
    puts.append(copies.local(qkv_s, qkv_out))
    puts.append(copies.local(lse_s, lse_out))
    for gather in shards:
        gather.finish()
    puts.append(copies.local(wo_s, wo_out))
    for k in range(grid.z_n):
        tokens_g.ready(k)
    puts.append(copies.local(g_s, g_out))
    for put in puts:
        put.wait()
    copies.drain()


def accumulate(dst, *sources):
    if len(dst.shape) == 3:

        @pl.loop(0, dst.shape[0])
        def _(i):
            accumulate(dst.at[i], *[source.at[i] for source in sources])

        return
    rows, step = dst.shape[0], 16

    @pl.loop(0, rows // step)
    def _(i):
        part = pl.ds(pl.multiple_of(i * step, step), step)
        total = sources[0][part, :].astype(F32)
        for source in sources[1:]:
            total = total + source[part, :].astype(F32)
        dst[part, :] = total.astype(dst.dtype)


class TokenScatter:
    def __init__(self, grid, copies, parts, from_x, from_z, total, half):
        self.grid, self.copies, self.parts = grid, copies, parts
        self.rows = total.shape[0]
        self.cols = pl.ds(half * (total.shape[1] // 2), total.shape[1] // 2)
        self.from_x, self.from_z = from_x.at[:, :, :, self.cols], from_z.at[:, :, self.cols]
        self.total = total.at[:, self.cols]
        self.along_x, self.sems, self.remotes = {}, {}, {}
        self.order = [t for i in range(grid.z_n // 2) for t in (grid.z_n - 1 - i, i)]

    def block(self, t, dx):
        x = (self.grid.x + dx) % self.grid.x_n
        rows = pl.ds(pl.multiple_of(x * self.rows, self.rows), self.rows)
        return self.parts.at[t, rows, self.cols]

    def launch(self, t):
        for l in range(1, self.grid.x_n):
            self.along_x[t, l] = self.copies.send(
                self.block(t, l), self.from_x.at[t, l - 1], ctx=self.grid.zx(0, l)
            )

    def collect(self, t):
        terms = [self.block(t, 0)]
        for l in range(1, self.grid.x_n):
            arrived(self.from_x.at[t, l - 1], self.along_x[t, l])
            terms.append(self.from_x.at[t, l - 1])
        accumulate(terms[0], *terms)

    def hop(self, t, way, first, z):
        grid, own, slot = self.grid, self.block(t, 0), self.from_z.at[t]
        if first:
            after = slot
            if way < 0:
                after = self.from_z.at[jnp.where(grid.z - 1 == t, grid.z_n, t)]
            remote, sem = self.copies.prepare(own, after, ctx=grid.zx(way, 0))
            self.remotes[t, way], self.sems[t, way] = remote, sem
            self.copies.perhaps.append((grid.z < t if way > 0 else grid.z > t, remote))

        @pl.when(grid.z == z)
        def _():
            if not first:
                arrived(slot, self.sems[t, way])
                accumulate(own, own, slot)
            self.remotes[t, way].start()

    def step(self, i):
        last = self.grid.z_n - 1
        if i <= last:
            self.collect(self.order[i])
        for j, t in enumerate(self.order):
            if 0 <= i - j < t:
                self.hop(t, 1, i == j, i - j)
            if 0 <= i - j < last - t:
                self.hop(t, -1, i == j, last - (i - j))

    def finish(self):
        grid = self.grid
        for t in range(grid.z_n):

            @pl.when(grid.z == t)
            def _(t=t):
                terms = [self.block(t, 0)]
                if t > 0:
                    arrived(self.from_z.at[t], self.sems[t, 1])
                    terms.append(self.from_z.at[t])
                if t < grid.z_n - 1:
                    arrived(self.from_z.at[grid.z_n], self.sems[t, -1])
                    terms.append(self.from_z.at[grid.z_n])
                accumulate(self.total, *terms)


class ShardScatter:
    def __init__(self, grid, copies, views, from_core, from_y):
        self.grid, self.copies, self.views = grid, copies, views
        self.from_core, self.from_y = from_core, from_y
        self.rounds = list(range(1, grid.y_n)) + [0]
        self.across = {
            k: [
                copies.send(part, from_core.at[k, i], fsdp=grid.yc(0, 1))
                for i, part in enumerate(views(grid.yc(k, 1)))
            ]
            for k in self.rounds
        }
        self.along_y = {}

    def step(self, k):
        for i, part in enumerate(self.views(self.grid.yc(k, 0))):
            arrived(self.from_core.at[k, i], self.across[k][i])
            accumulate(part, part, self.from_core.at[k, i])
            if k > 0:
                self.along_y[k, i] = self.copies.send(
                    part, self.from_y.at[k - 1, i], fsdp=self.grid.yc(k, 0)
                )

    def finish(self):
        for i, part in enumerate(self.views(self.grid.fsdp)):
            for k in range(1, self.grid.y_n):
                arrived(self.from_y.at[k - 1, i], self.along_y[k, i])
            accumulate(
                part, part, *[self.from_y.at[k - 1, i] for k in range(1, self.grid.y_n)]
            )


def to_sorted(row_ref, start, tile):
    length = row_ref.shape[1]
    place = lax.broadcasted_iota(jnp.int32, (tile, length), 0) + start
    return jnp.where(place == row_ref[0:1, :], 1.0, 0.0).astype(LOW)


def to_stored(row_ref, start, tile):
    length = row_ref.shape[1]
    place = lax.broadcasted_iota(jnp.int32, (length, tile), 0)
    return jnp.where(place == row_ref[0:1, pl.ds(start, tile)], 1.0, 0.0).astype(LOW)


def run_rows(i):
    return pl.ds(pl.multiple_of(i * RUN, RUN), RUN)


def attend_back(q_s, k_s, v_s, lse_s, g_s, dq_s, dk_s, dv_s):
    length = q_s.shape[0]
    dk_s[...] = jnp.zeros_like(dk_s)
    dv_s[...] = jnp.zeros_like(dv_s)
    tile = min(256, length)
    diagonal = lower_triangle(tile)
    for start in range(0, length, tile):
        rows, reach = slice(start, start + tile), start + tile

        @pl.loop(0, 2)
        def _(head, rows=rows, reach=reach, start=start):
            mine = head_lanes(tile, head)
            q_own, g_own = pick(mine, q_s[rows, :]), pick(mine, g_s[rows, :])
            lse = jnp.where(head == 0, lse_s[rows, 0:1], lse_s[rows, HEAD_DIM : HEAD_DIM + 1])
            scores = masked_tile(dot_nt(q_own, k_s[:reach, :]), diagonal, start)
            probs = jnp.exp(scores - lse)
            grad_probs = dot_nt(g_own, v_s[:reach, :])
            inner = jnp.sum(probs * grad_probs, axis=1, keepdims=True)
            grad_scores = (probs * (grad_probs - inner)).astype(LOW)
            grad_q = dot_nn(grad_scores, k_s[:reach, :]) * SCORE_SCALE
            dq_s[rows, :] = jnp.where(mine, grad_q, dq_s[rows, :])
            dk_s[:reach, :] += dot_tn(grad_scores, q_own)
            dv_s[:reach, :] += dot_tn(probs.astype(LOW), g_own)


def scatter_out_kernel(
    shape, hidden_in, wo_in, g_in, slope_in, qkv_in, lse_in,
    row_in, start_in, step_in,
    total_out, go_out, gup_out, gm_out,
    hidden_s, wo_s, g_s, slope_s, qkv_s, lse_s, po_s, po_x, po_z, po_sum,
    go_s, go_core, go_y, gup_s, gctx_s, gm_s, sorted_s, turned_s, dq_s, dk_s, dv_s, sems,
):
    grid = Grid(*shape).locate()
    copies = Copies(sems)
    length, fw = gup_s.shape
    dw = gctx_s.shape[1]
    width, cols = wo_s.shape
    pair = 2 * HEAD_DIM
    loads = [
        copies.local(src, dst)
        for src, dst in (
            (hidden_in, hidden_s), (wo_in, wo_s), (g_in, g_s),
            (slope_in, slope_s), (qkv_in, qkv_s), (lse_in, lse_s),
        )
    ]
    grid.greet()
    loads[0].wait()
    loads[1].wait()
    group = po_s.shape[1]
    tile = min(256, group)
    early, late = (
        TokenScatter(grid, copies, po_s, po_x, po_z, po_sum, half) for half in range(2)
    )
    unit = go_s.shape[2]
    block = grid.fsdp_n * unit
    part_n = grid.ctx_n // 2

    def make_out(first, count=1):
        @pl.loop(0, count * (group // tile) * (width // 256))
        def _(i):
            t, i = first - i // (group // tile * (width // 256)), i % (
                group // tile * (width // 256)
            )
            part = pl.multiple_of((i // (width // 256)) * tile, tile)
            at = pl.ds(pl.multiple_of((i % (width // 256)) * 256, 256), 256)
            rows = pl.ds(pl.multiple_of(t * group + part, tile), tile)
            result = dot_nt(hidden_s[rows, :], wo_s[at, :])
            po_s[t, pl.ds(part, tile), at] = result.astype(LOW)

        for t in range(first, first - count, -1):
            early.launch(t)

    def make_grad_out(part):
        @pl.loop(part * part_n, (part + 1) * part_n)
        def _(c):
            at = pl.ds(pl.multiple_of(c * block, block), block)
            result = dot_tn(g_s[:, at], hidden_s[...]).astype(LOW)
            go_s[c] = result.reshape(grid.fsdp_n, unit, cols)

        span = pl.ds(part * part_n, part_n)
        return ShardScatter(
            grid,
            copies,
            lambda f: [go_s.at[span, f]],
            go_core.at[:, :, span],
            go_y.at[:, :, span],
        )

    make_out(early.order[0])
    make_out(early.order[1])
    loads[2].wait()
    shards = [make_grad_out(0)]
    make_out(grid.z_n - 2, grid.z_n - 2)
    for t in late.order:
        late.launch(t)
    early.step(0)
    shards.append(make_grad_out(1))
    early.step(1)
    for k in shards[0].rounds:
        shards[0].step(k)
    early.step(2)
    for k in shards[1].rounds:
        shards[1].step(k)
    loads[3].wait()
    tall = min(256, length)

    @pl.loop(0, (length // tall) * (fw // 256))
    def _(i):
        rows = pl.ds(pl.multiple_of((i // (fw // 256)) * tall, tall), tall)
        at = pl.ds(pl.multiple_of((i % (fw // 256)) * 256, 256), 256)
        grad = dot_nn(g_s[rows, :], wo_s[:, at])
        gup_s[rows, at] = (grad * slope_s[rows, at].astype(F32)).astype(LOW)

    puts = [copies.local(gup_s, gup_out)]
    early.step(3)

    @pl.loop(0, length // tall)
    def _(i):
        rows = pl.ds(pl.multiple_of(i * tall, tall), tall)
        gctx_s[rows, :] = dot_nn(g_s[rows, :], wo_s[:, pl.ds(fw, dw)]).astype(LOW)

    early.step(grid.z_n)
    late.step(0)
    loads[4].wait()
    loads[5].wait()
    pairs = dw // pair

    @pl.loop(0, length // tall)
    def _(i):
        start = pl.multiple_of(i * tall, tall)
        result = dot_nn(to_sorted(row_in, start, tall), gctx_s[...]).astype(LOW)
        for p in range(pairs):
            sorted_s[p, pl.ds(start, tall), :] = result[:, p * pair : (p + 1) * pair]

    def attend_pairs(first, last):
        @pl.loop(first, last)
        def _(p):
            attend_back(
                qkv_s.at[0, p], qkv_s.at[1, p], qkv_s.at[2, p], lse_s.at[p],
                sorted_s.at[p], dq_s, dk_s, dv_s,
            )

            @pl.loop(0, length // RUN)
            def _(i):
                tables, rows = run_turn(start_in, step_in, i), run_rows(i)
                turned_s[0, p, rows, :] = turn(dq_s[rows, :], tables, -1.0).astype(LOW)
                turned_s[1, p, rows, :] = turn(dk_s[rows, :], tables, -1.0).astype(LOW)
                turned_s[2, p, rows, :] = dv_s[rows, :].astype(LOW)

    late.step(1)
    attend_pairs(0, (pairs + 1) // 2)
    late.step(2)
    late.step(3)
    for shard in shards:
        shard.finish()
    late.step(grid.z_n)
    if pairs > 1:
        attend_pairs((pairs + 1) // 2, pairs)
    puts.append(copies.local(go_s.at[:, grid.fsdp], go_out))

    @pl.loop(0, length // tall)
    def _(i):
        start = pl.multiple_of(i * tall, tall)
        back = to_stored(row_in, start, tall)
        for kind in range(3):
            for p in range(pairs):
                at = kind * dw + p * pair
                result = dot_tn(back, turned_s[kind, p])
                gm_s[pl.ds(start, tall), at : at + pair] = result.astype(LOW)

    puts.append(copies.local(gm_s, gm_out))
    early.finish()
    late.finish()
    puts.append(copies.local(po_sum, total_out))
    for put in puts:
        put.wait()
    copies.drain()


def scatter_in_kernel(
    shape, gm_in, wi_in, gup_in, wu_in, x_in, stats_in, normed_in, g_own_in, go_in,
    total_out, gu_out, gi_out, go_out, small_out,
    gm_s, wi_s, gup_s, wu_s, x_s, stats_s, normed_s, g_own_s, pn_s, pn_x, pn_z, pn_sum,
    gu_s, gu_core, gu_y, gi_s, gi_core, gi_y, gi_got, go_got,
    small_s, small_y, small_x, small_core, small_z, sems,
):
    grid = Grid(*shape).locate()
    copies = Copies(sems)
    length, fw = gup_s.shape
    width = wi_s.shape[1]
    dw = gm_s.shape[1] // 3
    unit = gi_got.shape[1]
    up_rows = fw // grid.fsdp_n
    loads = [
        copies.local(src, dst)
        for src, dst in (
            (gm_in, gm_s), (wi_in, wi_s), (gup_in, gup_s), (wu_in, wu_s),
            (x_in, x_s), (stats_in, stats_s), (normed_in, normed_s), (g_own_in, g_own_s),
        )
    ]
    grid.greet()
    peers = [(k, l) for k in range(grid.z_n) for l in range(grid.x_n) if k or l]
    own_o = copies.local(go_in.at[grid.ctx], go_got.at[grid.ctx])
    out_sems = [
        copies.send(go_in.at[grid.zx(k, l)], go_got.at[grid.ctx], ctx=grid.zx(k, l))
        for k, l in peers
    ]
    small_s[0] = jnp.zeros_like(small_s[0])
    for load in loads[:6]:
        load.wait()
    group = pn_s.shape[1]
    tile = min(256, group)
    early, late = (
        TokenScatter(grid, copies, pn_s, pn_x, pn_z, pn_sum, half) for half in range(2)
    )

    def make_normed(first, count=1):
        @pl.loop(0, count * (group // tile) * (width // 256))
        def _(i):
            t, i = first - i // (group // tile * (width // 256)), i % (
                group // tile * (width // 256)
            )
            part = pl.multiple_of((i // (width // 256)) * tile, tile)
            at = pl.ds(pl.multiple_of((i % (width // 256)) * 256, 256), 256)
            rows = pl.ds(pl.multiple_of(t * group + part, tile), tile)
            grad = dot_nn(gm_s[rows, :], wi_s[:, at]) + dot_nn(gup_s[rows, :], wu_s[:, at])
            pn_s[t, pl.ds(part, tile), at] = grad.astype(LOW)
            mean, spread = stats_s[rows, 0:1], stats_s[rows, HEAD_DIM : HEAD_DIM + 1]
            xhat = (x_s[rows, at].astype(F32) - mean) * spread
            small_s[0, 0:1, at] += jnp.sum(grad * xhat, axis=0, keepdims=True)
            small_s[0, 1:2, at] += jnp.sum(grad, axis=0, keepdims=True)

        for t in range(first, first - count, -1):
            early.launch(t)

    make_normed(early.order[0])
    make_normed(early.order[1])
    for load in loads[6:]:
        load.wait()

    span = width // 2

    @pl.loop(0, 3 * 2)
    def _(i):
        at = pl.ds(pl.multiple_of((i // 2) * dw, dw), dw)
        cols = pl.ds(pl.multiple_of((i % 2) * span, span), span)
        gi_s[at, cols] = dot_tn(gm_s[:, at], normed_s[:, cols]).astype(LOW)

    def piece_slot(f, m):
        kind, place = grid.qkv_piece(grid.ctx, f, m)
        return gi_s.at[pl.ds(pl.multiple_of((kind * grid.fsdp_n + place) * unit, unit), unit)]

    shards_i = ShardScatter(
        grid, copies, lambda f: [piece_slot(f, m) for m in range(3)], gi_core, gi_y
    )
    make_normed(grid.z_n - 2, grid.z_n - 2)
    for t in late.order:
        late.launch(t)

    small_s[0, 2:3, :] = jnp.sum(g_own_s[...].astype(F32), axis=0, keepdims=True)
    for kind in range(3):
        at = pl.ds(pl.multiple_of(grid.ctx * dw, 128), dw)
        terms = gm_s[:, kind * dw : (kind + 1) * dw].astype(F32)
        small_s[0, 4 + kind : 5 + kind, at] = jnp.sum(terms, axis=0, keepdims=True)
    offset = grid.ctx * fw
    at = pl.ds(pl.multiple_of(offset % width, 128), fw)
    terms = jnp.sum(gup_s[...].astype(F32), axis=0, keepdims=True)
    for row in range(4):
        small_s[0, 7 + row : 8 + row, at] = jnp.where(offset // width == row, terms, 0.0)

    def small_sum(step, buffer, stage):
        for i, sem in enumerate(stage):
            arrived(buffer.at[i], sem)
        accumulate(
            small_s.at[step + 1], small_s.at[step], *[buffer.at[i] for i in range(len(stage))]
        )

    stage = [
        copies.send(small_s.at[0], small_y.at[k - 1], fsdp=grid.yc(k, 0))
        for k in range(1, grid.y_n)
    ]

    def up_slot(f):
        return gu_s.at[pl.ds(pl.multiple_of(f * up_rows, up_rows), up_rows)]

    early.step(0)
    for k in shards_i.rounds:
        shards_i.step(k)
    early.step(1)

    @pl.loop(0, fw // 256 * 2)
    def _(i):
        at = pl.ds(pl.multiple_of((i // 2) * 256, 256), 256)
        cols = pl.ds(pl.multiple_of((i % 2) * span, span), span)
        gu_s[at, cols] = dot_tn(gup_s[:, at], normed_s[:, cols]).astype(LOW)

    shards_u = ShardScatter(grid, copies, lambda f: [up_slot(f)], gu_core, gu_y)
    early.step(2)
    small_sum(0, small_y, stage)
    stage = [
        copies.send(small_s.at[1], small_core.at[c - 1], fsdp=grid.yc(0, c))
        for c in range(1, grid.core_n)
    ]
    for k in shards_u.rounds:
        shards_u.step(k)
    early.step(3)
    early.step(grid.z_n)
    late.step(0)
    late.step(1)
    small_sum(1, small_core, stage)
    stage = [
        copies.send(small_s.at[2], small_x.at[l - 1], ctx=grid.zx(0, l))
        for l in range(1, grid.x_n)
    ]
    late.step(2)
    shards_i.finish()
    qkv_sems = []
    for m in range(3):
        owner = grid.qkv_owner(grid.ctx, grid.fsdp, m)
        qkv_sems.append(
            copies.send_or_keep(piece_slot(grid.fsdp, m), gi_got.at[m], owner, grid.ctx)
        )
    late.step(3)
    small_sum(2, small_x, stage)
    stage = [
        copies.send(small_s.at[3], small_z.at[k - 1], ctx=grid.zx(k, 0))
        for k in range(1, grid.z_n)
    ]
    shards_u.finish()
    puts = [copies.local(up_slot(grid.fsdp), gu_out)]
    late.step(grid.z_n)
    early.finish()
    late.finish()
    puts.append(copies.local(pn_sum, total_out))
    own_o.wait()
    for (k, l), sem in zip(peers, out_sems):
        arrived(go_got.at[grid.zx(-k, -l)], sem)
    puts.append(copies.local(go_got, go_out))
    for m in range(3):
        arrived(gi_got.at[m], qkv_sems[m])
    puts.append(copies.local(gi_got, gi_out))
    small_sum(3, small_z, stage)
    puts.append(copies.local(small_s.at[4], small_out))
    for put in puts:
        put.wait()
    copies.drain()


def solution(mesh):
    shape = mesh.shape["ctx"], mesh.shape["fsdp"]
    ctx_n, fsdp_n = shape
    n = ctx_n * fsdp_n
    plan = Grid(*shape)
    x_n, z_n, core_n, y_n = plan.x_n, plan.z_n, plan.core_n, plan.y_n

    def gather(x_own, g_own, w_qkv, w_fc1, w_fc2, w_dense, small, tables):
        local_len, width = x_own.shape
        unit, hidden_units = w_fc2.shape
        length = ctx_n * local_len
        fw, dw = hidden_units // ctx_n, width // ctx_n
        pair = 2 * HEAD_DIM
        small_rows = jax.ShapeDtypeStruct((16, width), LOW)
        kept = [
            jax.ShapeDtypeStruct((length, width), LOW),
            jax.ShapeDtypeStruct((length, width), LOW),
            jax.ShapeDtypeStruct((3 * fsdp_n * unit, width), LOW),
            jax.ShapeDtypeStruct((fw, width), LOW),
            jax.ShapeDtypeStruct((ctx_n, fsdp_n, unit, fw + dw), LOW),
        ]
        made = [
            jax.ShapeDtypeStruct((length, width), LOW),
            jax.ShapeDtypeStruct((length, fw + dw), LOW),
            jax.ShapeDtypeStruct((length, fw), LOW),
            jax.ShapeDtypeStruct((3, dw // pair, length, pair), LOW),
            jax.ShapeDtypeStruct((dw // pair, length, pair), F32),
            jax.ShapeDtypeStruct((length, pair), F32),
        ]
        return pl.pallas_call(
            functools.partial(gather_kernel, shape),
            out_shape=kept + [small_rows] + made,
            in_specs=[anywhere] * 6 + [inside] * 9,
            out_specs=[anywhere] * 12,
            scratch_shapes=[pltpu.VMEM(s.shape, s.dtype) for s in kept + made]
            + [pltpu.VMEM((length, 3 * dw), LOW), pltpu.VMEM((dw // pair, length, pair), LOW)]
            + [pltpu.VMEM((16, width), F32), pltpu.VMEM((3, 8, dw), F32)]
            + [pltpu.VMEM((max(fw // 256, 1), 8, min(fw, 256)), F32)]
            + [pltpu.VMEM((count, 16, width), LOW) for count in (5, x_n, core_n, y_n, z_n)]
            + [pltpu.SemaphoreType.DMA((SEMAPHORES,))],
            compiler_params=pltpu.CompilerParams(
                collective_id=0, has_side_effects=True, vmem_limit_bytes=VMEM_BYTES
            ),
            name="gather",
        )(x_own, g_own, w_qkv, w_fc1, w_fc2, w_dense, *small, *tables)

    def token_scratch(local_len, width):
        return [
            pltpu.VMEM((z_n, x_n * local_len, width), LOW),
            pltpu.VMEM((z_n, max(x_n - 1, 1), local_len, width), LOW),
            pltpu.VMEM((z_n + 1, local_len, width), LOW),
            pltpu.VMEM((local_len, width), F32),
        ]

    def shard_scratch(parts, *block):
        return [
            pltpu.VMEM((y_n, parts) + block, LOW),
            pltpu.VMEM((max(y_n - 1, 1), parts) + block, LOW),
        ]

    def inside_like(*arrays):
        return [pltpu.VMEM(a.shape, a.dtype) for a in arrays]

    anywhere = pl.BlockSpec(memory_space=pl.ANY)
    inside = pl.BlockSpec(memory_space=pltpu.VMEM)

    def scatter_out(hidden, wo, g_all, slope, qkv, lse, tables):
        length, cols = hidden.shape
        local_len, width = length // ctx_n, g_all.shape[1]
        unit = width // n
        fw = slope.shape[1]
        dw, pair = cols - fw, 2 * HEAD_DIM
        return pl.pallas_call(
            functools.partial(scatter_out_kernel, shape),
            out_shape=[
                jax.ShapeDtypeStruct((local_len, width), F32),
                jax.ShapeDtypeStruct((ctx_n, unit, cols), LOW),
                jax.ShapeDtypeStruct((length, fw), LOW),
                jax.ShapeDtypeStruct((length, 3 * dw), LOW),
            ],
            in_specs=[anywhere] * 6 + [inside] * 3,
            out_specs=[anywhere] * 4,
            scratch_shapes=inside_like(hidden, wo, g_all, slope, qkv, lse)
            + token_scratch(local_len, width)
            + [pltpu.VMEM((ctx_n, fsdp_n, unit, cols), LOW)]
            + shard_scratch(1, ctx_n, unit, cols)
            + [pltpu.VMEM((length, c), LOW) for c in (fw, dw, 3 * dw)]
            + [pltpu.VMEM((dw // pair, length, pair), LOW)]
            + inside_like(qkv)
            + [pltpu.VMEM((length, pair), F32)] * 3
            + [pltpu.SemaphoreType.DMA((SEMAPHORES,))],
            compiler_params=pltpu.CompilerParams(
                collective_id=1, has_side_effects=True, vmem_limit_bytes=VMEM_BYTES
            ),
            name="scatter_out",
        )(hidden, wo, g_all, slope, qkv, lse, *tables)

    def scatter_in(gm, wi, gup, wu, x_all, stats, normed, g_own, go):
        length, width = normed.shape
        local_len = length // ctx_n
        unit, up_rows = width // n, wu.shape[0] // fsdp_n
        return pl.pallas_call(
            functools.partial(scatter_in_kernel, shape),
            out_shape=[
                jax.ShapeDtypeStruct((local_len, width), F32),
                jax.ShapeDtypeStruct((up_rows, width), LOW),
                jax.ShapeDtypeStruct((3, unit, width), LOW),
                jax.ShapeDtypeStruct(go.shape, LOW),
                jax.ShapeDtypeStruct((16, width), F32),
            ],
            in_specs=[anywhere] * 9,
            out_specs=[anywhere] * 5,
            scratch_shapes=inside_like(gm, wi, gup, wu, x_all, stats, normed, g_own)
            + token_scratch(local_len, width)
            + inside_like(wu)
            + shard_scratch(1, up_rows, width)
            + inside_like(wi)
            + shard_scratch(3, unit, width)
            + [pltpu.VMEM((3, unit, width), LOW)]
            + inside_like(go)
            + [pltpu.VMEM((count, 16, width), F32) for count in (5, y_n, x_n, core_n, z_n)]
            + [pltpu.SemaphoreType.DMA((SEMAPHORES,))],
            compiler_params=pltpu.CompilerParams(
                collective_id=2, has_side_effects=True, vmem_limit_bytes=VMEM_BYTES
            ),
            name="scatter_in",
        )(gm, wi, gup, wu, x_all, stats, normed, g_own, go)

    def body(
        hidden_in, positions, ln_gain, ln_bias, w_qkv, b_qkv, w_dense, b_dense,
        w_fc1, b_fc1, w_fc2, b_fc2, out_grad,
    ):
        local_len, width = hidden_in.shape[1:]
        hidden_units = w_fc2.shape[1]
        unit = w_dense.shape[0]
        up_rows = w_fc1.shape[0]
        fw, dw = hidden_units // ctx_n, width // ctx_n
        my_ctx = lax.axis_index("ctx")
        me = my_ctx * fsdp_n + lax.axis_index("fsdp")
        length = positions.shape[1]
        x_own, g_own = hidden_in[0], out_grad[0]

        rank = positions[0, ::RUN] // RUN
        starts, steps = turning_tables(length)
        ranks = jnp.arange(length // RUN, dtype=jnp.int32)
        chosen = (rank[:, None] == ranks[None, :])[None, :, :, None]
        stored_starts = jnp.sum(jnp.where(chosen, starts[:, None], 0.0), axis=2)

        own_small = [
            a.reshape(-1, unit) for a in (ln_gain, ln_bias, b_dense, b_fc2, b_qkv, b_fc1)
        ]
        x_all, g_all, wi, wu, wo, small, normed, hidden, slope, qkv, lse, stats = gather(
            x_own, g_own, w_qkv, w_fc1, w_fc2, w_dense, own_small, (positions, stored_starts, steps)
        )
        small = small.astype(F32)
        gain, bias_dense, bias_down = small[0], small[2], small[3]
        total, grad_o, grad_upward, grad_mixed = scatter_out(
            hidden, wo.reshape(width, fw + dw), g_all, slope, qkv, lse, (positions, starts, steps)
        )
        grad_normed, grad_up, grad_qkv, grad_o, sums = scatter_in(
            grad_mixed, wi, grad_upward, wu, x_all, stats, normed, g_own, grad_o
        )

        def standardize(values):
            wide = values.astype(F32)
            centered = wide - jnp.mean(wide, axis=-1, keepdims=True)
            spread = lax.rsqrt(jnp.mean(centered * centered, axis=-1, keepdims=True) + EPSILON)
            return centered * spread, spread

        hidden_out = (total + x_own.astype(F32) + bias_dense + bias_down).astype(LOW)
        xhat, spread = standardize(x_own)
        e = grad_normed * gain
        grad_in = (
            e - jnp.mean(e, axis=-1, keepdims=True)
            - xhat * jnp.mean(e * xhat, axis=-1, keepdims=True)
        ) * spread + g_own.astype(F32)
        grad_o = grad_o.transpose(1, 0, 2).astype(F32)
        sums = sums.reshape(-1)

        def own_slice(row, size):
            return lax.dynamic_slice_in_dim(sums, row * width + me * size, size)

        grad_b_out = own_slice(2, unit)
        return (
            hidden_out[None],
            grad_in[None],
            own_slice(0, unit),
            own_slice(1, unit),
            grad_qkv.reshape(3 * unit, width).astype(F32),
            own_slice(4, 3 * unit),
            grad_o[:, :, fw:].reshape(unit, width),
            grad_b_out,
            grad_up.astype(F32),
            own_slice(7, up_rows),
            grad_o[:, :, :fw].reshape(unit, hidden_units),
            grad_b_out,
        )

    tokens, rows, cells = P("fsdp", "ctx", None), P(BOTH, None), P(BOTH)
    return jax.shard_map(
        body,
        mesh=mesh,
        in_specs=(
            tokens, P("fsdp", None), cells, cells, rows, cells, rows, cells,
            rows, cells, rows, cells, tokens,
        ),
        out_specs=(
            tokens, tokens, cells, cells, rows, cells, rows, cells, rows, cells, rows, cells,
        ),
        check_vma=False,
    )
```

```python
import functools

import jax
import jax.numpy as jnp
import numpy as np
from jax import lax
from jax.experimental import pallas as pl
from jax.experimental.pallas import tpu as pltpu
from jax.sharding import PartitionSpec as P

HEAD_DIM = 64
ROT_DIM = 32
RUN = 64
EPSILON = 1e-05
SCORE_SCALE = 0.125
BOTH = ("ctx", "fsdp")
F32 = jnp.float32
LOW = jnp.bfloat16
MESH = pl.DeviceIdType.MESH
SEMAPHORES = 512
VMEM_BYTES = 60 * 1024 * 1024
SMALL_ROWS = (
    [(row, (1, 0)) for row in range(4)]
    + [(4, (3, j)) for j in range(3)]
    + [(7, (4, j)) for j in range(4)]
)


def dot_nt(a, b):
    return lax.dot_general(a, b, (((1,), (1,)), ((), ())), preferred_element_type=F32)


def dot_nn(a, b):
    return lax.dot_general(a, b, (((1,), (0,)), ((), ())), preferred_element_type=F32)


def dot_tn(a, b):
    return lax.dot_general(a, b, (((0,), (0,)), ((), ())), preferred_element_type=F32)


def turning_tables(length):
    half_rot = ROT_DIM // 2
    lane = np.arange(2 * HEAD_DIM) % HEAD_DIM
    freqs = np.where(lane < ROT_DIM, 10000.0 ** (-(lane % half_rot) / half_rot), 0.0)
    starts = np.arange(0, length, RUN)[:, None] * freqs[None, :]
    steps = np.arange(RUN)[:, None] * freqs[None, :]
    return (
        np.stack([np.cos(starts), np.sin(starts)]).astype(np.float32),
        np.stack([np.cos(steps), np.sin(steps)]).astype(np.float32),
    )


def run_turn(start_ref, step_ref, run):
    lane = lax.broadcasted_iota(jnp.int32, (RUN, 2 * HEAD_DIM), 1) % HEAD_DIM
    half_rot = ROT_DIM // 2
    cos_a, sin_a = start_ref[0, pl.ds(run, 1), :], start_ref[1, pl.ds(run, 1), :]
    cos_b, sin_b = step_ref[0], step_ref[1]
    cosine = cos_a * cos_b - sin_a * sin_b
    sine = sin_a * cos_b + cos_a * sin_b
    above = jnp.where(lane < half_rot, -sine, 0.0)
    below = jnp.where((lane >= half_rot) & (lane < ROT_DIM), sine, 0.0)
    return cosine, above, below


def turn(u, tables, way=1.0):
    cosine, above, below = tables
    half_rot = ROT_DIM // 2
    width = 2 * HEAD_DIM
    moved = pltpu.roll(u, width - half_rot, 1) * above + pltpu.roll(u, half_rot, 1) * below
    return u * cosine + way * moved


def masked_tile(scores, diagonal, start):
    last = jnp.where(diagonal, scores[:, start:], -1e30)
    return jnp.concatenate([scores[:, :start], last], axis=1) if start > 0 else last


def lower_triangle(tile):
    return lax.broadcasted_iota(jnp.int32, (tile, tile), 1) <= lax.broadcasted_iota(
        jnp.int32, (tile, tile), 0
    )


def head_lanes(tile, head):
    lanes = lax.broadcasted_iota(jnp.int32, (tile, 2 * HEAD_DIM), 1)
    return (lanes // HEAD_DIM) == head


def pick(mine, values):
    return jnp.where(mine, values, jnp.zeros_like(values))


def attend(q_s, k_s, v_s, ctx_s, lse_s):
    length = q_s.shape[0]
    tile = min(256, length)
    diagonal = lower_triangle(tile)
    for start in range(0, length, tile):
        rows, reach = slice(start, start + tile), start + tile

        for head in range(2):
            mine = head_lanes(tile, head)
            scores = dot_nt(pick(mine, q_s[rows, :]), k_s[:reach, :])
            scores = masked_tile(scores, diagonal, start)
            peak = jnp.max(scores, axis=1, keepdims=True)
            exps = jnp.exp(scores - peak)
            total = jnp.sum(exps, axis=1, keepdims=True)
            probs_low = (exps * (1.0 / total)).astype(LOW)
            context = dot_nn(probs_low, v_s[:reach, :]).astype(LOW)
            ctx_s[rows, :] = jnp.where(mine, context, ctx_s[rows, :])
            lse_s[rows, :] = jnp.where(mine, peak + jnp.log(total), lse_s[rows, :])


class Grid:
    def __init__(self, ctx_n, fsdp_n):
        self.ctx_n, self.fsdp_n = ctx_n, fsdp_n
        self.x_n = 1 << ((ctx_n.bit_length() - 1) // 2)
        self.z_n = ctx_n // self.x_n
        self.core_n = 2 if fsdp_n % 2 == 0 else 1
        self.y_n = fsdp_n // self.core_n
        self.undo = 1 if ctx_n % 3 == 1 else 2

    def locate(self):
        self.ctx, self.fsdp = lax.axis_index("ctx"), lax.axis_index("fsdp")
        self.z, self.x = self.ctx // self.x_n, self.ctx % self.x_n
        self.y, self.core = self.fsdp // self.core_n, self.fsdp % self.core_n
        return self

    def zx(self, dz, dx):
        return ((self.z + dz + self.z_n) % self.z_n) * self.x_n + (
            self.x + dx + self.x_n
        ) % self.x_n

    def yc(self, dy, dc):
        return ((self.y + dy + self.y_n) % self.y_n) * self.core_n + (
            self.core + dc + self.core_n
        ) % self.core_n

    def nearest(self, j):
        place = 0
        for z in range(self.z_n):
            order = sorted(range(self.z_n), key=lambda other: (abs(other - z), other))
            place = place + jnp.where(self.z == z, order[j], 0)
        return place

    def qkv_piece(self, ctx, fsdp, m):
        span = 3 * self.fsdp_n
        v = (3 * fsdp + m + span * self.ctx_n - ctx * self.fsdp_n) % span
        return ((v // self.fsdp_n) * self.undo) % 3, v % self.fsdp_n

    def qkv_owner(self, ctx, fsdp, m):
        kind, place = self.qkv_piece(ctx, fsdp, m)
        piece = self.ctx_n * self.fsdp_n * kind + ctx * self.fsdp_n + place
        return piece // 3 // self.fsdp_n

    def qkv_user(self, ctx, fsdp, m):
        piece = 3 * (ctx * self.fsdp_n + fsdp) + m
        return (piece % (self.ctx_n * self.fsdp_n)) // self.fsdp_n

    def greet(self):
        barrier = pltpu.get_barrier_semaphore()
        for k in range(1, self.ctx_n):
            pl.semaphore_signal(
                barrier, inc=1, device_id={"ctx": (self.ctx + k) % self.ctx_n}, device_id_type=MESH
            )
        for k in range(1, self.fsdp_n):
            pl.semaphore_signal(
                barrier,
                inc=1,
                device_id={"fsdp": (self.fsdp + k) % self.fsdp_n},
                device_id_type=MESH,
            )
        pl.semaphore_wait(barrier, self.ctx_n + self.fsdp_n - 2)


class Copies:
    def __init__(self, sems):
        self.sems, self.used, self.sent, self.perhaps = sems, 0, [], []

    def sem(self):
        self.used += 1
        return self.sems.at[self.used - 1]

    def send(self, src, dst, **where):
        send_sem, recv_sem = self.sem(), self.sem()
        copy = pltpu.make_async_remote_copy(
            src_ref=src,
            dst_ref=dst,
            send_sem=send_sem,
            recv_sem=recv_sem,
            device_id=where,
            device_id_type=MESH,
        )
        copy.start()
        self.sent.append(copy)
        return recv_sem

    def send_or_keep(self, src, dst, ctx, own_ctx):
        send_sem, recv_sem = self.sem(), self.sem()
        remote = pltpu.make_async_remote_copy(
            src_ref=src,
            dst_ref=dst,
            send_sem=send_sem,
            recv_sem=recv_sem,
            device_id={"ctx": ctx},
            device_id_type=MESH,
        )

        @pl.when(ctx != own_ctx)
        def _():
            remote.start()

        @pl.when(ctx == own_ctx)
        def _():
            pltpu.make_async_copy(src, dst, recv_sem).start()

        self.perhaps.append((ctx != own_ctx, remote))
        return recv_sem

    def prepare(self, src, dst, **where):
        send_sem, recv_sem = self.sem(), self.sem()
        remote = pltpu.make_async_remote_copy(
            src_ref=src,
            dst_ref=dst,
            send_sem=send_sem,
            recv_sem=recv_sem,
            device_id=where,
            device_id_type=MESH,
        )
        return remote, recv_sem

    def start_if(self, when, remote):
        @pl.when(when)
        def _():
            remote.start()

        self.perhaps.append((when, remote))

    def send_if(self, when, src, dst, **where):
        remote, recv_sem = self.prepare(src, dst, **where)
        self.start_if(when, remote)
        return recv_sem

    def local(self, src, dst):
        copy = pltpu.make_async_copy(src, dst, self.sem())
        copy.start()
        return copy

    def drain(self):
        for copy in self.sent:
            copy.wait_send()
        for sent, copy in self.perhaps:

            @pl.when(sent)
            def _(copy=copy):
                copy.wait_send()


def arrived(ref, sem):
    pltpu.make_async_copy(ref, ref, sem).wait()


class TokenGather:
    def __init__(self, grid, copies, own, buffer):
        self.grid, self.copies, self.buffer = grid, copies, buffer
        self.rows = own.shape[0]
        self.across = []
        self.kept = copies.local(own, self.slot(0, 0))
        self.along = {
            way: copies.send_if(self.ends(way), own, self.slot(0, 0), ctx=grid.zx(way, 0))
            for way in (1, -1)
        }
        for l in range(1, grid.x_n):
            sem = copies.send(own, self.slot(0, 0), ctx=grid.zx(0, l))
            self.across.append((0, 1, l, sem))

    def slot(self, k, l):
        start = pl.multiple_of(self.grid.zx(-k, -l) * self.rows, self.rows)
        return self.buffer.at[pl.ds(start, self.rows)]

    def ends(self, way):
        return self.grid.z < self.grid.z_n - 1 if way > 0 else self.grid.z > 0

    def has(self, k, way):
        z = self.grid.z
        return z >= k if way > 0 else z + k < self.grid.z_n

    def step(self, k):
        grid, copies, along = self.grid, self.copies, {}
        for way in (1, -1):
            slot, here = self.slot(k * way, 0), self.has(k, way)

            @pl.when(here)
            def _(slot=slot, way=way):
                arrived(slot, self.along[way])

            if k < grid.z_n - 1:
                along[way] = copies.send_if(
                    here & self.ends(way), slot, slot, ctx=grid.zx(way, 0)
                )
            for l in range(1, grid.x_n):
                sem = copies.send_if(here, slot, slot, ctx=grid.zx(0, l))
                self.across.append((k, way, l, sem))
        self.along = along

    def ready(self, k):
        if k == 0:
            self.kept.wait()
        for m, way, l, sem in self.across:
            if m == k:

                @pl.when(self.has(k, way))
                def _(way=way, l=l, sem=sem):
                    arrived(self.slot(k * way, l), sem)


class ShardGather:
    def __init__(self, grid, copies, own, view):
        self.grid, self.copies, self.view = grid, copies, view
        self.along_y = [
            copies.send(own, view(grid.fsdp), fsdp=grid.yc(k, 0)) for k in range(1, grid.y_n)
        ]
        self.across = []
        self.cross(own, 0)

    def cross(self, src, k):
        for c in range(1, self.grid.core_n):
            slot = self.view(self.grid.yc(-k, 0))
            self.across.append((k, c, self.copies.send(src, slot, fsdp=self.grid.yc(0, c))))

    def forward(self):
        for k in range(1, self.grid.y_n):
            slot = self.view(self.grid.yc(-k, 0))
            arrived(slot, self.along_y[k - 1])
            self.cross(slot, k)

    def finish(self):
        for k, c, sem in self.across:
            arrived(self.view(self.grid.yc(-k, -c)), sem)


def gather_kernel(
    shape, x_in, g_in, wq_in, wu_in, wf_in, wd_in,
    gain_in, shift_in, bd_in, bf_in, bq_in, bu_in, row_in, start_in, step_in,
    x_out, g_out, wi_out, wu_out, wo_out, small_out, normed_out, hidden_out, slope_out,
    qkv_out, lse_out, stats_out,
    x_s, g_s, wi_s, wu_s, wo_s, normed_s, hidden_s, slope_s, qkv_s, lse_s, stats_s,
    mixed_s, ctx_s, small_f, qkv_bias_s, up_bias_s, small_s, small_x, small_core, small_y, small_z, sems,
):
    grid = Grid(*shape).locate()
    copies = Copies(sems)
    local_len, width = x_in.shape
    unit, up_rows = wd_in.shape[0], wu_in.shape[0]
    fw, dw = wf_in.shape[1] // grid.ctx_n, wd_in.shape[1] // grid.ctx_n
    n = grid.ctx_n * grid.fsdp_n
    me = grid.ctx * grid.fsdp_n + grid.fsdp
    peers = [(k, l) for k in range(grid.z_n) for l in range(grid.x_n) if k or l]
    pairs = dw // (2 * HEAD_DIM)
    small_in = gain_in, shift_in, bd_in, bf_in, bq_in, bu_in
    puts = []

    row_index = lax.broadcasted_iota(jnp.int32, (16, width), 0)
    placed = jnp.zeros((16, width), F32)
    small_f[...] = jnp.zeros_like(small_f)
    row = 0
    for piece_in in small_in:
        small_f[row : row + piece_in.shape[0], 0:unit] = piece_in[...].astype(F32)
        row += piece_in.shape[0]
    pieces_in = small_f[...]
    for row, (base, each) in enumerate(SMALL_ROWS):
        piece = each[0] * me + each[1]
        value = jnp.broadcast_to(pieces_in[row : row + 1, :], (16, width))
        value = pltpu.roll(value, (piece % n) * unit, 1)
        placed = placed + jnp.where(row_index == piece // n + base, value, 0.0)
    small_s[0] = placed.astype(LOW)
    grid.greet()

    def small_sum(step, buffer, stage):
        for i, sem in enumerate(stage):
            arrived(buffer.at[i], sem)
        accumulate(
            small_s.at[step + 1], small_s.at[step], *[buffer.at[i] for i in range(len(stage))]
        )

    stage = [
        copies.send(small_s.at[0], small_y.at[k - 1], fsdp=grid.yc(k, 0))
        for k in range(1, grid.y_n)
    ]

    def up_slot(f):
        return wu_s.at[pl.ds(pl.multiple_of(f * up_rows, up_rows), up_rows)]

    up_kept = copies.local(wu_in, up_slot(grid.fsdp))
    up = ShardGather(grid, copies, wu_in, up_slot)
    qkv_sems = []

    def piece_slot(ctx, fsdp, m):
        kind, place = grid.qkv_piece(ctx, fsdp, m)
        return wi_s.at[pl.ds(pl.multiple_of((kind * grid.fsdp_n + place) * unit, unit), unit)]

    for m in range(3):
        user = grid.qkv_user(grid.ctx, grid.fsdp, m)
        qkv_sems.append(
            copies.send_or_keep(
                wq_in.at[pl.ds(m * unit, unit)],
                piece_slot(user, grid.fsdp, m),
                user,
                grid.ctx,
            )
        )
    small_sum(0, small_y, stage)
    stage = [
        copies.send(small_s.at[1], small_x.at[l - 1], ctx=grid.zx(0, l))
        for l in range(1, grid.x_n)
    ]
    tokens_x = TokenGather(grid, copies, x_in, x_s)
    small_sum(1, small_x, stage)
    stage = [
        copies.send(small_s.at[2], small_core.at[c - 1], fsdp=grid.yc(0, c))
        for c in range(1, grid.core_n)
    ]
    small_sum(2, small_core, stage)
    stage = [
        copies.send(small_s.at[3], small_z.at[k - 1], ctx=grid.zx(k, 0))
        for k in range(1, grid.z_n)
    ]

    def column_block(ref, index, block):
        return ref.at[:, pl.ds(pl.multiple_of(index * block, 128), block)]

    mine = wo_s.at[grid.ctx, grid.fsdp]
    own_out = [
        copies.local(column_block(wf_in, grid.ctx, fw), mine.at[:, pl.ds(0, fw)]),
        copies.local(column_block(wd_in, grid.ctx, dw), mine.at[:, pl.ds(fw, dw)]),
    ]
    out_sems = {}

    def send_out(k):
        for l in range(grid.x_n):
            if k or l:
                target = grid.zx(k, l)
                out_sems[k, l] = (
                    copies.send(
                        column_block(wf_in, target, fw), mine.at[:, pl.ds(0, fw)], ctx=target
                    ),
                    copies.send(
                        column_block(wd_in, target, dw), mine.at[:, pl.ds(fw, dw)], ctx=target
                    ),
                )

    shards = []

    def spread_out(k):
        first = ((grid.z - k + grid.z_n) % grid.z_n) * grid.x_n
        for l in range(grid.x_n):
            slot = wo_s.at[grid.zx(-k, -l), grid.fsdp]
            if k or l:
                arrived(slot.at[:, pl.ds(0, fw)], out_sems[k, l][0])
                arrived(slot.at[:, pl.ds(fw, dw)], out_sems[k, l][1])
            else:
                own_out[0].wait()
                own_out[1].wait()

        def out_view(f):
            return wo_s.at[pl.ds(first, grid.x_n), f]

        shards.append(ShardGather(grid, copies, out_view(grid.fsdp), out_view))

    group = grid.x_n * local_len

    def group_rows(first, i, parts):
        place = grid.nearest(first)
        for later in range(first + 1, min(first + 2, grid.z_n)):
            place = jnp.where(i // parts == later - first, grid.nearest(later), place)
        return pl.multiple_of(place * group + (i % parts) * tile_rows, tile_rows)

    def normalize(k):
        first = pl.multiple_of(grid.nearest(k) * group, group)
        gain, shift = small_f[0:1, :], small_f[1:2, :]

        @pl.loop(0, group // 16)
        def _(i):
            rows = pl.ds(pl.multiple_of(first + i * 16, 16), 16)
            wide = x_s[rows, :].astype(F32)
            mean = jnp.mean(wide, axis=-1, keepdims=True)
            centered = wide - mean
            spread = lax.rsqrt(jnp.mean(centered * centered, axis=-1, keepdims=True) + EPSILON)
            normed_s[rows, :] = (centered * spread * gain + shift).astype(LOW)
            lane = lax.broadcasted_iota(jnp.int32, (16, 2 * HEAD_DIM), 1)
            stats_s[rows, :] = jnp.where(lane < HEAD_DIM, mean, spread)

    tile_rows = min(256, group)

    tiles = group // tile_rows

    def project_up(k, groups=1):
        block = min(256, fw)

        @pl.loop(0, groups * tiles * (fw // block))
        def _(i):
            col = (i % (fw // block)) * block
            rows = pl.ds(group_rows(k, i // (fw // block), tiles), tile_rows)
            cols = pl.ds(pl.multiple_of(col, block), block)
            bias = up_bias_s[i % (fw // block), 0:1, :]
            upward = dot_nt(normed_s[rows, :], wu_s[cols, :]) + bias
            square = upward * upward
            bend = jnp.tanh(0.7978845608028654 * (upward + 0.044715 * square * upward))
            half = 0.5 * (1.0 + bend)
            hidden_s[rows, cols] = (upward * half).astype(LOW)
            inner_slope = 0.7978845608028654 * (1.0 + 3.0 * 0.044715 * square)
            slope = half + 0.5 * upward * (1.0 - bend * bend) * inner_slope
            slope_s[rows, cols] = slope.astype(LOW)

    def project_qkv(k, groups=1):
        @pl.loop(0, groups * tiles)
        def _(i):
            start = group_rows(k, i, tiles)
            rows = pl.ds(start, tile_rows)
            for kind in range(3):
                result = dot_nt(normed_s[rows, :], wi_s[kind * dw : (kind + 1) * dw, :])
                result = result + qkv_bias_s[kind, 0:1, :]
                if kind == 2:
                    mixed_s[rows, kind * dw : (kind + 1) * dw] = result.astype(LOW)
                    continue
                for run in range(tile_rows // RUN):
                    tables = run_turn(start_in, step_in, start // RUN + run)
                    run_at = pl.ds(pl.multiple_of(start + run * RUN, RUN), RUN)
                    for p in range(pairs):
                        lanes = slice(p * 2 * HEAD_DIM, (p + 1) * 2 * HEAD_DIM)
                        turned = turn(result[run * RUN : (run + 1) * RUN, lanes], tables)
                        low = turned.astype(LOW)
                        if kind == 0:
                            low = (low * SCORE_SCALE).astype(LOW)
                        at = kind * dw + p * 2 * HEAD_DIM
                        mixed_s[run_at, at : at + 2 * HEAD_DIM] = low

    last = grid.z_n - 1
    tokens_x.step(1)
    send_out(0)
    for k in range(2, last):
        tokens_x.step(k)
        send_out(k - 1)
    tokens_g = TokenGather(grid, copies, g_in, g_s)
    send_out(last - 1)
    tokens_x.step(last)
    send_out(last)
    pieces = []
    for m in range(3):
        arrived(piece_slot(grid.ctx, grid.fsdp, m), qkv_sems[m])
        pieces.append(
            ShardGather(
                grid,
                copies,
                piece_slot(grid.ctx, grid.fsdp, m),
                lambda f, m=m: piece_slot(grid.ctx, f, m),
            )
        )
    up.forward()
    small_sum(3, small_z, stage)
    puts.append(copies.local(small_s.at[4], small_out))
    small_f[...] = small_s[4].astype(F32)
    for kind in range(3):
        at = pl.ds(pl.multiple_of(grid.ctx * dw, 128), dw)
        row = small_f[4 + kind : 5 + kind, at]
        qkv_bias_s[kind] = jnp.broadcast_to(row, qkv_bias_s.shape[1:])
    block = up_bias_s.shape[2]
    for i in range(fw // block):
        offset = grid.ctx * fw
        at = pl.ds(pl.multiple_of(offset % width + i * block, 128), block)
        row = jnp.zeros((1, block), F32)
        for j in range(4):
            row = row + jnp.where(offset // width == j, small_f[7 + j : 8 + j, at], 0.0)
        up_bias_s[i] = jnp.broadcast_to(row, up_bias_s.shape[1:])
    tokens_x.ready(0)
    normalize(0)
    up_kept.wait()
    up.finish()
    puts.append(copies.local(wu_s, wu_out))
    for gather in pieces:
        gather.forward()
    tokens_x.ready(1)
    normalize(1)
    project_up(0, 2)
    for gather in pieces:
        gather.finish()
    puts.append(copies.local(wi_s, wi_out))
    project_qkv(0, 2)
    tokens_g.step(1)
    spread_out(0)
    for k in range(2, grid.z_n):
        tokens_x.ready(k)
        normalize(k)
        project_up(k)
        project_qkv(k)
        spread_out(k - 1)
        shards[k - 2].forward()
        if k == last:
            spread_out(last)
        if k > 2:
            tokens_g.step(k - 1)
    puts.append(copies.local(x_s, x_out))
    puts.append(copies.local(normed_s, normed_out))
    puts.append(copies.local(slope_s, slope_out))
    puts.append(copies.local(stats_s, stats_out))
    length = x_s.shape[0]
    pair = 2 * HEAD_DIM

    tall = min(256, length)

    @pl.loop(0, length // tall)
    def _(i):
        start = pl.multiple_of(i * tall, tall)
        result = dot_nn(to_sorted(row_in, start, tall), mixed_s[...]).astype(LOW)
        for kind in range(3):
            for p in range(pairs):
                at = kind * dw + p * pair
                qkv_s[kind, p, pl.ds(start, tall), :] = result[:, at : at + pair]

    @pl.loop(0, pairs)
    def _(p):
        attend(qkv_s.at[0, p], qkv_s.at[1, p], qkv_s.at[2, p], ctx_s.at[p], lse_s.at[p])

    @pl.loop(0, length // tall)
    def _(i):
        start = pl.multiple_of(i * tall, tall)
        back = to_stored(row_in, start, tall)
        for p in range(pairs):
            at = slice(fw + p * pair, fw + (p + 1) * pair)
            hidden_s[pl.ds(start, tall), at] = dot_tn(back, ctx_s[p]).astype(LOW)

    tokens_g.step(last)
    for gather in shards[last - 1 :]:
        gather.forward()
    puts.append(copies.local(hidden_s, hidden_out))
    puts.append(copies.local(qkv_s, qkv_out))
    puts.append(copies.local(lse_s, lse_out))
    for gather in shards:
        gather.finish()
    puts.append(copies.local(wo_s, wo_out))
    for k in range(grid.z_n):
        tokens_g.ready(k)
    puts.append(copies.local(g_s, g_out))
    for put in puts:
        put.wait()
    copies.drain()


def accumulate(dst, *sources):
    if len(dst.shape) == 3:

        @pl.loop(0, dst.shape[0])
        def _(i):
            accumulate(dst.at[i], *[source.at[i] for source in sources])

        return
    rows, step = dst.shape[0], 16

    @pl.loop(0, rows // step)
    def _(i):
        part = pl.ds(pl.multiple_of(i * step, step), step)
        total = sources[0][part, :].astype(F32)
        for source in sources[1:]:
            total = total + source[part, :].astype(F32)
        dst[part, :] = total.astype(dst.dtype)


class TokenScatter:
    def __init__(self, grid, copies, parts, from_x, from_z, total, half):
        self.grid, self.copies, self.parts = grid, copies, parts
        self.rows = total.shape[0]
        self.cols = pl.ds(half * (total.shape[1] // 2), total.shape[1] // 2)
        self.from_x, self.from_z = from_x.at[:, :, :, self.cols], from_z.at[:, :, self.cols]
        self.total = total.at[:, self.cols]
        self.along_x, self.sems, self.remotes = {}, {}, {}
        self.order = [t for i in range(grid.z_n // 2) for t in (grid.z_n - 1 - i, i)]

    def block(self, t, dx):
        x = (self.grid.x + dx) % self.grid.x_n
        rows = pl.ds(pl.multiple_of(x * self.rows, self.rows), self.rows)
        return self.parts.at[t, rows, self.cols]

    def launch(self, t):
        for l in range(1, self.grid.x_n):
            self.along_x[t, l] = self.copies.send(
                self.block(t, l), self.from_x.at[t, l - 1], ctx=self.grid.zx(0, l)
            )

    def collect(self, t):
        terms = [self.block(t, 0)]
        for l in range(1, self.grid.x_n):
            arrived(self.from_x.at[t, l - 1], self.along_x[t, l])
            terms.append(self.from_x.at[t, l - 1])
        accumulate(terms[0], *terms)

    def hop(self, t, way, first, z):
        grid, own, slot = self.grid, self.block(t, 0), self.from_z.at[t]
        if first:
            after = slot
            if way < 0:
                after = self.from_z.at[jnp.where(grid.z - 1 == t, grid.z_n, t)]
            remote, sem = self.copies.prepare(own, after, ctx=grid.zx(way, 0))
            self.remotes[t, way], self.sems[t, way] = remote, sem
            self.copies.perhaps.append((grid.z < t if way > 0 else grid.z > t, remote))

        @pl.when(grid.z == z)
        def _():
            if not first:
                arrived(slot, self.sems[t, way])
                accumulate(own, own, slot)
            self.remotes[t, way].start()

    def step(self, i):
        last = self.grid.z_n - 1
        if i <= last:
            self.collect(self.order[i])
        for j, t in enumerate(self.order):
            if 0 <= i - j < t:
                self.hop(t, 1, i == j, i - j)
            if 0 <= i - j < last - t:
                self.hop(t, -1, i == j, last - (i - j))

    def finish(self):
        grid = self.grid
        for t in range(grid.z_n):

            @pl.when(grid.z == t)
            def _(t=t):
                terms = [self.block(t, 0)]
                if t > 0:
                    arrived(self.from_z.at[t], self.sems[t, 1])
                    terms.append(self.from_z.at[t])
                if t < grid.z_n - 1:
                    arrived(self.from_z.at[grid.z_n], self.sems[t, -1])
                    terms.append(self.from_z.at[grid.z_n])
                accumulate(self.total, *terms)


class ShardScatter:
    def __init__(self, grid, copies, views, from_core, from_y):
        self.grid, self.copies, self.views = grid, copies, views
        self.from_core, self.from_y = from_core, from_y
        self.rounds = list(range(1, grid.y_n)) + [0]
        self.across = {
            k: [
                copies.send(part, from_core.at[k, i], fsdp=grid.yc(0, 1))
                for i, part in enumerate(views(grid.yc(k, 1)))
            ]
            for k in self.rounds
        }
        self.along_y = {}

    def step(self, k):
        for i, part in enumerate(self.views(self.grid.yc(k, 0))):
            arrived(self.from_core.at[k, i], self.across[k][i])
            accumulate(part, part, self.from_core.at[k, i])
            if k > 0:
                self.along_y[k, i] = self.copies.send(
                    part, self.from_y.at[k - 1, i], fsdp=self.grid.yc(k, 0)
                )

    def finish(self):
        for i, part in enumerate(self.views(self.grid.fsdp)):
            for k in range(1, self.grid.y_n):
                arrived(self.from_y.at[k - 1, i], self.along_y[k, i])
            accumulate(
                part, part, *[self.from_y.at[k - 1, i] for k in range(1, self.grid.y_n)]
            )


def to_sorted(row_ref, start, tile):
    length = row_ref.shape[1]
    place = lax.broadcasted_iota(jnp.int32, (tile, length), 0) + start
    return jnp.where(place == row_ref[0:1, :], 1.0, 0.0).astype(LOW)


def to_stored(row_ref, start, tile):
    length = row_ref.shape[1]
    place = lax.broadcasted_iota(jnp.int32, (length, tile), 0)
    return jnp.where(place == row_ref[0:1, pl.ds(start, tile)], 1.0, 0.0).astype(LOW)


def run_rows(i):
    return pl.ds(pl.multiple_of(i * RUN, RUN), RUN)


def attend_back(q_s, k_s, v_s, lse_s, g_s, dq_s, dk_s, dv_s):
    length = q_s.shape[0]
    dk_s[...] = jnp.zeros_like(dk_s)
    dv_s[...] = jnp.zeros_like(dv_s)
    tile = min(256, length)
    diagonal = lower_triangle(tile)
    for start in range(0, length, tile):
        rows, reach = slice(start, start + tile), start + tile

        @pl.loop(0, 2)
        def _(head, rows=rows, reach=reach, start=start):
            mine = head_lanes(tile, head)
            q_own, g_own = pick(mine, q_s[rows, :]), pick(mine, g_s[rows, :])
            lse = jnp.where(head == 0, lse_s[rows, 0:1], lse_s[rows, HEAD_DIM : HEAD_DIM + 1])
            scores = masked_tile(dot_nt(q_own, k_s[:reach, :]), diagonal, start)
            probs = jnp.exp(scores - lse)
            grad_probs = dot_nt(g_own, v_s[:reach, :])
            inner = jnp.sum(probs * grad_probs, axis=1, keepdims=True)
            grad_scores = (probs * (grad_probs - inner)).astype(LOW)
            grad_q = dot_nn(grad_scores, k_s[:reach, :]) * SCORE_SCALE
            dq_s[rows, :] = jnp.where(mine, grad_q, dq_s[rows, :])
            dk_s[:reach, :] += dot_tn(grad_scores, q_own)
            dv_s[:reach, :] += dot_tn(probs.astype(LOW), g_own)


def scatter_out_kernel(
    shape, hidden_in, wo_in, g_in, slope_in, qkv_in, lse_in,
    row_in, start_in, step_in,
    total_out, go_out, gup_out, gm_out,
    hidden_s, wo_s, g_s, slope_s, qkv_s, lse_s, po_s, po_x, po_z, po_sum,
    go_s, go_core, go_y, gup_s, gctx_s, gm_s, sorted_s, turned_s, dq_s, dk_s, dv_s, sems,
):
    grid = Grid(*shape).locate()
    copies = Copies(sems)
    length, fw = gup_s.shape
    dw = gctx_s.shape[1]
    width, cols = wo_s.shape
    pair = 2 * HEAD_DIM
    loads = [
        copies.local(src, dst)
        for src, dst in (
            (hidden_in, hidden_s), (wo_in, wo_s), (g_in, g_s),
            (slope_in, slope_s), (qkv_in, qkv_s), (lse_in, lse_s),
        )
    ]
    grid.greet()
    loads[0].wait()
    loads[1].wait()
    group = po_s.shape[1]
    tile = min(256, group)
    early, late = (
        TokenScatter(grid, copies, po_s, po_x, po_z, po_sum, half) for half in range(2)
    )
    unit = go_s.shape[2]
    block = grid.fsdp_n * unit
    part_n = grid.ctx_n // 2

    def make_out(first, count=1):
        @pl.loop(0, count * (group // tile) * (width // 256))
        def _(i):
            t, i = first - i // (group // tile * (width // 256)), i % (
                group // tile * (width // 256)
            )
            part = pl.multiple_of((i // (width // 256)) * tile, tile)
            at = pl.ds(pl.multiple_of((i % (width // 256)) * 256, 256), 256)
            rows = pl.ds(pl.multiple_of(t * group + part, tile), tile)
            result = dot_nt(hidden_s[rows, :], wo_s[at, :])
            po_s[t, pl.ds(part, tile), at] = result.astype(LOW)

        for t in range(first, first - count, -1):
            early.launch(t)

    def make_grad_out(part):
        @pl.loop(part * part_n, (part + 1) * part_n)
        def _(c):
            at = pl.ds(pl.multiple_of(c * block, block), block)
            result = dot_tn(g_s[:, at], hidden_s[...]).astype(LOW)
            go_s[c] = result.reshape(grid.fsdp_n, unit, cols)

        span = pl.ds(part * part_n, part_n)
        return ShardScatter(
            grid,
            copies,
            lambda f: [go_s.at[span, f]],
            go_core.at[:, :, span],
            go_y.at[:, :, span],
        )

    make_out(early.order[0])
    make_out(early.order[1])
    loads[2].wait()
    shards = [make_grad_out(0)]
    make_out(grid.z_n - 2, grid.z_n - 2)
    for t in late.order:
        late.launch(t)
    early.step(0)
    shards.append(make_grad_out(1))
    early.step(1)
    for k in shards[0].rounds:
        shards[0].step(k)
    early.step(2)
    for k in shards[1].rounds:
        shards[1].step(k)
    loads[3].wait()
    tall = min(256, length)

    @pl.loop(0, (length // tall) * (fw // 256))
    def _(i):
        rows = pl.ds(pl.multiple_of((i // (fw // 256)) * tall, tall), tall)
        at = pl.ds(pl.multiple_of((i % (fw // 256)) * 256, 256), 256)
        grad = dot_nn(g_s[rows, :], wo_s[:, at])
        gup_s[rows, at] = (grad * slope_s[rows, at].astype(F32)).astype(LOW)

    puts = [copies.local(gup_s, gup_out)]
    early.step(3)

    @pl.loop(0, length // tall)
    def _(i):
        rows = pl.ds(pl.multiple_of(i * tall, tall), tall)
        gctx_s[rows, :] = dot_nn(g_s[rows, :], wo_s[:, pl.ds(fw, dw)]).astype(LOW)

    early.step(grid.z_n)
    late.step(0)
    loads[4].wait()
    loads[5].wait()
    pairs = dw // pair

    @pl.loop(0, length // tall)
    def _(i):
        start = pl.multiple_of(i * tall, tall)
        result = dot_nn(to_sorted(row_in, start, tall), gctx_s[...]).astype(LOW)
        for p in range(pairs):
            sorted_s[p, pl.ds(start, tall), :] = result[:, p * pair : (p + 1) * pair]

    def attend_pairs(first, last):
        @pl.loop(first, last)
        def _(p):
            attend_back(
                qkv_s.at[0, p], qkv_s.at[1, p], qkv_s.at[2, p], lse_s.at[p],
                sorted_s.at[p], dq_s, dk_s, dv_s,
            )

            @pl.loop(0, length // RUN)
            def _(i):
                tables, rows = run_turn(start_in, step_in, i), run_rows(i)
                turned_s[0, p, rows, :] = turn(dq_s[rows, :], tables, -1.0).astype(LOW)
                turned_s[1, p, rows, :] = turn(dk_s[rows, :], tables, -1.0).astype(LOW)
                turned_s[2, p, rows, :] = dv_s[rows, :].astype(LOW)

    late.step(1)
    attend_pairs(0, (pairs + 1) // 2)
    late.step(2)
    late.step(3)
    for shard in shards:
        shard.finish()
    late.step(grid.z_n)
    if pairs > 1:
        attend_pairs((pairs + 1) // 2, pairs)
    puts.append(copies.local(go_s.at[:, grid.fsdp], go_out))

    @pl.loop(0, length // tall)
    def _(i):
        start = pl.multiple_of(i * tall, tall)
        back = to_stored(row_in, start, tall)
        for kind in range(3):
            for p in range(pairs):
                at = kind * dw + p * pair
                result = dot_tn(back, turned_s[kind, p])
                gm_s[pl.ds(start, tall), at : at + pair] = result.astype(LOW)

    puts.append(copies.local(gm_s, gm_out))
    early.finish()
    late.finish()
    puts.append(copies.local(po_sum, total_out))
    for put in puts:
        put.wait()
    copies.drain()


def scatter_in_kernel(
    shape, gm_in, wi_in, gup_in, wu_in, x_in, stats_in, normed_in, g_own_in, go_in,
    total_out, gu_out, gi_out, go_out, small_out,
    gm_s, wi_s, gup_s, wu_s, x_s, stats_s, normed_s, g_own_s, pn_s, pn_x, pn_z, pn_sum,
    gu_s, gu_core, gu_y, gi_s, gi_core, gi_y, gi_got, go_got,
    small_s, small_y, small_x, small_core, small_z, sems,
):
    grid = Grid(*shape).locate()
    copies = Copies(sems)
    length, fw = gup_s.shape
    width = wi_s.shape[1]
    dw = gm_s.shape[1] // 3
    unit = gi_got.shape[1]
    up_rows = fw // grid.fsdp_n
    loads = [
        copies.local(src, dst)
        for src, dst in (
            (gm_in, gm_s), (wi_in, wi_s), (gup_in, gup_s), (wu_in, wu_s),
            (x_in, x_s), (stats_in, stats_s), (normed_in, normed_s), (g_own_in, g_own_s),
        )
    ]
    grid.greet()
    peers = [(k, l) for k in range(grid.z_n) for l in range(grid.x_n) if k or l]
    own_o = copies.local(go_in.at[grid.ctx], go_got.at[grid.ctx])
    out_sems = [
        copies.send(go_in.at[grid.zx(k, l)], go_got.at[grid.ctx], ctx=grid.zx(k, l))
        for k, l in peers
    ]
    small_s[0] = jnp.zeros_like(small_s[0])
    for load in loads[:6]:
        load.wait()
    group = pn_s.shape[1]
    tile = min(256, group)
    early, late = (
        TokenScatter(grid, copies, pn_s, pn_x, pn_z, pn_sum, half) for half in range(2)
    )

    def make_normed(first, count=1):
        @pl.loop(0, count * (group // tile) * (width // 256))
        def _(i):
            t, i = first - i // (group // tile * (width // 256)), i % (
                group // tile * (width // 256)
            )
            part = pl.multiple_of((i // (width // 256)) * tile, tile)
            at = pl.ds(pl.multiple_of((i % (width // 256)) * 256, 256), 256)
            rows = pl.ds(pl.multiple_of(t * group + part, tile), tile)
            grad = dot_nn(gm_s[rows, :], wi_s[:, at]) + dot_nn(gup_s[rows, :], wu_s[:, at])
            pn_s[t, pl.ds(part, tile), at] = grad.astype(LOW)
            mean, spread = stats_s[rows, 0:1], stats_s[rows, HEAD_DIM : HEAD_DIM + 1]
            xhat = (x_s[rows, at].astype(F32) - mean) * spread
            small_s[0, 0:1, at] += jnp.sum(grad * xhat, axis=0, keepdims=True)
            small_s[0, 1:2, at] += jnp.sum(grad, axis=0, keepdims=True)

        for t in range(first, first - count, -1):
            early.launch(t)

    make_normed(early.order[0])
    make_normed(early.order[1])
    for load in loads[6:]:
        load.wait()

    span = width // 2

    @pl.loop(0, 3 * 2)
    def _(i):
        at = pl.ds(pl.multiple_of((i // 2) * dw, dw), dw)
        cols = pl.ds(pl.multiple_of((i % 2) * span, span), span)
        gi_s[at, cols] = dot_tn(gm_s[:, at], normed_s[:, cols]).astype(LOW)

    def piece_slot(f, m):
        kind, place = grid.qkv_piece(grid.ctx, f, m)
        return gi_s.at[pl.ds(pl.multiple_of((kind * grid.fsdp_n + place) * unit, unit), unit)]

    shards_i = ShardScatter(
        grid, copies, lambda f: [piece_slot(f, m) for m in range(3)], gi_core, gi_y
    )
    make_normed(grid.z_n - 2, grid.z_n - 2)
    for t in late.order:
        late.launch(t)

    small_s[0, 2:3, :] = jnp.sum(g_own_s[...].astype(F32), axis=0, keepdims=True)
    for kind in range(3):
        at = pl.ds(pl.multiple_of(grid.ctx * dw, 128), dw)
        terms = gm_s[:, kind * dw : (kind + 1) * dw].astype(F32)
        small_s[0, 4 + kind : 5 + kind, at] = jnp.sum(terms, axis=0, keepdims=True)
    offset = grid.ctx * fw
    at = pl.ds(pl.multiple_of(offset % width, 128), fw)
    terms = jnp.sum(gup_s[...].astype(F32), axis=0, keepdims=True)
    for row in range(4):
        small_s[0, 7 + row : 8 + row, at] = jnp.where(offset // width == row, terms, 0.0)

    def small_sum(step, buffer, stage):
        for i, sem in enumerate(stage):
            arrived(buffer.at[i], sem)
        accumulate(
            small_s.at[step + 1], small_s.at[step], *[buffer.at[i] for i in range(len(stage))]
        )

    stage = [
        copies.send(small_s.at[0], small_y.at[k - 1], fsdp=grid.yc(k, 0))
        for k in range(1, grid.y_n)
    ]

    def up_slot(f):
        return gu_s.at[pl.ds(pl.multiple_of(f * up_rows, up_rows), up_rows)]

    early.step(0)
    for k in shards_i.rounds:
        shards_i.step(k)
    early.step(1)

    @pl.loop(0, fw // 256 * 2)
    def _(i):
        at = pl.ds(pl.multiple_of((i // 2) * 256, 256), 256)
        cols = pl.ds(pl.multiple_of((i % 2) * span, span), span)
        gu_s[at, cols] = dot_tn(gup_s[:, at], normed_s[:, cols]).astype(LOW)

    shards_u = ShardScatter(grid, copies, lambda f: [up_slot(f)], gu_core, gu_y)
    early.step(2)
    small_sum(0, small_y, stage)
    stage = [
        copies.send(small_s.at[1], small_core.at[c - 1], fsdp=grid.yc(0, c))
        for c in range(1, grid.core_n)
    ]
    for k in shards_u.rounds:
        shards_u.step(k)
    early.step(3)
    early.step(grid.z_n)
    late.step(0)
    late.step(1)
    shards_i.finish()
    qkv_sems = []
    for m in range(3):
        owner = grid.qkv_owner(grid.ctx, grid.fsdp, m)
        qkv_sems.append(
            copies.send_or_keep(piece_slot(grid.fsdp, m), gi_got.at[m], owner, grid.ctx)
        )
    small_sum(1, small_core, stage)
    stage = [
        copies.send(small_s.at[2], small_x.at[l - 1], ctx=grid.zx(0, l))
        for l in range(1, grid.x_n)
    ]
    late.step(2)
    late.step(3)
    small_sum(2, small_x, stage)
    stage = [
        copies.send(small_s.at[3], small_z.at[k - 1], ctx=grid.zx(k, 0))
        for k in range(1, grid.z_n)
    ]
    shards_u.finish()
    puts = [copies.local(up_slot(grid.fsdp), gu_out)]
    late.step(grid.z_n)
    early.finish()
    late.finish()
    puts.append(copies.local(pn_sum, total_out))
    own_o.wait()
    for (k, l), sem in zip(peers, out_sems):
        arrived(go_got.at[grid.zx(-k, -l)], sem)
    puts.append(copies.local(go_got, go_out))
    for m in range(3):
        arrived(gi_got.at[m], qkv_sems[m])
    puts.append(copies.local(gi_got, gi_out))
    small_sum(3, small_z, stage)
    puts.append(copies.local(small_s.at[4], small_out))
    for put in puts:
        put.wait()
    copies.drain()


def solution(mesh):
    shape = mesh.shape["ctx"], mesh.shape["fsdp"]
    ctx_n, fsdp_n = shape
    n = ctx_n * fsdp_n
    plan = Grid(*shape)
    x_n, z_n, core_n, y_n = plan.x_n, plan.z_n, plan.core_n, plan.y_n

    def gather(x_own, g_own, w_qkv, w_fc1, w_fc2, w_dense, small, tables):
        local_len, width = x_own.shape
        unit, hidden_units = w_fc2.shape
        length = ctx_n * local_len
        fw, dw = hidden_units // ctx_n, width // ctx_n
        pair = 2 * HEAD_DIM
        small_rows = jax.ShapeDtypeStruct((16, width), LOW)
        kept = [
            jax.ShapeDtypeStruct((length, width), LOW),
            jax.ShapeDtypeStruct((length, width), LOW),
            jax.ShapeDtypeStruct((3 * fsdp_n * unit, width), LOW),
            jax.ShapeDtypeStruct((fw, width), LOW),
            jax.ShapeDtypeStruct((ctx_n, fsdp_n, unit, fw + dw), LOW),
        ]
        made = [
            jax.ShapeDtypeStruct((length, width), LOW),
            jax.ShapeDtypeStruct((length, fw + dw), LOW),
            jax.ShapeDtypeStruct((length, fw), LOW),
            jax.ShapeDtypeStruct((3, dw // pair, length, pair), LOW),
            jax.ShapeDtypeStruct((dw // pair, length, pair), F32),
            jax.ShapeDtypeStruct((length, pair), F32),
        ]
        return pl.pallas_call(
            functools.partial(gather_kernel, shape),
            out_shape=kept + [small_rows] + made,
            in_specs=[anywhere] * 6 + [inside] * 9,
            out_specs=[anywhere] * 12,
            scratch_shapes=[pltpu.VMEM(s.shape, s.dtype) for s in kept + made]
            + [pltpu.VMEM((length, 3 * dw), LOW), pltpu.VMEM((dw // pair, length, pair), LOW)]
            + [pltpu.VMEM((16, width), F32), pltpu.VMEM((3, 8, dw), F32)]
            + [pltpu.VMEM((max(fw // 256, 1), 8, min(fw, 256)), F32)]
            + [pltpu.VMEM((count, 16, width), LOW) for count in (5, x_n, core_n, y_n, z_n)]
            + [pltpu.SemaphoreType.DMA((SEMAPHORES,))],
            compiler_params=pltpu.CompilerParams(
                collective_id=0, has_side_effects=True, vmem_limit_bytes=VMEM_BYTES
            ),
            name="gather",
        )(x_own, g_own, w_qkv, w_fc1, w_fc2, w_dense, *small, *tables)

    def token_scratch(local_len, width):
        return [
            pltpu.VMEM((z_n, x_n * local_len, width), LOW),
            pltpu.VMEM((z_n, max(x_n - 1, 1), local_len, width), LOW),
            pltpu.VMEM((z_n + 1, local_len, width), LOW),
            pltpu.VMEM((local_len, width), F32),
        ]

    def shard_scratch(parts, *block):
        return [
            pltpu.VMEM((y_n, parts) + block, LOW),
            pltpu.VMEM((max(y_n - 1, 1), parts) + block, LOW),
        ]

    def inside_like(*arrays):
        return [pltpu.VMEM(a.shape, a.dtype) for a in arrays]

    anywhere = pl.BlockSpec(memory_space=pl.ANY)
    inside = pl.BlockSpec(memory_space=pltpu.VMEM)

    def scatter_out(hidden, wo, g_all, slope, qkv, lse, tables):
        length, cols = hidden.shape
        local_len, width = length // ctx_n, g_all.shape[1]
        unit = width // n
        fw = slope.shape[1]
        dw, pair = cols - fw, 2 * HEAD_DIM
        return pl.pallas_call(
            functools.partial(scatter_out_kernel, shape),
            out_shape=[
                jax.ShapeDtypeStruct((local_len, width), F32),
                jax.ShapeDtypeStruct((ctx_n, unit, cols), LOW),
                jax.ShapeDtypeStruct((length, fw), LOW),
                jax.ShapeDtypeStruct((length, 3 * dw), LOW),
            ],
            in_specs=[anywhere] * 6 + [inside] * 3,
            out_specs=[anywhere] * 4,
            scratch_shapes=inside_like(hidden, wo, g_all, slope, qkv, lse)
            + token_scratch(local_len, width)
            + [pltpu.VMEM((ctx_n, fsdp_n, unit, cols), LOW)]
            + shard_scratch(1, ctx_n, unit, cols)
            + [pltpu.VMEM((length, c), LOW) for c in (fw, dw, 3 * dw)]
            + [pltpu.VMEM((dw // pair, length, pair), LOW)]
            + inside_like(qkv)
            + [pltpu.VMEM((length, pair), F32)] * 3
            + [pltpu.SemaphoreType.DMA((SEMAPHORES,))],
            compiler_params=pltpu.CompilerParams(
                collective_id=1, has_side_effects=True, vmem_limit_bytes=VMEM_BYTES
            ),
            name="scatter_out",
        )(hidden, wo, g_all, slope, qkv, lse, *tables)

    def scatter_in(gm, wi, gup, wu, x_all, stats, normed, g_own, go):
        length, width = normed.shape
        local_len = length // ctx_n
        unit, up_rows = width // n, wu.shape[0] // fsdp_n
        return pl.pallas_call(
            functools.partial(scatter_in_kernel, shape),
            out_shape=[
                jax.ShapeDtypeStruct((local_len, width), F32),
                jax.ShapeDtypeStruct((up_rows, width), LOW),
                jax.ShapeDtypeStruct((3, unit, width), LOW),
                jax.ShapeDtypeStruct(go.shape, LOW),
                jax.ShapeDtypeStruct((16, width), F32),
            ],
            in_specs=[anywhere] * 9,
            out_specs=[anywhere] * 5,
            scratch_shapes=inside_like(gm, wi, gup, wu, x_all, stats, normed, g_own)
            + token_scratch(local_len, width)
            + inside_like(wu)
            + shard_scratch(1, up_rows, width)
            + inside_like(wi)
            + shard_scratch(3, unit, width)
            + [pltpu.VMEM((3, unit, width), LOW)]
            + inside_like(go)
            + [pltpu.VMEM((count, 16, width), F32) for count in (5, y_n, x_n, core_n, z_n)]
            + [pltpu.SemaphoreType.DMA((SEMAPHORES,))],
            compiler_params=pltpu.CompilerParams(
                collective_id=2, has_side_effects=True, vmem_limit_bytes=VMEM_BYTES
            ),
            name="scatter_in",
        )(gm, wi, gup, wu, x_all, stats, normed, g_own, go)

    def body(
        hidden_in, positions, ln_gain, ln_bias, w_qkv, b_qkv, w_dense, b_dense,
        w_fc1, b_fc1, w_fc2, b_fc2, out_grad,
    ):
        local_len, width = hidden_in.shape[1:]
        hidden_units = w_fc2.shape[1]
        unit = w_dense.shape[0]
        up_rows = w_fc1.shape[0]
        fw, dw = hidden_units // ctx_n, width // ctx_n
        my_ctx = lax.axis_index("ctx")
        me = my_ctx * fsdp_n + lax.axis_index("fsdp")
        length = positions.shape[1]
        x_own, g_own = hidden_in[0], out_grad[0]

        rank = positions[0, ::RUN] // RUN
        starts, steps = turning_tables(length)
        ranks = jnp.arange(length // RUN, dtype=jnp.int32)
        chosen = (rank[:, None] == ranks[None, :])[None, :, :, None]
        stored_starts = jnp.sum(jnp.where(chosen, starts[:, None], 0.0), axis=2)

        own_small = [
            a.reshape(-1, unit) for a in (ln_gain, ln_bias, b_dense, b_fc2, b_qkv, b_fc1)
        ]
        x_all, g_all, wi, wu, wo, small, normed, hidden, slope, qkv, lse, stats = gather(
            x_own, g_own, w_qkv, w_fc1, w_fc2, w_dense, own_small, (positions, stored_starts, steps)
        )
        small = small.astype(F32)
        gain, bias_dense, bias_down = small[0], small[2], small[3]
        total, grad_o, grad_upward, grad_mixed = scatter_out(
            hidden, wo.reshape(width, fw + dw), g_all, slope, qkv, lse, (positions, starts, steps)
        )
        grad_normed, grad_up, grad_qkv, grad_o, sums = scatter_in(
            grad_mixed, wi, grad_upward, wu, x_all, stats, normed, g_own, grad_o
        )

        def standardize(values):
            wide = values.astype(F32)
            centered = wide - jnp.mean(wide, axis=-1, keepdims=True)
            spread = lax.rsqrt(jnp.mean(centered * centered, axis=-1, keepdims=True) + EPSILON)
            return centered * spread, spread

        hidden_out = (total + x_own.astype(F32) + bias_dense + bias_down).astype(LOW)
        xhat, spread = standardize(x_own)
        e = grad_normed * gain
        grad_in = (
            e - jnp.mean(e, axis=-1, keepdims=True)
            - xhat * jnp.mean(e * xhat, axis=-1, keepdims=True)
        ) * spread + g_own.astype(F32)
        grad_o = grad_o.transpose(1, 0, 2).astype(F32)
        sums = sums.reshape(-1)

        def own_slice(row, size):
            return lax.dynamic_slice_in_dim(sums, row * width + me * size, size)

        grad_b_out = own_slice(2, unit)
        return (
            hidden_out[None],
            grad_in[None],
            own_slice(0, unit),
            own_slice(1, unit),
            grad_qkv.reshape(3 * unit, width).astype(F32),
            own_slice(4, 3 * unit),
            grad_o[:, :, fw:].reshape(unit, width),
            grad_b_out,
            grad_up.astype(F32),
            own_slice(7, up_rows),
            grad_o[:, :, :fw].reshape(unit, hidden_units),
            grad_b_out,
        )

    tokens, rows, cells = P("fsdp", "ctx", None), P(BOTH, None), P(BOTH)
    return jax.shard_map(
        body,
        mesh=mesh,
        in_specs=(
            tokens, P("fsdp", None), cells, cells, rows, cells, rows, cells,
            rows, cells, rows, cells, tokens,
        ),
        out_specs=(
            tokens, tokens, cells, cells, rows, cells, rows, cells, rows, cells, rows, cells,
        ),
        check_vma=False,
    )
```

```python
import functools

import jax
import jax.numpy as jnp
import numpy as np
from jax import lax
from jax.experimental import pallas as pl
from jax.experimental.pallas import tpu as pltpu
from jax.sharding import PartitionSpec as P

HEAD_DIM = 64
ROT_DIM = 32
RUN = 64
EPSILON = 1e-05
SCORE_SCALE = 0.125
BOTH = ("ctx", "fsdp")
F32 = jnp.float32
LOW = jnp.bfloat16
MESH = pl.DeviceIdType.MESH
SEMAPHORES = 512
VMEM_BYTES = 60 * 1024 * 1024
SMALL_ROWS = (
    [(row, (1, 0)) for row in range(4)]
    + [(4, (3, j)) for j in range(3)]
    + [(7, (4, j)) for j in range(4)]
)


def dot_nt(a, b):
    return lax.dot_general(a, b, (((1,), (1,)), ((), ())), preferred_element_type=F32)


def dot_nn(a, b):
    return lax.dot_general(a, b, (((1,), (0,)), ((), ())), preferred_element_type=F32)


def dot_tn(a, b):
    return lax.dot_general(a, b, (((0,), (0,)), ((), ())), preferred_element_type=F32)


def turning_tables(length):
    half_rot = ROT_DIM // 2
    lane = np.arange(2 * HEAD_DIM) % HEAD_DIM
    freqs = np.where(lane < ROT_DIM, 10000.0 ** (-(lane % half_rot) / half_rot), 0.0)
    starts = np.arange(0, length, RUN)[:, None] * freqs[None, :]
    steps = np.arange(RUN)[:, None] * freqs[None, :]
    return (
        np.stack([np.cos(starts), np.sin(starts)]).astype(np.float32),
        np.stack([np.cos(steps), np.sin(steps)]).astype(np.float32),
    )


def run_turn(start_ref, step_ref, run):
    lane = lax.broadcasted_iota(jnp.int32, (RUN, 2 * HEAD_DIM), 1) % HEAD_DIM
    half_rot = ROT_DIM // 2
    cos_a, sin_a = start_ref[0, pl.ds(run, 1), :], start_ref[1, pl.ds(run, 1), :]
    cos_b, sin_b = step_ref[0], step_ref[1]
    cosine = cos_a * cos_b - sin_a * sin_b
    sine = sin_a * cos_b + cos_a * sin_b
    above = jnp.where(lane < half_rot, -sine, 0.0)
    below = jnp.where((lane >= half_rot) & (lane < ROT_DIM), sine, 0.0)
    return cosine, above, below


def turn(u, tables, way=1.0):
    cosine, above, below = tables
    half_rot = ROT_DIM // 2
    width = 2 * HEAD_DIM
    moved = pltpu.roll(u, width - half_rot, 1) * above + pltpu.roll(u, half_rot, 1) * below
    return u * cosine + way * moved


def masked_tile(scores, diagonal, start):
    last = jnp.where(diagonal, scores[:, start:], -1e30)
    return jnp.concatenate([scores[:, :start], last], axis=1) if start > 0 else last


def lower_triangle(tile):
    return lax.broadcasted_iota(jnp.int32, (tile, tile), 1) <= lax.broadcasted_iota(
        jnp.int32, (tile, tile), 0
    )


def head_lanes(tile, head):
    lanes = lax.broadcasted_iota(jnp.int32, (tile, 2 * HEAD_DIM), 1)
    return (lanes // HEAD_DIM) == head


def pick(mine, values):
    return jnp.where(mine, values, jnp.zeros_like(values))


def attend(q_s, k_s, v_s, ctx_s, lse_s):
    length = q_s.shape[0]
    tile = min(256, length)
    diagonal = lower_triangle(tile)
    for start in range(0, length, tile):
        rows, reach = slice(start, start + tile), start + tile

        for head in range(2):
            mine = head_lanes(tile, head)
            scores = dot_nt(pick(mine, q_s[rows, :]), k_s[:reach, :])
            scores = masked_tile(scores, diagonal, start)
            peak = jnp.max(scores, axis=1, keepdims=True)
            exps = jnp.exp(scores - peak)
            total = jnp.sum(exps, axis=1, keepdims=True)
            probs_low = (exps * (1.0 / total)).astype(LOW)
            context = dot_nn(probs_low, v_s[:reach, :]).astype(LOW)
            ctx_s[rows, :] = jnp.where(mine, context, ctx_s[rows, :])
            lse_s[rows, :] = jnp.where(mine, peak + jnp.log(total), lse_s[rows, :])


class Grid:
    def __init__(self, ctx_n, fsdp_n):
        self.ctx_n, self.fsdp_n = ctx_n, fsdp_n
        self.x_n = 1 << ((ctx_n.bit_length() - 1) // 2)
        self.z_n = ctx_n // self.x_n
        self.core_n = 2 if fsdp_n % 2 == 0 else 1
        self.y_n = fsdp_n // self.core_n
        self.undo = 1 if ctx_n % 3 == 1 else 2

    def locate(self):
        self.ctx, self.fsdp = lax.axis_index("ctx"), lax.axis_index("fsdp")
        self.z, self.x = self.ctx // self.x_n, self.ctx % self.x_n
        self.y, self.core = self.fsdp // self.core_n, self.fsdp % self.core_n
        return self

    def zx(self, dz, dx):
        return ((self.z + dz + self.z_n) % self.z_n) * self.x_n + (
            self.x + dx + self.x_n
        ) % self.x_n

    def yc(self, dy, dc):
        return ((self.y + dy + self.y_n) % self.y_n) * self.core_n + (
            self.core + dc + self.core_n
        ) % self.core_n

    def nearest(self, j):
        place = 0
        for z in range(self.z_n):
            order = sorted(range(self.z_n), key=lambda other: (abs(other - z), other))
            place = place + jnp.where(self.z == z, order[j], 0)
        return place

    def qkv_piece(self, ctx, fsdp, m):
        span = 3 * self.fsdp_n
        v = (3 * fsdp + m + span * self.ctx_n - ctx * self.fsdp_n) % span
        return ((v // self.fsdp_n) * self.undo) % 3, v % self.fsdp_n

    def qkv_owner(self, ctx, fsdp, m):
        kind, place = self.qkv_piece(ctx, fsdp, m)
        piece = self.ctx_n * self.fsdp_n * kind + ctx * self.fsdp_n + place
        return piece // 3 // self.fsdp_n

    def qkv_user(self, ctx, fsdp, m):
        piece = 3 * (ctx * self.fsdp_n + fsdp) + m
        return (piece % (self.ctx_n * self.fsdp_n)) // self.fsdp_n

    def greet(self):
        barrier = pltpu.get_barrier_semaphore()
        for k in range(1, self.ctx_n):
            pl.semaphore_signal(
                barrier, inc=1, device_id={"ctx": (self.ctx + k) % self.ctx_n}, device_id_type=MESH
            )
        for k in range(1, self.fsdp_n):
            pl.semaphore_signal(
                barrier,
                inc=1,
                device_id={"fsdp": (self.fsdp + k) % self.fsdp_n},
                device_id_type=MESH,
            )
        pl.semaphore_wait(barrier, self.ctx_n + self.fsdp_n - 2)


class Copies:
    def __init__(self, sems):
        self.sems, self.used, self.sent, self.perhaps = sems, 0, [], []

    def sem(self):
        self.used += 1
        return self.sems.at[self.used - 1]

    def send(self, src, dst, **where):
        send_sem, recv_sem = self.sem(), self.sem()
        copy = pltpu.make_async_remote_copy(
            src_ref=src,
            dst_ref=dst,
            send_sem=send_sem,
            recv_sem=recv_sem,
            device_id=where,
            device_id_type=MESH,
        )
        copy.start()
        self.sent.append(copy)
        return recv_sem

    def send_or_keep(self, src, dst, ctx, own_ctx):
        send_sem, recv_sem = self.sem(), self.sem()
        remote = pltpu.make_async_remote_copy(
            src_ref=src,
            dst_ref=dst,
            send_sem=send_sem,
            recv_sem=recv_sem,
            device_id={"ctx": ctx},
            device_id_type=MESH,
        )

        @pl.when(ctx != own_ctx)
        def _():
            remote.start()

        @pl.when(ctx == own_ctx)
        def _():
            pltpu.make_async_copy(src, dst, recv_sem).start()

        self.perhaps.append((ctx != own_ctx, remote))
        return recv_sem

    def prepare(self, src, dst, **where):
        send_sem, recv_sem = self.sem(), self.sem()
        remote = pltpu.make_async_remote_copy(
            src_ref=src,
            dst_ref=dst,
            send_sem=send_sem,
            recv_sem=recv_sem,
            device_id=where,
            device_id_type=MESH,
        )
        return remote, recv_sem

    def start_if(self, when, remote):
        @pl.when(when)
        def _():
            remote.start()

        self.perhaps.append((when, remote))

    def send_if(self, when, src, dst, **where):
        remote, recv_sem = self.prepare(src, dst, **where)
        self.start_if(when, remote)
        return recv_sem

    def local(self, src, dst):
        copy = pltpu.make_async_copy(src, dst, self.sem())
        copy.start()
        return copy

    def drain(self):
        for copy in self.sent:
            copy.wait_send()
        for sent, copy in self.perhaps:

            @pl.when(sent)
            def _(copy=copy):
                copy.wait_send()


def arrived(ref, sem):
    pltpu.make_async_copy(ref, ref, sem).wait()


class TokenGather:
    def __init__(self, grid, copies, own, buffer):
        self.grid, self.copies, self.buffer = grid, copies, buffer
        self.rows = own.shape[0]
        self.across = []
        self.kept = copies.local(own, self.slot(0, 0))
        self.along = {
            way: copies.send_if(self.ends(way), own, self.slot(0, 0), ctx=grid.zx(way, 0))
            for way in (1, -1)
        }
        for l in range(1, grid.x_n):
            sem = copies.send(own, self.slot(0, 0), ctx=grid.zx(0, l))
            self.across.append((0, 1, l, sem))

    def slot(self, k, l):
        start = pl.multiple_of(self.grid.zx(-k, -l) * self.rows, self.rows)
        return self.buffer.at[pl.ds(start, self.rows)]

    def ends(self, way):
        return self.grid.z < self.grid.z_n - 1 if way > 0 else self.grid.z > 0

    def has(self, k, way):
        z = self.grid.z
        return z >= k if way > 0 else z + k < self.grid.z_n

    def step(self, k):
        grid, copies, along = self.grid, self.copies, {}
        for way in (1, -1):
            slot, here = self.slot(k * way, 0), self.has(k, way)

            @pl.when(here)
            def _(slot=slot, way=way):
                arrived(slot, self.along[way])

            if k < grid.z_n - 1:
                along[way] = copies.send_if(
                    here & self.ends(way), slot, slot, ctx=grid.zx(way, 0)
                )
            for l in range(1, grid.x_n):
                sem = copies.send_if(here, slot, slot, ctx=grid.zx(0, l))
                self.across.append((k, way, l, sem))
        self.along = along

    def ready(self, k):
        if k == 0:
            self.kept.wait()
        for m, way, l, sem in self.across:
            if m == k:

                @pl.when(self.has(k, way))
                def _(way=way, l=l, sem=sem):
                    arrived(self.slot(k * way, l), sem)


class ShardGather:
    def __init__(self, grid, copies, own, view):
        self.grid, self.copies, self.view = grid, copies, view
        self.along_y = [
            copies.send(own, view(grid.fsdp), fsdp=grid.yc(k, 0)) for k in range(1, grid.y_n)
        ]
        self.across = []
        self.cross(own, 0)

    def cross(self, src, k):
        for c in range(1, self.grid.core_n):
            slot = self.view(self.grid.yc(-k, 0))
            self.across.append((k, c, self.copies.send(src, slot, fsdp=self.grid.yc(0, c))))

    def forward(self):
        for k in range(1, self.grid.y_n):
            slot = self.view(self.grid.yc(-k, 0))
            arrived(slot, self.along_y[k - 1])
            self.cross(slot, k)

    def finish(self):
        for k, c, sem in self.across:
            arrived(self.view(self.grid.yc(-k, -c)), sem)


def gather_kernel(
    shape, x_in, g_in, wq_in, wu_in, wf_in, wd_in,
    gain_in, shift_in, bd_in, bf_in, bq_in, bu_in, row_in, start_in, step_in,
    x_out, g_out, wi_out, wu_out, wo_out, small_out, normed_out, hidden_out, slope_out,
    qkv_out, lse_out, stats_out,
    x_s, g_s, wi_s, wu_s, wo_s, normed_s, hidden_s, slope_s, qkv_s, lse_s, stats_s,
    mixed_s, ctx_s, small_f, qkv_bias_s, up_bias_s, small_s, small_x, small_core, small_y, small_z, sems,
):
    grid = Grid(*shape).locate()
    copies = Copies(sems)
    local_len, width = x_in.shape
    unit, up_rows = wd_in.shape[0], wu_in.shape[0]
    fw, dw = wf_in.shape[1] // grid.ctx_n, wd_in.shape[1] // grid.ctx_n
    n = grid.ctx_n * grid.fsdp_n
    me = grid.ctx * grid.fsdp_n + grid.fsdp
    peers = [(k, l) for k in range(grid.z_n) for l in range(grid.x_n) if k or l]
    pairs = dw // (2 * HEAD_DIM)
    small_in = gain_in, shift_in, bd_in, bf_in, bq_in, bu_in
    puts = []

    row_index = lax.broadcasted_iota(jnp.int32, (16, width), 0)
    placed = jnp.zeros((16, width), F32)
    small_f[...] = jnp.zeros_like(small_f)
    row = 0
    for piece_in in small_in:
        small_f[row : row + piece_in.shape[0], 0:unit] = piece_in[...].astype(F32)
        row += piece_in.shape[0]
    pieces_in = small_f[...]
    for row, (base, each) in enumerate(SMALL_ROWS):
        piece = each[0] * me + each[1]
        value = jnp.broadcast_to(pieces_in[row : row + 1, :], (16, width))
        value = pltpu.roll(value, (piece % n) * unit, 1)
        placed = placed + jnp.where(row_index == piece // n + base, value, 0.0)
    small_s[0] = placed.astype(LOW)
    grid.greet()

    def small_sum(step, buffer, stage):
        for i, sem in enumerate(stage):
            arrived(buffer.at[i], sem)
        accumulate(
            small_s.at[step + 1], small_s.at[step], *[buffer.at[i] for i in range(len(stage))]
        )

    stage = [
        copies.send(small_s.at[0], small_y.at[k - 1], fsdp=grid.yc(k, 0))
        for k in range(1, grid.y_n)
    ]

    def up_slot(f):
        return wu_s.at[pl.ds(pl.multiple_of(f * up_rows, up_rows), up_rows)]

    up_kept = copies.local(wu_in, up_slot(grid.fsdp))
    up = ShardGather(grid, copies, wu_in, up_slot)
    qkv_sems = []

    def piece_slot(ctx, fsdp, m):
        kind, place = grid.qkv_piece(ctx, fsdp, m)
        return wi_s.at[pl.ds(pl.multiple_of((kind * grid.fsdp_n + place) * unit, unit), unit)]

    for m in range(3):
        user = grid.qkv_user(grid.ctx, grid.fsdp, m)
        qkv_sems.append(
            copies.send_or_keep(
                wq_in.at[pl.ds(m * unit, unit)],
                piece_slot(user, grid.fsdp, m),
                user,
                grid.ctx,
            )
        )
    small_sum(0, small_y, stage)
    stage = [
        copies.send(small_s.at[1], small_x.at[l - 1], ctx=grid.zx(0, l))
        for l in range(1, grid.x_n)
    ]
    tokens_x = TokenGather(grid, copies, x_in, x_s)
    small_sum(1, small_x, stage)
    stage = [
        copies.send(small_s.at[2], small_core.at[c - 1], fsdp=grid.yc(0, c))
        for c in range(1, grid.core_n)
    ]
    small_sum(2, small_core, stage)
    stage = [
        copies.send(small_s.at[3], small_z.at[k - 1], ctx=grid.zx(k, 0))
        for k in range(1, grid.z_n)
    ]

    def column_block(ref, index, block):
        return ref.at[:, pl.ds(pl.multiple_of(index * block, 128), block)]

    mine = wo_s.at[grid.ctx, grid.fsdp]
    own_out = [
        copies.local(column_block(wf_in, grid.ctx, fw), mine.at[:, pl.ds(0, fw)]),
        copies.local(column_block(wd_in, grid.ctx, dw), mine.at[:, pl.ds(fw, dw)]),
    ]
    out_sems = {}

    def send_out(k):
        for l in range(grid.x_n):
            if k or l:
                target = grid.zx(k, l)
                out_sems[k, l] = (
                    copies.send(
                        column_block(wf_in, target, fw), mine.at[:, pl.ds(0, fw)], ctx=target
                    ),
                    copies.send(
                        column_block(wd_in, target, dw), mine.at[:, pl.ds(fw, dw)], ctx=target
                    ),
                )

    shards = []

    def spread_out(k):
        first = ((grid.z - k + grid.z_n) % grid.z_n) * grid.x_n
        for l in range(grid.x_n):
            slot = wo_s.at[grid.zx(-k, -l), grid.fsdp]
            if k or l:
                arrived(slot.at[:, pl.ds(0, fw)], out_sems[k, l][0])
                arrived(slot.at[:, pl.ds(fw, dw)], out_sems[k, l][1])
            else:
                own_out[0].wait()
                own_out[1].wait()

        def out_view(f):
            return wo_s.at[pl.ds(first, grid.x_n), f]

        shards.append(ShardGather(grid, copies, out_view(grid.fsdp), out_view))

    group = grid.x_n * local_len

    def group_rows(first, i, parts):
        place = grid.nearest(first)
        for later in range(first + 1, min(first + 2, grid.z_n)):
            place = jnp.where(i // parts == later - first, grid.nearest(later), place)
        return pl.multiple_of(place * group + (i % parts) * tile_rows, tile_rows)

    def normalize(k):
        first = pl.multiple_of(grid.nearest(k) * group, group)
        gain, shift = small_f[0:1, :], small_f[1:2, :]

        @pl.loop(0, group // 16)
        def _(i):
            rows = pl.ds(pl.multiple_of(first + i * 16, 16), 16)
            wide = x_s[rows, :].astype(F32)
            mean = jnp.mean(wide, axis=-1, keepdims=True)
            centered = wide - mean
            spread = lax.rsqrt(jnp.mean(centered * centered, axis=-1, keepdims=True) + EPSILON)
            normed_s[rows, :] = (centered * spread * gain + shift).astype(LOW)
            lane = lax.broadcasted_iota(jnp.int32, (16, 2 * HEAD_DIM), 1)
            stats_s[rows, :] = jnp.where(lane < HEAD_DIM, mean, spread)

    tile_rows = min(256, group)

    tiles = group // tile_rows

    def project_up(k, groups=1):
        block = min(256, fw)

        @pl.loop(0, groups * tiles * (fw // block))
        def _(i):
            col = (i % (fw // block)) * block
            rows = pl.ds(group_rows(k, i // (fw // block), tiles), tile_rows)
            cols = pl.ds(pl.multiple_of(col, block), block)
            bias = up_bias_s[i % (fw // block), 0:1, :]
            upward = dot_nt(normed_s[rows, :], wu_s[cols, :]) + bias
            square = upward * upward
            bend = jnp.tanh(0.7978845608028654 * (upward + 0.044715 * square * upward))
            half = 0.5 * (1.0 + bend)
            hidden_s[rows, cols] = (upward * half).astype(LOW)
            inner_slope = 0.7978845608028654 * (1.0 + 3.0 * 0.044715 * square)
            slope = half + 0.5 * upward * (1.0 - bend * bend) * inner_slope
            slope_s[rows, cols] = slope.astype(LOW)

    def project_qkv(k, groups=1):
        @pl.loop(0, groups * tiles)
        def _(i):
            start = group_rows(k, i, tiles)
            rows = pl.ds(start, tile_rows)
            for kind in range(3):
                result = dot_nt(normed_s[rows, :], wi_s[kind * dw : (kind + 1) * dw, :])
                result = result + qkv_bias_s[kind, 0:1, :]
                if kind == 2:
                    mixed_s[rows, kind * dw : (kind + 1) * dw] = result.astype(LOW)
                    continue
                for run in range(tile_rows // RUN):
                    tables = run_turn(start_in, step_in, start // RUN + run)
                    run_at = pl.ds(pl.multiple_of(start + run * RUN, RUN), RUN)
                    for p in range(pairs):
                        lanes = slice(p * 2 * HEAD_DIM, (p + 1) * 2 * HEAD_DIM)
                        turned = turn(result[run * RUN : (run + 1) * RUN, lanes], tables)
                        low = turned.astype(LOW)
                        if kind == 0:
                            low = (low * SCORE_SCALE).astype(LOW)
                        at = kind * dw + p * 2 * HEAD_DIM
                        mixed_s[run_at, at : at + 2 * HEAD_DIM] = low

    last = grid.z_n - 1
    tokens_x.step(1)
    send_out(0)
    for k in range(2, last):
        tokens_x.step(k)
        send_out(k - 1)
    tokens_g = TokenGather(grid, copies, g_in, g_s)
    send_out(last - 1)
    tokens_x.step(last)
    send_out(last)
    pieces = []
    for m in range(3):
        arrived(piece_slot(grid.ctx, grid.fsdp, m), qkv_sems[m])
        pieces.append(
            ShardGather(
                grid,
                copies,
                piece_slot(grid.ctx, grid.fsdp, m),
                lambda f, m=m: piece_slot(grid.ctx, f, m),
            )
        )
    up.forward()
    small_sum(3, small_z, stage)
    puts.append(copies.local(small_s.at[4], small_out))
    small_f[...] = small_s[4].astype(F32)
    for kind in range(3):
        at = pl.ds(pl.multiple_of(grid.ctx * dw, 128), dw)
        row = small_f[4 + kind : 5 + kind, at]
        qkv_bias_s[kind] = jnp.broadcast_to(row, qkv_bias_s.shape[1:])
    block = up_bias_s.shape[2]
    for i in range(fw // block):
        offset = grid.ctx * fw
        at = pl.ds(pl.multiple_of(offset % width + i * block, 128), block)
        row = jnp.zeros((1, block), F32)
        for j in range(4):
            row = row + jnp.where(offset // width == j, small_f[7 + j : 8 + j, at], 0.0)
        up_bias_s[i] = jnp.broadcast_to(row, up_bias_s.shape[1:])
    tokens_x.ready(0)
    normalize(0)
    up_kept.wait()
    up.finish()
    puts.append(copies.local(wu_s, wu_out))
    for gather in pieces:
        gather.forward()
    tokens_x.ready(1)
    normalize(1)
    project_up(0, 2)
    for gather in pieces:
        gather.finish()
    puts.append(copies.local(wi_s, wi_out))
    tokens_g.step(1)
    project_qkv(0, 2)
    spread_out(0)
    for k in range(2, grid.z_n):
        tokens_x.ready(k)
        normalize(k)
        project_up(k)
        project_qkv(k)
        spread_out(k - 1)
        shards[k - 2].forward()
        if k == last:
            spread_out(last)
        if k > 2:
            tokens_g.step(k - 1)
    puts.append(copies.local(x_s, x_out))
    puts.append(copies.local(normed_s, normed_out))
    puts.append(copies.local(slope_s, slope_out))
    puts.append(copies.local(stats_s, stats_out))
    length = x_s.shape[0]
    pair = 2 * HEAD_DIM

    tall = min(256, length)

    @pl.loop(0, length // tall)
    def _(i):
        start = pl.multiple_of(i * tall, tall)
        result = dot_nn(to_sorted(row_in, start, tall), mixed_s[...]).astype(LOW)
        for kind in range(3):
            for p in range(pairs):
                at = kind * dw + p * pair
                qkv_s[kind, p, pl.ds(start, tall), :] = result[:, at : at + pair]

    @pl.loop(0, pairs)
    def _(p):
        attend(qkv_s.at[0, p], qkv_s.at[1, p], qkv_s.at[2, p], ctx_s.at[p], lse_s.at[p])

    @pl.loop(0, length // tall)
    def _(i):
        start = pl.multiple_of(i * tall, tall)
        back = to_stored(row_in, start, tall)
        for p in range(pairs):
            at = slice(fw + p * pair, fw + (p + 1) * pair)
            hidden_s[pl.ds(start, tall), at] = dot_tn(back, ctx_s[p]).astype(LOW)

    tokens_g.step(last)
    for gather in shards[last - 1 :]:
        gather.forward()
    puts.append(copies.local(hidden_s, hidden_out))
    puts.append(copies.local(qkv_s, qkv_out))
    puts.append(copies.local(lse_s, lse_out))
    for gather in shards:
        gather.finish()
    puts.append(copies.local(wo_s, wo_out))
    for k in range(grid.z_n):
        tokens_g.ready(k)
    puts.append(copies.local(g_s, g_out))
    for put in puts:
        put.wait()
    copies.drain()


def accumulate(dst, *sources):
    if len(dst.shape) == 3:

        @pl.loop(0, dst.shape[0])
        def _(i):
            accumulate(dst.at[i], *[source.at[i] for source in sources])

        return
    rows, step = dst.shape[0], 16

    @pl.loop(0, rows // step)
    def _(i):
        part = pl.ds(pl.multiple_of(i * step, step), step)
        total = sources[0][part, :].astype(F32)
        for source in sources[1:]:
            total = total + source[part, :].astype(F32)
        dst[part, :] = total.astype(dst.dtype)


class TokenScatter:
    def __init__(self, grid, copies, parts, from_x, from_z, total, half):
        self.grid, self.copies, self.parts = grid, copies, parts
        self.rows = total.shape[0]
        self.cols = pl.ds(half * (total.shape[1] // 2), total.shape[1] // 2)
        self.from_x, self.from_z = from_x.at[:, :, :, self.cols], from_z.at[:, :, self.cols]
        self.total = total.at[:, self.cols]
        self.along_x, self.sems, self.remotes = {}, {}, {}
        self.order = [t for i in range(grid.z_n // 2) for t in (grid.z_n - 1 - i, i)]

    def block(self, t, dx):
        x = (self.grid.x + dx) % self.grid.x_n
        rows = pl.ds(pl.multiple_of(x * self.rows, self.rows), self.rows)
        return self.parts.at[t, rows, self.cols]

    def launch(self, t):
        for l in range(1, self.grid.x_n):
            self.along_x[t, l] = self.copies.send(
                self.block(t, l), self.from_x.at[t, l - 1], ctx=self.grid.zx(0, l)
            )

    def collect(self, t):
        terms = [self.block(t, 0)]
        for l in range(1, self.grid.x_n):
            arrived(self.from_x.at[t, l - 1], self.along_x[t, l])
            terms.append(self.from_x.at[t, l - 1])
        accumulate(terms[0], *terms)

    def hop(self, t, way, first, z):
        grid, own, slot = self.grid, self.block(t, 0), self.from_z.at[t]
        if first:
            after = slot
            if way < 0:
                after = self.from_z.at[jnp.where(grid.z - 1 == t, grid.z_n, t)]
            remote, sem = self.copies.prepare(own, after, ctx=grid.zx(way, 0))
            self.remotes[t, way], self.sems[t, way] = remote, sem
            self.copies.perhaps.append((grid.z < t if way > 0 else grid.z > t, remote))

        @pl.when(grid.z == z)
        def _():
            if not first:
                arrived(slot, self.sems[t, way])
                accumulate(own, own, slot)
            self.remotes[t, way].start()

    def step(self, i):
        last = self.grid.z_n - 1
        if i <= last:
            self.collect(self.order[i])
        for j, t in enumerate(self.order):
            if 0 <= i - j < t:
                self.hop(t, 1, i == j, i - j)
            if 0 <= i - j < last - t:
                self.hop(t, -1, i == j, last - (i - j))

    def finish(self):
        grid = self.grid
        for t in range(grid.z_n):

            @pl.when(grid.z == t)
            def _(t=t):
                terms = [self.block(t, 0)]
                if t > 0:
                    arrived(self.from_z.at[t], self.sems[t, 1])
                    terms.append(self.from_z.at[t])
                if t < grid.z_n - 1:
                    arrived(self.from_z.at[grid.z_n], self.sems[t, -1])
                    terms.append(self.from_z.at[grid.z_n])
                accumulate(self.total, *terms)


class ShardScatter:
    def __init__(self, grid, copies, views, from_core, from_y):
        self.grid, self.copies, self.views = grid, copies, views
        self.from_core, self.from_y = from_core, from_y
        self.rounds = list(range(1, grid.y_n)) + [0]
        self.across = {
            k: [
                copies.send(part, from_core.at[k, i], fsdp=grid.yc(0, 1))
                for i, part in enumerate(views(grid.yc(k, 1)))
            ]
            for k in self.rounds
        }
        self.along_y = {}

    def step(self, k):
        for i, part in enumerate(self.views(self.grid.yc(k, 0))):
            arrived(self.from_core.at[k, i], self.across[k][i])
            accumulate(part, part, self.from_core.at[k, i])
            if k > 0:
                self.along_y[k, i] = self.copies.send(
                    part, self.from_y.at[k - 1, i], fsdp=self.grid.yc(k, 0)
                )

    def finish(self):
        for i, part in enumerate(self.views(self.grid.fsdp)):
            for k in range(1, self.grid.y_n):
                arrived(self.from_y.at[k - 1, i], self.along_y[k, i])
            accumulate(
                part, part, *[self.from_y.at[k - 1, i] for k in range(1, self.grid.y_n)]
            )


def to_sorted(row_ref, start, tile):
    length = row_ref.shape[1]
    place = lax.broadcasted_iota(jnp.int32, (tile, length), 0) + start
    return jnp.where(place == row_ref[0:1, :], 1.0, 0.0).astype(LOW)


def to_stored(row_ref, start, tile):
    length = row_ref.shape[1]
    place = lax.broadcasted_iota(jnp.int32, (length, tile), 0)
    return jnp.where(place == row_ref[0:1, pl.ds(start, tile)], 1.0, 0.0).astype(LOW)


def run_rows(i):
    return pl.ds(pl.multiple_of(i * RUN, RUN), RUN)


def attend_back(q_s, k_s, v_s, lse_s, g_s, dq_s, dk_s, dv_s):
    length = q_s.shape[0]
    dk_s[...] = jnp.zeros_like(dk_s)
    dv_s[...] = jnp.zeros_like(dv_s)
    tile = min(256, length)
    diagonal = lower_triangle(tile)
    for start in range(0, length, tile):
        rows, reach = slice(start, start + tile), start + tile

        @pl.loop(0, 2)
        def _(head, rows=rows, reach=reach, start=start):
            mine = head_lanes(tile, head)
            q_own, g_own = pick(mine, q_s[rows, :]), pick(mine, g_s[rows, :])
            lse = jnp.where(head == 0, lse_s[rows, 0:1], lse_s[rows, HEAD_DIM : HEAD_DIM + 1])
            scores = masked_tile(dot_nt(q_own, k_s[:reach, :]), diagonal, start)
            probs = jnp.exp(scores - lse)
            grad_probs = dot_nt(g_own, v_s[:reach, :])
            inner = jnp.sum(probs * grad_probs, axis=1, keepdims=True)
            grad_scores = (probs * (grad_probs - inner)).astype(LOW)
            grad_q = dot_nn(grad_scores, k_s[:reach, :]) * SCORE_SCALE
            dq_s[rows, :] = jnp.where(mine, grad_q, dq_s[rows, :])
            dk_s[:reach, :] += dot_tn(grad_scores, q_own)
            dv_s[:reach, :] += dot_tn(probs.astype(LOW), g_own)


def scatter_out_kernel(
    shape, hidden_in, wo_in, g_in, slope_in, qkv_in, lse_in,
    row_in, start_in, step_in,
    total_out, go_out, gup_out, gm_out,
    hidden_s, wo_s, g_s, slope_s, qkv_s, lse_s, po_s, po_x, po_z, po_sum,
    go_s, go_core, go_y, gup_s, gctx_s, gm_s, sorted_s, turned_s, dq_s, dk_s, dv_s, sems,
):
    grid = Grid(*shape).locate()
    copies = Copies(sems)
    length, fw = gup_s.shape
    dw = gctx_s.shape[1]
    width, cols = wo_s.shape
    pair = 2 * HEAD_DIM
    loads = [
        copies.local(src, dst)
        for src, dst in (
            (hidden_in, hidden_s), (wo_in, wo_s), (g_in, g_s),
            (slope_in, slope_s), (qkv_in, qkv_s), (lse_in, lse_s),
        )
    ]
    grid.greet()
    loads[0].wait()
    loads[1].wait()
    group = po_s.shape[1]
    tile = min(256, group)
    early, late = (
        TokenScatter(grid, copies, po_s, po_x, po_z, po_sum, half) for half in range(2)
    )
    unit = go_s.shape[2]
    block = grid.fsdp_n * unit
    part_n = grid.ctx_n // 2

    def make_out(first, count=1):
        @pl.loop(0, count * (group // tile) * (width // 256))
        def _(i):
            t, i = first - i // (group // tile * (width // 256)), i % (
                group // tile * (width // 256)
            )
            part = pl.multiple_of((i // (width // 256)) * tile, tile)
            at = pl.ds(pl.multiple_of((i % (width // 256)) * 256, 256), 256)
            rows = pl.ds(pl.multiple_of(t * group + part, tile), tile)
            result = dot_nt(hidden_s[rows, :], wo_s[at, :])
            po_s[t, pl.ds(part, tile), at] = result.astype(LOW)

        for t in range(first, first - count, -1):
            early.launch(t)

    def make_grad_out(part):
        @pl.loop(part * part_n, (part + 1) * part_n)
        def _(c):
            at = pl.ds(pl.multiple_of(c * block, block), block)
            result = dot_tn(g_s[:, at], hidden_s[...]).astype(LOW)
            go_s[c] = result.reshape(grid.fsdp_n, unit, cols)

        span = pl.ds(part * part_n, part_n)
        return ShardScatter(
            grid,
            copies,
            lambda f: [go_s.at[span, f]],
            go_core.at[:, :, span],
            go_y.at[:, :, span],
        )

    make_out(early.order[0])
    make_out(early.order[1])
    loads[2].wait()
    shards = [make_grad_out(0)]
    make_out(grid.z_n - 2, grid.z_n - 2)
    for t in late.order:
        late.launch(t)
    early.step(0)
    shards.append(make_grad_out(1))
    early.step(1)
    for k in shards[0].rounds:
        shards[0].step(k)
    early.step(2)
    for k in shards[1].rounds:
        shards[1].step(k)
    loads[3].wait()
    tall = min(256, length)

    @pl.loop(0, (length // tall) * (fw // 256))
    def _(i):
        rows = pl.ds(pl.multiple_of((i // (fw // 256)) * tall, tall), tall)
        at = pl.ds(pl.multiple_of((i % (fw // 256)) * 256, 256), 256)
        grad = dot_nn(g_s[rows, :], wo_s[:, at])
        gup_s[rows, at] = (grad * slope_s[rows, at].astype(F32)).astype(LOW)

    puts = [copies.local(gup_s, gup_out)]
    early.step(3)

    @pl.loop(0, length // tall)
    def _(i):
        rows = pl.ds(pl.multiple_of(i * tall, tall), tall)
        gctx_s[rows, :] = dot_nn(g_s[rows, :], wo_s[:, pl.ds(fw, dw)]).astype(LOW)

    early.step(grid.z_n)
    late.step(0)
    loads[4].wait()
    loads[5].wait()
    pairs = dw // pair

    @pl.loop(0, length // tall)
    def _(i):
        start = pl.multiple_of(i * tall, tall)
        result = dot_nn(to_sorted(row_in, start, tall), gctx_s[...]).astype(LOW)
        for p in range(pairs):
            sorted_s[p, pl.ds(start, tall), :] = result[:, p * pair : (p + 1) * pair]

    def attend_pairs(first, last):
        @pl.loop(first, last)
        def _(p):
            attend_back(
                qkv_s.at[0, p], qkv_s.at[1, p], qkv_s.at[2, p], lse_s.at[p],
                sorted_s.at[p], dq_s, dk_s, dv_s,
            )

            @pl.loop(0, length // RUN)
            def _(i):
                tables, rows = run_turn(start_in, step_in, i), run_rows(i)
                turned_s[0, p, rows, :] = turn(dq_s[rows, :], tables, -1.0).astype(LOW)
                turned_s[1, p, rows, :] = turn(dk_s[rows, :], tables, -1.0).astype(LOW)
                turned_s[2, p, rows, :] = dv_s[rows, :].astype(LOW)

    late.step(1)
    attend_pairs(0, (pairs + 1) // 2)
    late.step(2)
    late.step(3)
    for shard in shards:
        shard.finish()
    late.step(grid.z_n)
    if pairs > 1:
        attend_pairs((pairs + 1) // 2, pairs)
    puts.append(copies.local(go_s.at[:, grid.fsdp], go_out))

    @pl.loop(0, length // tall)
    def _(i):
        start = pl.multiple_of(i * tall, tall)
        back = to_stored(row_in, start, tall)
        for kind in range(3):
            for p in range(pairs):
                at = kind * dw + p * pair
                result = dot_tn(back, turned_s[kind, p])
                gm_s[pl.ds(start, tall), at : at + pair] = result.astype(LOW)

    puts.append(copies.local(gm_s, gm_out))
    early.finish()
    late.finish()
    puts.append(copies.local(po_sum, total_out))
    for put in puts:
        put.wait()
    copies.drain()


def scatter_in_kernel(
    shape, gm_in, wi_in, gup_in, wu_in, x_in, stats_in, normed_in, g_own_in, go_in,
    total_out, gu_out, gi_out, go_out, small_out,
    gm_s, wi_s, gup_s, wu_s, x_s, stats_s, normed_s, g_own_s, pn_s, pn_x, pn_z, pn_sum,
    gu_s, gu_core, gu_y, gi_s, gi_core, gi_y, gi_got, go_got,
    small_s, small_y, small_x, small_core, small_z, sems,
):
    grid = Grid(*shape).locate()
    copies = Copies(sems)
    length, fw = gup_s.shape
    width = wi_s.shape[1]
    dw = gm_s.shape[1] // 3
    unit = gi_got.shape[1]
    up_rows = fw // grid.fsdp_n
    loads = [
        copies.local(src, dst)
        for src, dst in (
            (gm_in, gm_s), (wi_in, wi_s), (gup_in, gup_s), (wu_in, wu_s),
            (x_in, x_s), (stats_in, stats_s), (normed_in, normed_s), (g_own_in, g_own_s),
        )
    ]
    grid.greet()
    peers = [(k, l) for k in range(grid.z_n) for l in range(grid.x_n) if k or l]
    own_o = copies.local(go_in.at[grid.ctx], go_got.at[grid.ctx])
    out_sems = [
        copies.send(go_in.at[grid.zx(k, l)], go_got.at[grid.ctx], ctx=grid.zx(k, l))
        for k, l in peers
    ]
    small_s[0] = jnp.zeros_like(small_s[0])
    for load in loads[:6]:
        load.wait()
    group = pn_s.shape[1]
    tile = min(256, group)
    early, late = (
        TokenScatter(grid, copies, pn_s, pn_x, pn_z, pn_sum, half) for half in range(2)
    )

    def make_normed(first, count=1):
        @pl.loop(0, count * (group // tile) * (width // 256))
        def _(i):
            t, i = first - i // (group // tile * (width // 256)), i % (
                group // tile * (width // 256)
            )
            part = pl.multiple_of((i // (width // 256)) * tile, tile)
            at = pl.ds(pl.multiple_of((i % (width // 256)) * 256, 256), 256)
            rows = pl.ds(pl.multiple_of(t * group + part, tile), tile)
            grad = dot_nn(gm_s[rows, :], wi_s[:, at]) + dot_nn(gup_s[rows, :], wu_s[:, at])
            pn_s[t, pl.ds(part, tile), at] = grad.astype(LOW)
            mean, spread = stats_s[rows, 0:1], stats_s[rows, HEAD_DIM : HEAD_DIM + 1]
            xhat = (x_s[rows, at].astype(F32) - mean) * spread
            small_s[0, 0:1, at] += jnp.sum(grad * xhat, axis=0, keepdims=True)
            small_s[0, 1:2, at] += jnp.sum(grad, axis=0, keepdims=True)

        for t in range(first, first - count, -1):
            early.launch(t)

    make_normed(early.order[0])
    make_normed(early.order[1])
    for load in loads[6:]:
        load.wait()

    span = width // 2

    @pl.loop(0, 3 * 2)
    def _(i):
        at = pl.ds(pl.multiple_of((i // 2) * dw, dw), dw)
        cols = pl.ds(pl.multiple_of((i % 2) * span, span), span)
        gi_s[at, cols] = dot_tn(gm_s[:, at], normed_s[:, cols]).astype(LOW)

    def piece_slot(f, m):
        kind, place = grid.qkv_piece(grid.ctx, f, m)
        return gi_s.at[pl.ds(pl.multiple_of((kind * grid.fsdp_n + place) * unit, unit), unit)]

    shards_i = ShardScatter(
        grid, copies, lambda f: [piece_slot(f, m) for m in range(3)], gi_core, gi_y
    )
    make_normed(grid.z_n - 2, grid.z_n - 2)
    for t in late.order:
        late.launch(t)

    small_s[0, 2:3, :] = jnp.sum(g_own_s[...].astype(F32), axis=0, keepdims=True)
    for kind in range(3):
        at = pl.ds(pl.multiple_of(grid.ctx * dw, 128), dw)
        terms = gm_s[:, kind * dw : (kind + 1) * dw].astype(F32)
        small_s[0, 4 + kind : 5 + kind, at] = jnp.sum(terms, axis=0, keepdims=True)
    offset = grid.ctx * fw
    at = pl.ds(pl.multiple_of(offset % width, 128), fw)
    terms = jnp.sum(gup_s[...].astype(F32), axis=0, keepdims=True)
    for row in range(4):
        small_s[0, 7 + row : 8 + row, at] = jnp.where(offset // width == row, terms, 0.0)

    def small_sum(step, buffer, stage):
        for i, sem in enumerate(stage):
            arrived(buffer.at[i], sem)
        accumulate(
            small_s.at[step + 1], small_s.at[step], *[buffer.at[i] for i in range(len(stage))]
        )

    stage = [
        copies.send(small_s.at[0], small_y.at[k - 1], fsdp=grid.yc(k, 0))
        for k in range(1, grid.y_n)
    ]

    def up_slot(f):
        return gu_s.at[pl.ds(pl.multiple_of(f * up_rows, up_rows), up_rows)]

    early.step(0)
    for k in shards_i.rounds:
        shards_i.step(k)
    early.step(1)

    @pl.loop(0, fw // 256 * 2)
    def _(i):
        at = pl.ds(pl.multiple_of((i // 2) * 256, 256), 256)
        cols = pl.ds(pl.multiple_of((i % 2) * span, span), span)
        gu_s[at, cols] = dot_tn(gup_s[:, at], normed_s[:, cols]).astype(LOW)

    shards_u = ShardScatter(grid, copies, lambda f: [up_slot(f)], gu_core, gu_y)
    early.step(2)
    small_sum(0, small_y, stage)
    stage = [
        copies.send(small_s.at[1], small_core.at[c - 1], fsdp=grid.yc(0, c))
        for c in range(1, grid.core_n)
    ]
    for k in shards_u.rounds:
        shards_u.step(k)
    early.step(3)
    early.step(grid.z_n)
    late.step(0)
    late.step(1)
    shards_i.finish()
    qkv_sems = []
    for m in range(3):
        owner = grid.qkv_owner(grid.ctx, grid.fsdp, m)
        qkv_sems.append(
            copies.send_or_keep(piece_slot(grid.fsdp, m), gi_got.at[m], owner, grid.ctx)
        )
    small_sum(1, small_core, stage)
    stage = [
        copies.send(small_s.at[2], small_x.at[l - 1], ctx=grid.zx(0, l))
        for l in range(1, grid.x_n)
    ]
    late.step(2)
    late.step(3)
    small_sum(2, small_x, stage)
    stage = [
        copies.send(small_s.at[3], small_z.at[k - 1], ctx=grid.zx(k, 0))
        for k in range(1, grid.z_n)
    ]
    shards_u.finish()
    puts = [copies.local(up_slot(grid.fsdp), gu_out)]
    late.step(grid.z_n)
    early.finish()
    late.finish()
    puts.append(copies.local(pn_sum, total_out))
    own_o.wait()
    for (k, l), sem in zip(peers, out_sems):
        arrived(go_got.at[grid.zx(-k, -l)], sem)
    puts.append(copies.local(go_got, go_out))
    for m in range(3):
        arrived(gi_got.at[m], qkv_sems[m])
    puts.append(copies.local(gi_got, gi_out))
    small_sum(3, small_z, stage)
    puts.append(copies.local(small_s.at[4], small_out))
    for put in puts:
        put.wait()
    copies.drain()


def solution(mesh):
    shape = mesh.shape["ctx"], mesh.shape["fsdp"]
    ctx_n, fsdp_n = shape
    n = ctx_n * fsdp_n
    plan = Grid(*shape)
    x_n, z_n, core_n, y_n = plan.x_n, plan.z_n, plan.core_n, plan.y_n

    def gather(x_own, g_own, w_qkv, w_fc1, w_fc2, w_dense, small, tables):
        local_len, width = x_own.shape
        unit, hidden_units = w_fc2.shape
        length = ctx_n * local_len
        fw, dw = hidden_units // ctx_n, width // ctx_n
        pair = 2 * HEAD_DIM
        small_rows = jax.ShapeDtypeStruct((16, width), LOW)
        kept = [
            jax.ShapeDtypeStruct((length, width), LOW),
            jax.ShapeDtypeStruct((length, width), LOW),
            jax.ShapeDtypeStruct((3 * fsdp_n * unit, width), LOW),
            jax.ShapeDtypeStruct((fw, width), LOW),
            jax.ShapeDtypeStruct((ctx_n, fsdp_n, unit, fw + dw), LOW),
        ]
        made = [
            jax.ShapeDtypeStruct((length, width), LOW),
            jax.ShapeDtypeStruct((length, fw + dw), LOW),
            jax.ShapeDtypeStruct((length, fw), LOW),
            jax.ShapeDtypeStruct((3, dw // pair, length, pair), LOW),
            jax.ShapeDtypeStruct((dw // pair, length, pair), F32),
            jax.ShapeDtypeStruct((length, pair), F32),
        ]
        return pl.pallas_call(
            functools.partial(gather_kernel, shape),
            out_shape=kept + [small_rows] + made,
            in_specs=[anywhere] * 6 + [inside] * 9,
            out_specs=[anywhere] * 12,
            scratch_shapes=[pltpu.VMEM(s.shape, s.dtype) for s in kept + made]
            + [pltpu.VMEM((length, 3 * dw), LOW), pltpu.VMEM((dw // pair, length, pair), LOW)]
            + [pltpu.VMEM((16, width), F32), pltpu.VMEM((3, 8, dw), F32)]
            + [pltpu.VMEM((max(fw // 256, 1), 8, min(fw, 256)), F32)]
            + [pltpu.VMEM((count, 16, width), LOW) for count in (5, x_n, core_n, y_n, z_n)]
            + [pltpu.SemaphoreType.DMA((SEMAPHORES,))],
            compiler_params=pltpu.CompilerParams(
                collective_id=0, has_side_effects=True, vmem_limit_bytes=VMEM_BYTES
            ),
            name="gather",
        )(x_own, g_own, w_qkv, w_fc1, w_fc2, w_dense, *small, *tables)

    def token_scratch(local_len, width):
        return [
            pltpu.VMEM((z_n, x_n * local_len, width), LOW),
            pltpu.VMEM((z_n, max(x_n - 1, 1), local_len, width), LOW),
            pltpu.VMEM((z_n + 1, local_len, width), LOW),
            pltpu.VMEM((local_len, width), F32),
        ]

    def shard_scratch(parts, *block):
        return [
            pltpu.VMEM((y_n, parts) + block, LOW),
            pltpu.VMEM((max(y_n - 1, 1), parts) + block, LOW),
        ]

    def inside_like(*arrays):
        return [pltpu.VMEM(a.shape, a.dtype) for a in arrays]

    anywhere = pl.BlockSpec(memory_space=pl.ANY)
    inside = pl.BlockSpec(memory_space=pltpu.VMEM)

    def scatter_out(hidden, wo, g_all, slope, qkv, lse, tables):
        length, cols = hidden.shape
        local_len, width = length // ctx_n, g_all.shape[1]
        unit = width // n
        fw = slope.shape[1]
        dw, pair = cols - fw, 2 * HEAD_DIM
        return pl.pallas_call(
            functools.partial(scatter_out_kernel, shape),
            out_shape=[
                jax.ShapeDtypeStruct((local_len, width), F32),
                jax.ShapeDtypeStruct((ctx_n, unit, cols), LOW),
                jax.ShapeDtypeStruct((length, fw), LOW),
                jax.ShapeDtypeStruct((length, 3 * dw), LOW),
            ],
            in_specs=[anywhere] * 6 + [inside] * 3,
            out_specs=[anywhere] * 4,
            scratch_shapes=inside_like(hidden, wo, g_all, slope, qkv, lse)
            + token_scratch(local_len, width)
            + [pltpu.VMEM((ctx_n, fsdp_n, unit, cols), LOW)]
            + shard_scratch(1, ctx_n, unit, cols)
            + [pltpu.VMEM((length, c), LOW) for c in (fw, dw, 3 * dw)]
            + [pltpu.VMEM((dw // pair, length, pair), LOW)]
            + inside_like(qkv)
            + [pltpu.VMEM((length, pair), F32)] * 3
            + [pltpu.SemaphoreType.DMA((SEMAPHORES,))],
            compiler_params=pltpu.CompilerParams(
                collective_id=1, has_side_effects=True, vmem_limit_bytes=VMEM_BYTES
            ),
            name="scatter_out",
        )(hidden, wo, g_all, slope, qkv, lse, *tables)

    def scatter_in(gm, wi, gup, wu, x_all, stats, normed, g_own, go):
        length, width = normed.shape
        local_len = length // ctx_n
        unit, up_rows = width // n, wu.shape[0] // fsdp_n
        return pl.pallas_call(
            functools.partial(scatter_in_kernel, shape),
            out_shape=[
                jax.ShapeDtypeStruct((local_len, width), F32),
                jax.ShapeDtypeStruct((up_rows, width), LOW),
                jax.ShapeDtypeStruct((3, unit, width), LOW),
                jax.ShapeDtypeStruct(go.shape, LOW),
                jax.ShapeDtypeStruct((16, width), F32),
            ],
            in_specs=[anywhere] * 9,
            out_specs=[anywhere] * 5,
            scratch_shapes=inside_like(gm, wi, gup, wu, x_all, stats, normed, g_own)
            + token_scratch(local_len, width)
            + inside_like(wu)
            + shard_scratch(1, up_rows, width)
            + inside_like(wi)
            + shard_scratch(3, unit, width)
            + [pltpu.VMEM((3, unit, width), LOW)]
            + inside_like(go)
            + [pltpu.VMEM((count, 16, width), F32) for count in (5, y_n, x_n, core_n, z_n)]
            + [pltpu.SemaphoreType.DMA((SEMAPHORES,))],
            compiler_params=pltpu.CompilerParams(
                collective_id=2, has_side_effects=True, vmem_limit_bytes=VMEM_BYTES
            ),
            name="scatter_in",
        )(gm, wi, gup, wu, x_all, stats, normed, g_own, go)

    def body(
        hidden_in, positions, ln_gain, ln_bias, w_qkv, b_qkv, w_dense, b_dense,
        w_fc1, b_fc1, w_fc2, b_fc2, out_grad,
    ):
        local_len, width = hidden_in.shape[1:]
        hidden_units = w_fc2.shape[1]
        unit = w_dense.shape[0]
        up_rows = w_fc1.shape[0]
        fw, dw = hidden_units // ctx_n, width // ctx_n
        my_ctx = lax.axis_index("ctx")
        me = my_ctx * fsdp_n + lax.axis_index("fsdp")
        length = positions.shape[1]
        x_own, g_own = hidden_in[0], out_grad[0]

        rank = positions[0, ::RUN] // RUN
        starts, steps = turning_tables(length)
        ranks = jnp.arange(length // RUN, dtype=jnp.int32)
        chosen = (rank[:, None] == ranks[None, :])[None, :, :, None]
        stored_starts = jnp.sum(jnp.where(chosen, starts[:, None], 0.0), axis=2)

        own_small = [
            a.reshape(-1, unit) for a in (ln_gain, ln_bias, b_dense, b_fc2, b_qkv, b_fc1)
        ]
        x_all, g_all, wi, wu, wo, small, normed, hidden, slope, qkv, lse, stats = gather(
            x_own, g_own, w_qkv, w_fc1, w_fc2, w_dense, own_small, (positions, stored_starts, steps)
        )
        small = small.astype(F32)
        gain, bias_dense, bias_down = small[0], small[2], small[3]
        total, grad_o, grad_upward, grad_mixed = scatter_out(
            hidden, wo.reshape(width, fw + dw), g_all, slope, qkv, lse, (positions, starts, steps)
        )
        grad_normed, grad_up, grad_qkv, grad_o, sums = scatter_in(
            grad_mixed, wi, grad_upward, wu, x_all, stats, normed, g_own, grad_o
        )

        def standardize(values):
            wide = values.astype(F32)
            centered = wide - jnp.mean(wide, axis=-1, keepdims=True)
            spread = lax.rsqrt(jnp.mean(centered * centered, axis=-1, keepdims=True) + EPSILON)
            return centered * spread, spread

        hidden_out = (total + x_own.astype(F32) + bias_dense + bias_down).astype(LOW)
        xhat, spread = standardize(x_own)
        e = grad_normed * gain
        grad_in = (
            e - jnp.mean(e, axis=-1, keepdims=True)
            - xhat * jnp.mean(e * xhat, axis=-1, keepdims=True)
        ) * spread + g_own.astype(F32)
        grad_o = grad_o.transpose(1, 0, 2).astype(F32)
        sums = sums.reshape(-1)

        def own_slice(row, size):
            return lax.dynamic_slice_in_dim(sums, row * width + me * size, size)

        grad_b_out = own_slice(2, unit)
        return (
            hidden_out[None],
            grad_in[None],
            own_slice(0, unit),
            own_slice(1, unit),
            grad_qkv.reshape(3 * unit, width).astype(F32),
            own_slice(4, 3 * unit),
            grad_o[:, :, fw:].reshape(unit, width),
            grad_b_out,
            grad_up.astype(F32),
            own_slice(7, up_rows),
            grad_o[:, :, :fw].reshape(unit, hidden_units),
            grad_b_out,
        )

    tokens, rows, cells = P("fsdp", "ctx", None), P(BOTH, None), P(BOTH)
    return jax.shard_map(
        body,
        mesh=mesh,
        in_specs=(
            tokens, P("fsdp", None), cells, cells, rows, cells, rows, cells,
            rows, cells, rows, cells, tokens,
        ),
        out_specs=(
            tokens, tokens, cells, cells, rows, cells, rows, cells, rows, cells, rows, cells,
        ),
        check_vma=False,
    )
```
